128 devices in a mesh: lon: 32 (over z, y, x_lo), lat: 4 (over x_hi, core).
Axes of the slice: x: 4 (x_hi: 2, x_lo: 2; x = x_hi * 2 + x_lo), y: 4, z: 4, core: 2. Of those that a mesh axis runs over, the one named last changes fastest.
Arguments:
- points: bfloat16 [256, 69, 5216], P('lat', None, 'lon'), may hold values from -6 to 6
- row_len: int32 [256], P('lat'), may hold values from 20 to 5136, as said below
- w_embed: bfloat16 [69, 256], replicated, may hold values from -0.75 to 0.75
- kernel1: bfloat16 [25, 256], replicated, may hold values from -1.1953125 to 1.1953125
- gain1: float32 [256], replicated, may hold values from 0.5 to 1.5
- point1: bfloat16 [256, 256], replicated, may hold values from -0.375 to 0.375
- kernel2: bfloat16 [25, 256], replicated, may hold values from -1.1953125 to 1.1953125
- gain2: float32 [256], replicated, may hold values from 0.5 to 1.5
- point2: bfloat16 [256, 256], replicated, may hold values from -0.375 to 0.375
- cotangent: bfloat16 [256, 768, 256], P('lat', 'lon'), may hold values from -6 to 6
Outputs:
- out: bfloat16 [256, 768, 256], P('lat', 'lon')
- grad_embed: float32 [69, 256], replicated
- grad_kernel1: float32 [25, 256], replicated
- grad_kernel2: float32 [25, 256], replicated
- grad_point1: float32 [256, 256], replicated
- grad_point2: float32 [256, 256], replicated
- grad_gain1: float32 [256], replicated
- grad_gain2: float32 [256], replicated
The draws below stay inside these ranges and needn't reach their ends.
Inputs may be any that keep to these rules, and one draw needn't show every extreme that they name: `row_len`: every row holds 20 plus a multiple of 4 points; some row holds exactly 5136.
All inputs are finite; a program needn't handle non-finite values.
Results may differ from the reference program's by a relative error of at most 0.012.
Values may be sent and summed in bfloat16 or wider, within the bound.
No kernel may reach another device: no remote copies, remote signals or barrier semaphores. Data moves between devices by JAX's collectives and lax.ppermute only.
A program may use at most 128 MiB of HBM per device.

```python
import jax
import jax.numpy as jnp
from jax import lax

LON_DEV = 24
VARS = 69
C = 256
ROWMAX = 5136
ROWS = 256
LON = 768
SLOT = 163
N_LON = 32


def draw_row_len(key, part):
    base = jax.random.fold_in(key, 11)
    first_key, second_key = jax.random.split(base)
    steps = jax.random.randint(first_key, (ROWS,), 0, (ROWMAX - 20) // 4 + 1)
    lengths = 20 + 4 * steps
    chosen = jax.random.randint(second_key, (), 0, ROWS)
    return jnp.where(jnp.arange(ROWS) == chosen, ROWMAX, lengths).astype(jnp.int32)


def shard_levels(key, shape, cuts, low, high):
    loudness, own = 1.0, jax.random.fold_in(key, 6)
    for position, parts in cuts:
        steps = jnp.exp(jax.random.uniform(jax.random.fold_in(own, position), (parts,), jnp.float32, low / len(cuts), high / len(cuts)))
        loudness = loudness * jnp.repeat(steps, shape[position] // parts).reshape([-1 if axis == position else 1 for axis in range(len(shape))])
    return loudness


def normal_values(key, extent, spread, bound, cuts=(), held_as=jnp.bfloat16):
    factor_of = shard_levels(key, extent, cuts, -0.22, 0.18) if cuts else 1.0
    values = jax.random.normal(key, extent, jnp.float32) * spread * factor_of
    return jnp.minimum(jnp.maximum(values, -bound), bound).astype(held_as)


def setup_inputs(seed: int = 0) -> dict:
    arg_keys = jax.random.split(jax.random.key(seed), 11)
    return {
        "points": normal_values(arg_keys[0], (ROWS, VARS, SLOT * N_LON), 1.0, 6.0, ((0, 4), (2, 32))),
        "row_len": draw_row_len(jax.random.fold_in(arg_keys[10], 71), 0),
        "w_embed": normal_values(arg_keys[2], (VARS, C), VARS ** -0.5, 0.75),
        "kernel1": normal_values(arg_keys[3], (25, C), 0.2, 1.1953125),
        "gain1": jnp.clip(1.0 + 0.1 * jax.random.normal(arg_keys[4], (C,), jnp.float32), 0.5, 1.5),
        "point1": normal_values(arg_keys[5], (C, C), C ** -0.5, 0.375),
        "kernel2": normal_values(arg_keys[6], (25, C), 0.2, 1.1953125),
        "gain2": jnp.clip(1.0 + 0.1 * jax.random.normal(arg_keys[7], (C,), jnp.float32), 0.5, 1.5),
        "point2": normal_values(arg_keys[8], (C, C), C ** -0.5, 0.375),
        "cotangent": normal_values(arg_keys[9], (ROWS, LON, C), 1.0, 6.0, ((0, 4), (1, 32))),
    }


def regrid(points, lengths, first_sector, lon_dev, lon_total):
    nrows, nvars, nsec, slots = points.shape
    sector = jnp.arange(nsec, dtype=jnp.int32) + first_sector
    cell = sector[:, None] * lon_dev + jnp.arange(lon_dev, dtype=jnp.int32)[None, :]
    count = lengths.astype(jnp.int32)[:, None, None]
    product = cell[None] * count
    lower = product // lon_total
    start = sector[None, :, None] * lon_dev * count // lon_total
    frac = (product - lower * lon_total).astype(jnp.float32) / lon_total
    offset = (lower - start)[..., None]
    marks = jnp.arange(slots, dtype=jnp.int32)
    weights = jnp.where(marks == offset, 1.0 - frac[..., None], 0.0) + jnp.where(marks == offset + 1, frac[..., None], 0.0)
    weights = weights.astype(jnp.float32)
    result = jnp.einsum('rvsm,rsjm->rvsj', points.astype(jnp.float32), weights, precision=lax.Precision.HIGHEST)
    return result.reshape(nrows, nvars, nsec * lon_dev)

def embed(regridded, w_embed):
    return jnp.einsum('rvj,vc->rjc', regridded, w_embed.astype(jnp.float32), precision=lax.Precision.HIGHEST).astype(jnp.bfloat16)

def depthwise(padded, kernel):
    nrows = padded.shape[0] - 4
    ncols = padded.shape[1] - 4
    taps = kernel.astype(jnp.float32)
    wide = padded.astype(jnp.float32)
    total = jnp.zeros((nrows, ncols, padded.shape[2]), jnp.float32)
    for first in range(5):
        for second in range(5):
            total = total + wide[first:first + nrows, second:second + ncols] * taps[5 * first + second]
    return total

def mix_forward(conv, gain, point):
    scale = lax.rsqrt(lax.optimization_barrier(jnp.mean(conv * conv, -1, keepdims=True)) + 1e-06)
    normed = (conv * scale * gain.astype(jnp.float32)).astype(jnp.bfloat16)
    mixed = jnp.dot(normed, point, preferred_element_type=jnp.float32)
    return (normed, scale, mixed)

def residual(inputs, mixed):
    return (inputs.astype(jnp.float32) + jax.nn.silu(mixed)).astype(jnp.bfloat16)

def mix_backward(upstream, conv, scale, normed, mixed, gain, point):
    chans = normed.shape[-1]
    sig = jax.nn.sigmoid(mixed)
    dmixed = (upstream * sig * (1.0 + mixed * (1.0 - sig))).astype(jnp.bfloat16)
    dpoint = jnp.dot(normed.reshape(-1, chans).T, dmixed.reshape(-1, chans), preferred_element_type=jnp.float32)
    dnormed = jnp.dot(dmixed, point.T, preferred_element_type=jnp.float32)
    dgain = lax.optimization_barrier(jnp.sum((dnormed * conv * scale).reshape(-1, chans), 0))
    gained = gain.astype(jnp.float32) * dnormed
    dconv = scale * gained - conv * scale ** 3 * lax.optimization_barrier(jnp.mean(gained * conv, -1, keepdims=True))
    return (dpoint, dgain, dconv.astype(jnp.bfloat16))

def kernel_grad(padded, dconv):
    nrows, ncols, chans = dconv.shape
    wide = padded.astype(jnp.float32)
    back = dconv.astype(jnp.float32)
    pieces = []
    for first in range(5):
        for second in range(5):
            pieces.append(lax.optimization_barrier(jnp.sum((wide[first:first + nrows, second:second + ncols] * back).reshape(-1, chans), 0)))
    return jnp.stack(pieces)

def wrap_pad(field):
    beside_all = jnp.concatenate([field[:, -2:], field, field[:, :2]], 1)
    return jnp.pad(beside_all, ((2, 2), (0, 0), (0, 0)))

def reference(points, row_len, w_embed, kernel1, gain1, point1, kernel2, gain2, point2, cotangent):
    slots = points.shape[2] // N_LON
    grid = points.reshape(ROWS, VARS, N_LON, slots)

    def one_row(item):
        row_points, count = item
        regridded = regrid(row_points[None], count[None], 0, LON_DEV, LON)
        return (regridded[0], embed(regridded, w_embed)[0])
    regridded, h0 = lax.map(one_row, (grid, row_len))
    pad1 = wrap_pad(h0)
    conv1 = depthwise(pad1, kernel1)
    normed1, scale1, mixed1 = mix_forward(conv1, gain1, point1)
    h1 = residual(h0, mixed1)
    pad2 = wrap_pad(h1)
    conv2 = depthwise(pad2, kernel2)
    normed2, scale2, mixed2 = mix_forward(conv2, gain2, point2)
    out = residual(h1, mixed2)
    upstream = cotangent.astype(jnp.float32)
    dpoint2, dgain2, dconv2 = mix_backward(upstream, conv2, scale2, normed2, mixed2, gain2, point2)
    dkernel2 = kernel_grad(pad2, dconv2)
    grad1 = upstream + depthwise(wrap_pad(dconv2), kernel2[::-1])
    dpoint1, dgain1, dconv1 = mix_backward(grad1, conv1, scale1, normed1, mixed1, gain1, point1)
    dkernel1 = kernel_grad(pad1, dconv1)
    grad0 = grad1 + depthwise(wrap_pad(dconv1), kernel1[::-1])
    dembed = jnp.einsum('rvj,rjc->vc', regridded, grad0, precision=lax.Precision.HIGHEST)
    factor = float(ROWS * LON) ** (-0.5)
    return (out, dembed * factor, dkernel1 * factor, dkernel2 * factor, dpoint1 * factor, dpoint2 * factor, dgain1 * factor, dgain2 * factor)
```

```python
import jax
import jax.numpy as jnp
from jax import lax
from jax.sharding import PartitionSpec as P


def with_halo(array, sides, width, wrap):
    for axis, dim in sides:
        devices, length = (lax.axis_size(axis), array.shape[dim])
        up = [(i, (i + 1) % devices) for i in range(devices if wrap else devices - 1)]
        down = [(j, i) for i, j in up]
        last = lax.slice_in_dim(array, length - width, length, axis=dim)
        initial = lax.slice_in_dim(array, 0, width, axis=dim)
        before = lax.ppermute(last, axis, up)
        after = lax.ppermute(initial, axis, down)
        array = jnp.concatenate([before, array, after], axis=dim)
    return array


def together(arrays, axes):
    devices = 1
    for axis in axes:
        devices *= lax.axis_size(axis)
    sizes = [a.size for a in arrays]
    share = -(-sum(sizes) // (128 * devices)) * 128
    padding = jnp.zeros((share * devices - sum(sizes),), jnp.float32)
    flat = jnp.concatenate([a.ravel() for a in arrays] + [padding])
    parts = lax.all_to_all(flat.reshape(devices, share), axes, 0, 0)
    mine = jnp.broadcast_to(jnp.sum(parts, 0), (devices, share))
    total = lax.all_to_all(mine, axes, 0, 0).ravel()
    ends = [0]
    for size in sizes:
        ends.append(ends[-1] + size)
    return tuple((total[b:e].reshape(a.shape) for a, b, e in zip(arrays, ends, ends[1:])))


def regrid(points, lengths, first_sector, lon_dev, lon_total):
    nrows, nvars, nsec, slots = points.shape
    sector = jnp.arange(nsec, dtype=jnp.int32) + first_sector
    cell = sector[:, None] * lon_dev + jnp.arange(lon_dev, dtype=jnp.int32)[None, :]
    count = lengths[:, None, None]
    product = cell[None] * count
    lower = product // lon_total
    start = sector[None, :, None] * lon_dev * count // lon_total
    frac = (product - lower * lon_total).astype(jnp.float32) / lon_total
    offset = (lower - start)[..., None]
    marks = jnp.arange(slots, dtype=jnp.int32)
    weights = jnp.where(marks == offset, 1.0 - frac[..., None], 0.0) + jnp.where(
        marks == offset + 1, frac[..., None], 0.0
    )
    result = jnp.einsum(
        "rvsm,rsjm->rvsj", points.astype(jnp.float32), weights, precision=lax.Precision.HIGHEST
    )
    return result.reshape(nrows, nvars, nsec * lon_dev)


def embed(regridded, w_embed):
    return jnp.einsum(
        "rvj,vc->rjc", regridded, w_embed.astype(jnp.float32), precision=lax.Precision.HIGHEST
    ).astype(jnp.bfloat16)


def depthwise(padded, kernel):
    nrows = padded.shape[0] - 4
    ncols = padded.shape[1] - 4
    taps = kernel.astype(jnp.float32)
    wide = padded.astype(jnp.float32)
    total = jnp.zeros((nrows, ncols, padded.shape[2]), jnp.float32)
    for first in range(5):
        for second in range(5):
            total = (
                total
                + wide[first : first + nrows, second : second + ncols] * taps[5 * first + second]
            )
    return total


def mix_forward(conv, gain, point):
    scale = lax.rsqrt(jnp.mean(conv * conv, -1, keepdims=True) + 1e-06)
    normed = (conv * scale * gain).astype(jnp.bfloat16)
    mixed = jnp.dot(normed, point, preferred_element_type=jnp.float32)
    return (normed, scale, mixed)


def residual(inputs, mixed):
    return (inputs.astype(jnp.float32) + jax.nn.silu(mixed)).astype(jnp.bfloat16)


def mix_backward(upstream, conv, scale, normed, mixed, gain, point):
    chans = normed.shape[-1]
    sig = jax.nn.sigmoid(mixed)
    dmixed = (upstream * sig * (1.0 + mixed * (1.0 - sig))).astype(jnp.bfloat16)
    dpoint = jnp.dot(
        normed.reshape(-1, chans).T, dmixed.reshape(-1, chans), preferred_element_type=jnp.float32
    )
    dnormed = jnp.dot(dmixed, point.T, preferred_element_type=jnp.float32)
    dgain = jnp.sum((dnormed * conv * scale).reshape(-1, chans), 0)
    gained = gain * dnormed
    dconv = scale * gained - conv * scale**3 * jnp.mean(gained * conv, -1, keepdims=True)
    return (dpoint, dgain, dconv.astype(jnp.bfloat16))


def kernel_grad(padded, dconv):
    nrows, ncols, chans = dconv.shape
    wide = padded.astype(jnp.float32)
    back = dconv.astype(jnp.float32)
    pieces = []
    for first in range(5):
        for second in range(5):
            pieces.append(
                jnp.sum(
                    (wide[first : first + nrows, second : second + ncols] * back).reshape(
                        -1, chans
                    ),
                    0,
                )
            )
    return jnp.stack(pieces)


def extend(field):
    beside_all = with_halo(field, (("lon", 1),), 2, True)
    return with_halo(beside_all, (("lat", 0),), 2, False)


def on_device(points, row_len, w_embed, kernel1, gain1, point1, kernel2, gain2, point2, cotangent):
    nrows, nvars, slots = points.shape
    lon_dev = cotangent.shape[1]
    lon_total = lon_dev * lax.axis_size("lon")
    rows_total = nrows * lax.axis_size("lat")
    regridded = regrid(
        points.reshape(nrows, nvars, 1, slots), row_len, lax.axis_index("lon"), lon_dev, lon_total
    )
    h0 = embed(regridded, w_embed)
    wide = with_halo(h0, (("lon", 1),), 4, True)
    wide = with_halo(wide, (("lat", 0),), 4, False)
    conv_wide = depthwise(wide, kernel1)
    normed_wide, scale_wide, mixed_wide = mix_forward(conv_wide, gain1, point1)
    h1_wide = residual(wide[2:-2, 2:-2], mixed_wide)
    row_ids = lax.axis_index("lat") * nrows - 2 + jnp.arange(nrows + 4, dtype=jnp.int32)
    inside = (row_ids >= 0) & (row_ids < rows_total)
    h1_wide = jnp.where(inside[:, None, None], h1_wide, jnp.zeros_like(h1_wide))
    pad1 = wide[2:-2, 2:-2]
    conv1 = conv_wide[2:-2, 2:-2]
    normed1 = normed_wide[2:-2, 2:-2]
    scale1 = scale_wide[2:-2, 2:-2]
    mixed1 = mixed_wide[2:-2, 2:-2]
    h1 = h1_wide[2:-2, 2:-2]
    conv2 = depthwise(h1_wide, kernel2)
    normed2, scale2, mixed2 = mix_forward(conv2, gain2, point2)
    out = residual(h1, mixed2)
    upstream = cotangent.astype(jnp.float32)
    dpoint2, dgain2, dconv2 = mix_backward(upstream, conv2, scale2, normed2, mixed2, gain2, point2)
    dkernel2 = kernel_grad(h1_wide, dconv2)
    grad1 = upstream + depthwise(extend(dconv2), kernel2[::-1])
    dpoint1, dgain1, dconv1 = mix_backward(grad1, conv1, scale1, normed1, mixed1, gain1, point1)
    dkernel1 = kernel_grad(pad1, dconv1)
    grad0 = grad1 + depthwise(extend(dconv1), kernel1[::-1])
    dembed = jnp.einsum("rvj,rjc->vc", regridded, grad0, precision=lax.Precision.HIGHEST)
    dembed, dkernel1, dkernel2, dpoint1, dpoint2, dgain1, dgain2 = together(
        (dembed, dkernel1, dkernel2, dpoint1, dpoint2, dgain1, dgain2), ("lon", "lat")
    )
    factor = float(rows_total * lon_total) ** (-0.5)
    return (
        out,
        dembed * factor,
        dkernel1 * factor,
        dkernel2 * factor,
        dpoint1 * factor,
        dpoint2 * factor,
        dgain1 * factor,
        dgain2 * factor,
    )


def solution(mesh):
    in_specs = (
        P("lat", None, "lon"),
        P("lat"),
        P(),
        P(),
        P(),
        P(),
        P(),
        P(),
        P(),
        P("lat", "lon", None),
    )
    out_specs = (P("lat", "lon", None), P(), P(), P(), P(), P(), P(), P())
    return jax.shard_map(
        on_device, mesh=mesh, in_specs=in_specs, out_specs=out_specs, check_vma=False
    )
```

```python
import functools

import jax
import jax.numpy as jnp
from jax import lax
from jax.experimental import pallas as pl
from jax.experimental.pallas import tpu as pltpu
from jax.sharding import PartitionSpec as P

F32 = jnp.float32
BF16 = jnp.bfloat16
ROWS = 64
COLS = 24
HALO = 8
PITCH = COLS + 2 * HALO
TALL = ROWS + 2 * HALO
LEAD = 16
FLAT = LEAD + PITCH * TALL + 16
CHANS = 256
VARS = 69
TILES = 128
AXES = ("lon", "lat")


def regrid_kernel(row_len, sector, points, w_embed, h0, left, right, regridded, *, lon_total):
    step = pl.program_id(0)
    first = sector[0] * COLS
    cell = first.astype(F32) + lax.broadcasted_iota(jnp.int32, (COLS, 163), 0).astype(F32)
    mark = lax.broadcasted_iota(jnp.int32, (COLS, 163), 1).astype(F32)
    weight = w_embed[...]
    for group in range(points.shape[0] // 4):
        found = []
        for k in range(4):
            local = 4 * group + k
            count = row_len[step * points.shape[0] + local]
            start = (first * count // lon_total).astype(F32)
            product = cell * count.astype(F32)
            lower = jnp.floor((product + 2.0) * (1.0 / lon_total))
            share = (product - lower * lon_total) * 0.25
            away = mark - (lower - start)
            whole = lon_total // 4
            mix = jnp.where(away == 0.0, whole - share, jnp.where(away == 1.0, share, 0.0))
            found.append(
                lax.dot_general(
                    mix.astype(BF16),
                    points[local],
                    (((1,), (1,)), ((), ())),
                    preferred_element_type=F32,
                )
            )
        values = jnp.concatenate(found, 0) * (4.0 / lon_total)
        high = values.astype(BF16)
        low = (values - high.astype(F32)).astype(BF16)
        field = jnp.dot(high, weight, preferred_element_type=F32) + jnp.dot(
            low, weight, preferred_element_type=F32
        )
        field = field.reshape(4, COLS, CHANS).astype(BF16)
        rows = slice(4 * group, 4 * group + 4)
        h0[rows] = field
        left[rows] = field[:, :HALO]
        right[rows] = field[:, COLS - HALO :]
        regridded[slice(4 * COLS * group, 4 * COLS * (group + 1)), :VARS] = high


def regrid_embed(points, row_len, w_embed, lon_total):
    steps = 4
    rows = ROWS // steps
    slots = points.shape[2]
    return pl.pallas_call(
        functools.partial(regrid_kernel, lon_total=lon_total),
        grid_spec=pltpu.PrefetchScalarGridSpec(
            num_scalar_prefetch=2,
            grid=(steps,),
            in_specs=[
                pl.BlockSpec((rows, VARS, slots), lambda i, *_: (i, 0, 0)),
                pl.BlockSpec((VARS, CHANS), lambda i, *_: (0, 0)),
            ],
            out_specs=[
                pl.BlockSpec((rows, COLS, CHANS), lambda i, *_: (i, 0, 0)),
                pl.BlockSpec((rows, HALO, CHANS), lambda i, *_: (i, 0, 0)),
                pl.BlockSpec((rows, HALO, CHANS), lambda i, *_: (i, 0, 0)),
                pl.BlockSpec((rows * COLS, 128), lambda i, *_: (i, 0)),
            ],
        ),
        out_shape=[
            jax.ShapeDtypeStruct((ROWS, COLS, CHANS), BF16),
            jax.ShapeDtypeStruct((ROWS, HALO, CHANS), BF16),
            jax.ShapeDtypeStruct((ROWS, HALO, CHANS), BF16),
            jax.ShapeDtypeStruct((ROWS * COLS, 128), BF16),
        ],
        name="regrid_embed",
    )(row_len, jnp.reshape(lax.axis_index("lon"), (1,)).astype(jnp.int32), points, w_embed)


def at(row):
    return LEAD + PITCH * row


def conv(source, half, start, rows, cols, taps, visit=None):
    sums = [None] * rows
    for e in range(5):
        weights = [taps[half, 5 * a + e] for a in range(5)]
        for i in range(rows + 4):
            x = source[half, pl.ds(start + PITCH * (i - 2) + e - 2, cols), :]
            x = x.reshape(cols // 8, 8, 128)
            for a in range(5):
                r = i - a
                if 0 <= r < rows:
                    term = x * weights[a]
                    sums[r] = term if sums[r] is None else sums[r] + term
                    if visit is not None:
                        visit(a, e, r, x)
        if visit is not None:
            visit(None, e, None, None)
    return sums


class TapSums:
    def __init__(self, store, half, centre):
        self.store, self.half, self.centre, self.live = store, half, centre, {}

    def __call__(self, a, e, r, x):
        if a is None:
            for tap, value in self.live.items():
                self.store[self.half, tap] += value
            self.live = {}
            return
        tap = 24 - (5 * a + e)
        if x.shape[0] == 5:
            x = x[1:4]
        term = jnp.sum(self.centre[r] * x, 0)
        self.live[tap] = term if tap not in self.live else self.live[tap] + term


def local_part(x, rows):
    return x.reshape(rows, PITCH, x.shape[-1])[:, HALO : HALO + COLS].reshape(
        rows * COLS, x.shape[-1]
    )


def blocks_kernel(
    lat, h0, left, right, above, below, cot, cot_left, cot_right,
    kernel1, gain1, point1, kernel2, gain2, point2, regridded,
    out, packed,
    x0, cots, d, h1, xhat1, scale1, slope1, dd2, g1, dd1,
    taps1, taps2, flip1, flip2, turned1, turned2,
    u1, dp1, u2, dp2, g0, gk1, gk2, gg1, gg2,
    *, lat_devices,
):
    halves = (slice(0, 128), slice(128, 256))

    for k in range(25):
        for h in (0, 1):
            one = jnp.broadcast_to(kernel1[k : k + 1, halves[h]].astype(F32), (8, 128))
            two = jnp.broadcast_to(kernel2[k : k + 1, halves[h]].astype(F32), (8, 128))
            taps1[h, k] = one
            flip1[h, 24 - k] = one
            taps2[h, k] = two
            flip2[h, 24 - k] = two
    turned1[...] = jnp.transpose(point1[...].astype(F32)).astype(BF16)
    turned2[...] = jnp.transpose(point2[...].astype(F32)).astype(BF16)
    zeros = jnp.zeros((8, 128), F32)
    for h in (0, 1):
        for ref in (gg1, gg2):
            ref[h] = zeros
        for ref in (gk1, gk2):
            ref[h] = jnp.zeros((25, 8, 128), F32)
        for ref in (x0, cots, h1, dd2, dd1):
            ref[h, 0:LEAD] = jnp.zeros((LEAD, 128), F32)
            ref[h, FLAT - 16 : FLAT] = jnp.zeros((16, 128), F32)

    def put(ref, row, value):
        for h in (0, 1):
            ref[h, pl.ds(pl.multiple_of(at(row), 8), PITCH), :] = value[:, halves[h]]

    def fill(pair, carry):
        sides = [cot_left[pair].astype(F32), cot_right[pair].astype(F32)]
        swapped = [pltpu.roll(s, 4, 0) for s in sides]
        for odd in (0, 1):
            row = 2 * pair + odd
            field = [left[row].astype(F32), h0[row].astype(F32), right[row].astype(F32)]
            put(x0, row + HALO, jnp.concatenate(field, 0))
            west = sides[0] if odd else swapped[0]
            east = swapped[1] if odd else sides[1]
            put(cots, row + HALO, jnp.concatenate([west, cot[row].astype(F32), east], 0))
        return carry

    lax.fori_loop(0, ROWS // 2, fill, 0)
    for k in range(HALO):
        put(x0, k, above[k].astype(F32))
        put(x0, k + HALO + ROWS, below[k].astype(F32))
    for k in range(4):
        put(cots, k + 4, above[k + HALO].astype(F32))
        put(cots, k + HALO + ROWS, below[k + HALO].astype(F32))

    def get(ref, start, rows):
        return [ref[h, pl.ds(pl.multiple_of(start, 8), rows * PITCH), :] for h in (0, 1)]

    def keep(ref, start, rows, values):
        for h in (0, 1):
            ref[h, pl.ds(pl.multiple_of(start, 8), rows * PITCH), :] = values[h]

    def plain_conv(source, taps, target, start, rows):
        for h in (0, 1):
            sums = conv(source, h, start, rows, PITCH, taps)
            flat = jnp.concatenate(sums, 0).reshape(rows * PITCH, 128)
            target[h, pl.ds(pl.multiple_of(start, 8), rows * PITCH), :] = flat

    def gains(ref):
        return [ref[:, halves[h]] for h in (0, 1)]

    def normalised(start, rows):
        raw = get(d, start, rows)
        mean = jnp.sum(raw[0] * raw[0] + raw[1] * raw[1], -1, keepdims=True) * (1.0 / CHANS)
        scale = lax.rsqrt(mean + 1e-06)
        return scale, [raw[h] * scale for h in (0, 1)]

    def activated(xhat, gain, point):
        u = [xhat[h] * gain[h] for h in (0, 1)]
        p = jnp.dot(
            jnp.concatenate(u, 1).astype(BF16), point[...], preferred_element_type=F32
        )
        p = [p[:, s] for s in halves]
        sig = [0.5 * jnp.tanh(0.5 * v) + 0.5 for v in p]
        silu = [p[h] * sig[h] for h in (0, 1)]
        slope = [sig[h] + silu[h] * (1.0 - sig[h]) for h in (0, 1)]
        return u, silu, slope

    def through_norm(grad, slope, xhat, scale, gain, turned):
        dp = [grad[h] * slope[h] for h in (0, 1)]
        du = jnp.dot(
            jnp.concatenate(dp, 1).astype(BF16), turned[...], preferred_element_type=F32
        )
        du = [du[:, s] for s in halves]
        gained = [du[h] * gain[h] for h in (0, 1)]
        mean = jnp.sum(gained[0] * xhat[0] + gained[1] * xhat[1], -1, keepdims=True) * (
            1.0 / CHANS
        )
        dd = [
            (scale * (gained[h] - xhat[h] * mean)).astype(BF16).astype(F32) for h in (0, 1)
        ]
        return dp, du, dd

    def gain_sums(store, du, xhat, rows):
        for h in (0, 1):
            terms = local_part(du[h] * xhat[h], rows).reshape(-1, 8, 128)
            store[h] += jnp.sum(terms, 0)

    def pipeline(blocks, first, second):
        first(0)

        def step(i, carry):
            second(i - 1)
            first(i)
            return carry

        lax.fori_loop(1, blocks, step, 0)
        second(blocks - 1)

    size = 4 * PITCH

    def first_conv(i):
        plain_conv(x0, taps1, d, at(2) + i * size, 4)

    def first_mix(i):
        start = at(2) + i * size
        scale, xhat = normalised(start, 4)
        _, silu, slope = activated(xhat, gains(gain1), point1)
        x = get(x0, start, 4)
        keep(h1, start, 4, [(x[h] + silu[h]).astype(BF16).astype(F32) for h in (0, 1)])
        keep(xhat1, start, 4, xhat)
        keep(slope1, start, 4, slope)
        scale1[pl.ds(pl.multiple_of(start, 8), size), :] = jnp.broadcast_to(scale, (size, 128))

    pipeline((TALL - 4) // 4, first_conv, first_mix)

    def clear(ref, row, rows):
        for h in (0, 1):
            ref[h, at(row) : at(row + rows)] = jnp.zeros((rows * PITCH, 128), F32)

    @pl.when(lat[0] == 0)
    def _():
        clear(h1, 2, 6)

    @pl.when(lat[0] == lat_devices - 1)
    def _():
        clear(h1, HALO + ROWS, 6)

    def second_conv(start):
        plain_conv(h1, taps2, d, start, 4)

    def second_mix(start, local):
        scale, xhat = normalised(start, 4)
        gain = gains(gain2)
        u, silu, slope = activated(xhat, gain, point2)
        dp, du, dd = through_norm(get(cots, start, 4), slope, xhat, scale, gain, turned2)
        keep(dd2, start, 4, dd)
        if local is not None:
            x = get(h1, start, 4)
            result = [local_part(x[h] + silu[h], 4) for h in (0, 1)]
            out[pl.ds(local * 4, 4)] = (
                jnp.concatenate(result, 1).reshape(4, COLS, CHANS).astype(BF16)
            )
            spot = pl.ds(pl.multiple_of(local * 96, 96), 96)
            u2[spot] = jnp.concatenate([local_part(v, 4) for v in u], 1).astype(BF16)
            dp2[spot] = jnp.concatenate([local_part(v, 4) for v in dp], 1).astype(BF16)
            gain_sums(gg2, du, xhat, 4)

    def outer(k, carry):
        start = at(4) + k * PITCH * (ROWS + 4)
        second_conv(start)
        second_mix(start, None)
        return carry

    lax.fori_loop(0, 2, outer, 0)
    pipeline(
        ROWS // 4,
        lambda i: second_conv(at(HALO) + i * size),
        lambda i: second_mix(at(HALO) + i * size, i),
    )

    def third_conv(start, rows, local):
        for h in (0, 1):
            visit = None
            if local:
                centre = [
                    h1[h, pl.ds(pl.multiple_of(start + PITCH * r + HALO, 8), COLS), :].reshape(
                        3, 8, 128
                    )
                    for r in range(rows)
                ]
                visit = TapSums(gk2, h, centre)
            sums = conv(dd2, h, start, rows, PITCH, flip2, visit)
            spot = pl.ds(pl.multiple_of(start, 8), rows * PITCH)
            flat = jnp.concatenate(sums, 0).reshape(rows * PITCH, 128)
            g1[h, spot, :] = flat + cots[h, spot, :]

    def third_mix(start, rows, local):
        gain = gains(gain1)
        xhat = get(xhat1, start, rows)
        spot = pl.ds(pl.multiple_of(start, 8), rows * PITCH)
        dp, du, dd = through_norm(
            get(g1, start, rows), get(slope1, start, rows), xhat, scale1[spot], gain, turned1
        )
        keep(dd1, start, rows, dd)
        if local is not None:
            spot = pl.ds(pl.multiple_of(local * 96, 96), 96)
            u = [local_part(xhat[h] * gain[h], 4) for h in (0, 1)]
            u1[spot] = jnp.concatenate(u, 1).astype(BF16)
            dp1[spot] = jnp.concatenate([local_part(v, 4) for v in dp], 1).astype(BF16)
            gain_sums(gg1, du, xhat, 4)

    def margin(k, carry):
        start = at(6) + k * PITCH * (ROWS + 2)
        third_conv(start, 2, False)
        third_mix(start, 2, None)
        return carry

    lax.fori_loop(0, 2, margin, 0)
    pipeline(
        ROWS // 4,
        lambda i: third_conv(at(HALO) + i * size, 4, True),
        lambda i: third_mix(at(HALO) + i * size, 4, i),
    )

    @pl.when(lat[0] == 0)
    def _():
        clear(dd1, 6, 2)

    @pl.when(lat[0] == lat_devices - 1)
    def _():
        clear(dd1, HALO + ROWS, 2)

    def fourth_conv(i, carry):
        start = at(HALO) + i * size + HALO
        total = []
        for h in (0, 1):
            centre = [
                x0[h, pl.ds(pl.multiple_of(start + PITCH * r, 8), COLS), :].reshape(3, 8, 128)
                for r in range(4)
            ]
            sums = conv(dd1, h, start, 4, COLS, flip1, TapSums(gk1, h, centre))
            base = [
                g1[h, pl.ds(pl.multiple_of(start + PITCH * r, 8), COLS), :] for r in range(4)
            ]
            total.append(
                jnp.concatenate([sums[r].reshape(COLS, 128) + base[r] for r in range(4)], 0)
            )
        g0[pl.ds(pl.multiple_of(i * 96, 96), 96)] = jnp.concatenate(total, 1).astype(BF16)
        return carry

    lax.fori_loop(0, ROWS // 4, fourth_conv, 0)

    def across(a, b):
        return lax.dot_general(
            a, b, (((0,), (0,)), ((), ())), preferred_element_type=F32
        )

    def pack(place, value):
        rows = value.shape[0]
        for h in (0, 1):
            packed[place : place + rows // 8, h] = value[:, halves[h]].reshape(rows // 8, 8, 128)

    pack(0, across(u1[...], dp1[...]))
    pack(32, across(u2[...], dp2[...]))
    embed = across(regridded[:, :VARS], g0[...])

    def tidy(ref, rows):
        return [jnp.sum(ref[h], -2) for h in (0, 1)]

    top1 = [jnp.sum(gg1[h], 0, keepdims=True) for h in (0, 1)]
    top2 = [jnp.sum(gg2[h], 0, keepdims=True) for h in (0, 1)]
    gain_rows = jnp.concatenate(
        [jnp.concatenate(top1, 1), jnp.concatenate(top2, 1), jnp.zeros((1, CHANS), F32)], 0
    )
    pack(64, jnp.concatenate([embed, gain_rows], 0))
    for place, ref in ((73, gk1), (77, gk2)):
        both = jnp.concatenate([jnp.sum(ref[h], 1) for h in (0, 1)], 1)
        pack(place, jnp.concatenate([both, jnp.zeros((7, CHANS), F32)], 0))
    packed[81:TILES] = jnp.zeros((TILES - 81, 2, 8, 128), F32)


def blocks(fields, weights, regridded, lat_devices):
    wide = pltpu.VMEM((2, FLAT, 128), F32)
    taps = pltpu.VMEM((2, 25, 8, 128), F32)
    square = pltpu.VMEM((CHANS, CHANS), BF16)
    local = pltpu.VMEM((ROWS * COLS, CHANS), BF16)
    eight = pltpu.VMEM((2, 8, 128), F32)
    lat = jnp.reshape(lax.axis_index("lat"), (1,)).astype(jnp.int32)
    operands = (*fields, *weights, regridded)
    vmem = pl.BlockSpec(memory_space=pltpu.VMEM)
    return pl.pallas_call(
        functools.partial(blocks_kernel, lat_devices=lat_devices),
        in_specs=[pl.BlockSpec(memory_space=pltpu.SMEM)] + [vmem] * len(operands),
        out_specs=[vmem, vmem],
        out_shape=[
            jax.ShapeDtypeStruct((ROWS, COLS, CHANS), BF16),
            jax.ShapeDtypeStruct((TILES, 2, 8, 128), F32),
        ],
        scratch_shapes=[wide] * 5
        + [pltpu.VMEM((FLAT, 128), F32)]
        + [wide] * 4
        + [taps] * 4
        + [square] * 2
        + [local] * 5
        + [taps] * 2
        + [eight] * 2,
        compiler_params=pltpu.CompilerParams(vmem_limit_bytes=60 * 1024 * 1024),
        name="both_blocks",
    )(lat, *operands)


def unpack_kernel(packed, embed, kernel1, kernel2, point1, point2, gain1, gain2, *, factor):
    for h in (0, 1):
        lanes = slice(128 * h, 128 * h + 128)
        point1[:, lanes] = packed[0:32, h].reshape(CHANS, 128) * factor
        point2[:, lanes] = packed[32:64, h].reshape(CHANS, 128) * factor
        mixed = packed[64:73, h].reshape(72, 128) * factor
        embed[:, lanes] = mixed[:VARS]
        gain1[:, lanes] = mixed[VARS : VARS + 1]
        gain2[:, lanes] = mixed[VARS + 1 : VARS + 2]
        kernel1[:, lanes] = (packed[73:77, h].reshape(32, 128) * factor)[:25]
        kernel2[:, lanes] = (packed[77:81, h].reshape(32, 128) * factor)[:25]


def summed(packed, factor):
    devices = lax.axis_size(AXES)
    parts = lax.all_to_all(packed, AXES, 0, 0, tiled=True)
    mine = jnp.sum(parts.reshape(devices, -1, 2, 8, 128), 0)
    total = lax.all_to_all(jnp.tile(mine, (devices, 1, 1, 1)), AXES, 0, 0, tiled=True)
    shapes = [(VARS, CHANS), (25, CHANS), (25, CHANS), (CHANS, CHANS), (CHANS, CHANS)]
    results = pl.pallas_call(
        functools.partial(unpack_kernel, factor=factor),
        out_shape=[jax.ShapeDtypeStruct(s, F32) for s in shapes + [(1, CHANS)] * 2],
        name="unpack",
    )(total)
    return (*results[:5], results[5].reshape(CHANS), results[6].reshape(CHANS))


def shifted(before, after, axis, wrap):
    devices = lax.axis_size(axis)
    up = [(i, (i + 1) % devices) for i in range(devices if wrap else devices - 1)]
    down = [(j, i) for i, j in up]
    return lax.ppermute(after, axis, up), lax.ppermute(before, axis, down)


def on_device(points, row_len, w_embed, kernel1, gain1, point1, kernel2, gain2, point2, cotangent):
    lon_total = COLS * lax.axis_size("lon")
    rows_total = ROWS * lax.axis_size("lat")
    cot_left, cot_right = shifted(
        cotangent[:, :4].reshape(ROWS // 2, 8, CHANS),
        cotangent[:, COLS - 4 :].reshape(ROWS // 2, 8, CHANS),
        "lon",
        True,
    )
    h0, west, east, regridded = regrid_embed(points, row_len, w_embed, lon_total)
    left, right = shifted(west, east, "lon", True)
    blank = jnp.zeros((4, 4, CHANS), BF16)

    def band(rows, narrow, pairs):
        field = jnp.concatenate([left[rows], h0[rows], right[rows]], 1)
        sides = [c[pairs].reshape(4, 4, CHANS) for c in (cot_left, cot_right)]
        given = jnp.concatenate([blank, sides[0], cotangent[narrow], sides[1], blank], 1)
        return jnp.concatenate([field, given], 0)

    above, below = shifted(
        band(slice(0, HALO), slice(0, 4), slice(0, 2)),
        band(slice(ROWS - HALO, ROWS), slice(ROWS - 4, ROWS), slice(-2, None)),
        "lat",
        False,
    )
    fields = (h0, left, right, above, below, cotangent, cot_left, cot_right)
    weights = (
        kernel1, gain1.reshape(1, CHANS), point1, kernel2, gain2.reshape(1, CHANS), point2,
    )
    out, packed = blocks(fields, weights, regridded, lax.axis_size("lat"))
    return (out, *summed(packed, float(rows_total * lon_total) ** (-0.5)))


def solution(mesh):
    in_specs = (
        P("lat", None, "lon"),
        P("lat"),
        P(),
        P(),
        P(),
        P(),
        P(),
        P(),
        P(),
        P("lat", "lon", None),
    )
    out_specs = (P("lat", "lon", None), P(), P(), P(), P(), P(), P(), P())
    return jax.shard_map(
        on_device, mesh=mesh, in_specs=in_specs, out_specs=out_specs, check_vma=False
    )
```

```python
import functools

import jax
import jax.numpy as jnp
from jax import lax
from jax.experimental import pallas as pl
from jax.experimental.pallas import tpu as pltpu
from jax.sharding import PartitionSpec as P

F32 = jnp.float32
BF16 = jnp.bfloat16
ROWS = 64
COLS = 24
HALO = 8
PITCH = COLS + 2 * HALO
TALL = ROWS + 2 * HALO
INNER = COLS + 8
LEAD = 16
FLAT = LEAD + PITCH * TALL + 16
SLIM = LEAD + INNER * TALL + 16
CHANS = 256
VARS = 69
TILES = 128
AXES = ("lon", "lat")


GROUP = 8 * COLS
STRIP = 8 * HALO


def regrid_kernel(row_len, sector, points, high, low, west, east, *, lon_total):
    first = (sector[0] * COLS).astype(F32)
    whole = lon_total // 4
    lane = lax.broadcasted_iota(jnp.int32, (8, GROUP), 1)
    row = lane % 8
    cell = first + (lane // 8).astype(F32)
    own = lax.broadcasted_iota(jnp.int32, (8, GROUP), 0) == row
    mark = lax.broadcasted_iota(jnp.int32, (points.shape[3], GROUP), 0).astype(F32)
    found = []
    for k in range(points.shape[1]):
        group = pl.program_id(0) * points.shape[1] + k
        count = jnp.zeros((8, GROUP), F32)
        for q in range(8):
            count = jnp.where(row == q, row_len[8 * group + q].astype(F32), count)
        product = cell * count
        lower = jnp.floor((product + 2.0) * (1.0 / lon_total))
        start = jnp.floor((first * count + 2.0) * (1.0 / lon_total))
        share = (product - lower * lon_total) * 0.25
        away = mark - (lower - start)[:1]
        mix = jnp.where(
            away == 0.0, whole - share[:1], jnp.where(away == 1.0, share[:1], 0.0)
        )
        rows = points[:, k].reshape(VARS * 8, points.shape[3])
        every = jnp.dot(rows, mix.astype(BF16), preferred_element_type=F32)
        kept = jnp.where(own[None], every.reshape(VARS, 8, GROUP), 0.0)
        found.append(jnp.sum(kept, 1) * (1.0 / whole))
    values = jnp.concatenate(found, 1)
    rounded = values.astype(BF16)
    high[...] = rounded
    low[...] = (values - rounded.astype(F32)).astype(BF16)
    west[...] = jnp.concatenate([f[:, :STRIP] for f in found], 1).astype(BF16)
    east[...] = jnp.concatenate([f[:, GROUP - STRIP :] for f in found], 1).astype(BF16)


def regrid(points, row_len, lon_total):
    nvars, nrows, slots = points.shape
    groups = 2
    steps = nrows // (8 * groups)
    strips = jax.ShapeDtypeStruct((nvars, nrows * HALO), BF16)
    full = jax.ShapeDtypeStruct((nvars, nrows * COLS), BF16)
    return pl.pallas_call(
        functools.partial(regrid_kernel, lon_total=lon_total),
        grid_spec=pltpu.PrefetchScalarGridSpec(
            num_scalar_prefetch=2,
            grid=(steps,),
            in_specs=[pl.BlockSpec((nvars, groups, 8, slots), lambda i, *_: (0, i, 0, 0))],
            out_specs=[
                pl.BlockSpec((nvars, groups * GROUP), lambda i, *_: (0, i)),
                pl.BlockSpec((nvars, groups * GROUP), lambda i, *_: (0, i)),
                pl.BlockSpec((nvars, groups * STRIP), lambda i, *_: (0, i)),
                pl.BlockSpec((nvars, groups * STRIP), lambda i, *_: (0, i)),
            ],
        ),
        out_shape=[full, full, strips, strips],
        name="regrid",
    )(
        row_len,
        jnp.reshape(lax.axis_index("lon"), (1,)).astype(jnp.int32),
        points.reshape(nvars, nrows // 8, 8, slots),
    )


def at(row):
    return LEAD + PITCH * row


def inner(row):
    return LEAD + INNER * row


def conv(source, half, start, pitch, rows, cols, taps, visit=None):
    sums = [None] * rows
    for e in range(5):
        weights = [taps[half, 5 * a + e] for a in range(5)]
        for i in range(rows + 4):
            x = source[half, pl.ds(start + pitch * (i - 2) + e - 2, cols), :]
            x = x.reshape(cols // 8, 8, 128)
            for a in range(5):
                r = i - a
                if 0 <= r < rows:
                    term = x * weights[a]
                    sums[r] = term if sums[r] is None else sums[r] + term
                    if visit is not None:
                        visit(a, e, r, x)
        if visit is not None:
            visit(None, e, None, None)
    return sums


class TapSums:
    def __init__(self, store, half, centre):
        self.store, self.half, self.centre, self.live = store, half, centre, {}

    def __call__(self, a, e, r, x):
        if a is None:
            for tap, value in self.live.items():
                self.store[self.half, tap] += value
            self.live = {}
            return
        tap = 24 - (5 * a + e)
        term = jnp.sum(self.centre[r] * x, 0)
        self.live[tap] = term if tap not in self.live else self.live[tap] + term


def blocks_kernel(
    lat, high, low, left, right, above, below, cot, cot_left, cot_right, cot_above, cot_below,
    w_embed, kernel1, gain1, point1, kernel2, gain2, point2,
    out, packed,
    x0, cots, d, h1, xhat1, scale1, slope1, dd2, g1, dd1,
    taps1, taps2, flip1, flip2, turned1, turned2,
    u1, dp1, u2, dp2, g0, gk1, gk2, gg1, gg2, swap, lifted,
    *, lat_devices,
):
    halves = (slice(0, 128), slice(128, 256))

    for k in range(25):
        for h in (0, 1):
            one = jnp.broadcast_to(kernel1[k : k + 1, halves[h]].astype(F32), (8, 128))
            two = jnp.broadcast_to(kernel2[k : k + 1, halves[h]].astype(F32), (8, 128))
            taps1[h, k] = one
            flip1[h, 24 - k] = one
            taps2[h, k] = two
            flip2[h, 24 - k] = two
    turned1[...] = jnp.transpose(point1[...].astype(F32)).astype(BF16)
    turned2[...] = jnp.transpose(point2[...].astype(F32)).astype(BF16)
    zeros = jnp.zeros((8, 128), F32)
    for h in (0, 1):
        for ref in (gg1, gg2):
            ref[h] = zeros
        for ref in (gk1, gk2):
            ref[h] = jnp.zeros((25, 8, 128), F32)
        for ref, size in ((x0, FLAT), (h1, FLAT), (dd2, SLIM), (dd1, SLIM)):
            ref[h, 0:LEAD] = jnp.zeros((LEAD, 128), F32)
            ref[h, size - 16 : size] = jnp.zeros((16, 128), F32)

    weight = w_embed[...]

    def across(a, b):
        return lax.dot_general(a, b, (((0,), (0,)), ((), ())), preferred_element_type=F32)

    def embed(spot, values):
        values = values.astype(BF16).astype(F32)
        for h in (0, 1):
            swap[h, pl.ds(pl.multiple_of(spot, 64), values.shape[0]), :] = values[:, halves[h]]

    def spread(spot, row):
        for k in range(8):
            for h in (0, 1):
                x0[h, pl.ds(pl.multiple_of(at(row + k), 8), PITCH), :] = swap[
                    h, pl.ds(spot + k, PITCH, stride=8), :
                ]

    for i in range(ROWS // 16):
        edge = slice(2 * STRIP * i, 2 * STRIP * (i + 1))
        middle = slice(2 * GROUP * i, 2 * GROUP * (i + 1))
        west = across(left[:, edge], weight)
        east = across(right[:, edge], weight)
        centre = across(high[:, middle], weight) + across(low[:, middle], weight)
        for k in (0, 1):
            spot = 8 * PITCH * (2 * i + k)
            embed(spot, west[STRIP * k : STRIP * (k + 1)])
            embed(spot + STRIP, centre[GROUP * k : GROUP * (k + 1)])
            embed(spot + STRIP + GROUP, east[STRIP * k : STRIP * (k + 1)])
    embed(8 * PITCH * (ROWS // 8), across(above[...], weight))
    embed(8 * PITCH * (ROWS // 8 + 1), across(below[...], weight))

    def unravel(i, carry):
        spread(8 * PITCH * i, HALO + 8 * i)
        return carry

    lax.fori_loop(0, ROWS // 8, unravel, 0)
    spread(8 * PITCH * (ROWS // 8), 0)
    spread(8 * PITCH * (ROWS // 8 + 1), HALO + ROWS)

    later = lax.broadcasted_iota(jnp.int32, (8, 128), 0) >= 4

    def put(row, value):
        for h in (0, 1):
            cots[h, pl.ds(pl.multiple_of(inner(row), 8), INNER), :] = value[:, halves[h]]

    def fill(pair, carry):
        sides = [cot_left[pair].astype(F32), cot_right[pair].astype(F32)]
        for odd in (0, 1):
            row = 2 * pair + odd
            edges = [s[4 * odd : 4 * odd + 4] for s in sides]
            put(
                row + HALO, jnp.concatenate([edges[0], cot[row].astype(F32), edges[1]], 0)
            )
        return carry

    lax.fori_loop(0, ROWS // 2, fill, 0)
    for k in range(4):
        put(k + 4, cot_above[k].astype(F32))
        put(k + HALO + ROWS, cot_below[k].astype(F32))

    def get(ref, start, count):
        return [ref[h, pl.ds(pl.multiple_of(start, 8), count), :] for h in (0, 1)]

    def keep(ref, start, values):
        for h in (0, 1):
            ref[h, pl.ds(pl.multiple_of(start, 8), values[h].shape[0]), :] = values[h]

    def from_wide(ref, row, rows):
        return [
            jnp.concatenate(
                [ref[h, pl.ds(at(row + r) + 4, INNER), :] for r in range(rows)], 0
            )
            for h in (0, 1)
        ]

    def joined(sums):
        return jnp.concatenate(sums, 0).reshape(-1, 128)

    def local_part(x):
        x = x.reshape(-1, 4, 8, 128)
        ends = jnp.where(later, x[:, 0], x[:, 3])
        return jnp.stack([ends, x[:, 1], x[:, 2]], 1).reshape(-1, 128)

    def gains(ref):
        return [ref[:, halves[h]] for h in (0, 1)]

    def normalised(raw):
        mean = jnp.sum(raw[0] * raw[0] + raw[1] * raw[1], -1, keepdims=True) * (1.0 / CHANS)
        scale = lax.rsqrt(mean + 1e-06)
        return scale, [raw[h] * scale for h in (0, 1)]

    def activated(xhat, gain, point):
        u = [xhat[h] * gain[h] for h in (0, 1)]
        p = jnp.dot(
            jnp.concatenate(u, 1).astype(BF16), point[...], preferred_element_type=F32
        )
        p = [p[:, s] for s in halves]
        sig = [0.5 * jnp.tanh(0.5 * v) + 0.5 for v in p]
        silu = [p[h] * sig[h] for h in (0, 1)]
        slope = [sig[h] + silu[h] * (1.0 - sig[h]) for h in (0, 1)]
        return u, silu, slope

    def through_norm(grad, slope, xhat, scale, gain, turned):
        dp = [grad[h] * slope[h] for h in (0, 1)]
        du = jnp.dot(
            jnp.concatenate(dp, 1).astype(BF16), turned[...], preferred_element_type=F32
        )
        gained = [du[:, halves[h]] * gain[h] for h in (0, 1)]
        both = [gained[h] * xhat[h] for h in (0, 1)]
        mean = jnp.sum(both[0] + both[1], -1, keepdims=True) * (1.0 / CHANS)
        dd = [
            (scale * (gained[h] - xhat[h] * mean)).astype(BF16).astype(F32) for h in (0, 1)
        ]
        return dp, both, dd

    def gain_sums(store, both):
        for h in (0, 1):
            store[h] += jnp.sum(local_part(both[h]).reshape(-1, 8, 128), 0)

    def pipeline(blocks, first, second):
        first(0)

        def step(i, carry):
            second(i - 1)
            first(i)
            return carry

        lax.fori_loop(1, blocks, step, 0)
        second(blocks - 1)

    size = 4 * PITCH

    def first_conv(i):
        start = at(2) + i * size
        keep(d, start, [joined(conv(x0, h, start, PITCH, 4, PITCH, taps1)) for h in (0, 1)])

    def first_mix(i):
        start = at(2) + i * size
        scale, xhat = normalised(get(d, start, size))
        _, silu, slope = activated(xhat, gains(gain1), point1)
        x = get(x0, start, size)
        keep(h1, start, [(x[h] + silu[h]).astype(BF16).astype(F32) for h in (0, 1)])
        keep(xhat1, start, xhat)
        keep(slope1, start, slope)
        scale1[pl.ds(pl.multiple_of(start, 8), size), :] = jnp.broadcast_to(scale, (size, 128))

    pipeline((TALL - 4) // 4, first_conv, first_mix)

    @pl.when(lat[0] == 0)
    def _():
        for h in (0, 1):
            h1[h, at(2) : at(HALO)] = jnp.zeros((6 * PITCH, 128), F32)

    @pl.when(lat[0] == lat_devices - 1)
    def _():
        for h in (0, 1):
            h1[h, at(HALO + ROWS) : at(HALO + ROWS + 6)] = jnp.zeros((6 * PITCH, 128), F32)

    def second_conv(row):
        keep(
            d,
            inner(row),
            [joined(conv(h1, h, at(row) + 4, PITCH, 4, INNER, taps2)) for h in (0, 1)],
        )

    def second_mix(row, local):
        start = inner(row)
        scale, xhat = normalised(get(d, start, 4 * INNER))
        gain = gains(gain2)
        u, silu, slope = activated(xhat, gain, point2)
        dp, both, dd = through_norm(
            get(cots, start, 4 * INNER), slope, xhat, scale, gain, turned2
        )
        keep(dd2, start, dd)
        if local is not None:
            keep(lifted, LEAD + 4 * INNER * local, silu)
            spot = pl.ds(pl.multiple_of(local * 96, 96), 96)
            u2[spot] = jnp.concatenate([local_part(v) for v in u], 1).astype(BF16)
            dp2[spot] = jnp.concatenate([local_part(v) for v in dp], 1).astype(BF16)
            gain_sums(gg2, both)

    def result(i):
        total = []
        for h in (0, 1):
            rows = []
            for r in range(4):
                place = LEAD + INNER * (4 * i + r) + 4
                base = h1[h, pl.ds(pl.multiple_of(at(HALO + 4 * i + r) + HALO, 8), COLS), :]
                rows.append(base + lifted[h, pl.ds(place, COLS), :])
            total.append(jnp.concatenate(rows, 0))
        out[pl.ds(i * 4, 4)] = jnp.concatenate(total, 1).reshape(4, COLS, CHANS).astype(BF16)

    def outer(k, carry):
        row = 4 + k * (ROWS + 4)
        second_conv(row)
        second_mix(row, None)
        return carry

    lax.fori_loop(0, 2, outer, 0)
    pipeline(
        ROWS // 4,
        lambda i: second_conv(HALO + 4 * i),
        lambda i: second_mix(HALO + 4 * i, i),
    )

    def third_conv(row, rows, local):
        start = inner(row)
        total = []
        for h in (0, 1):
            visit = None
            if local:
                centre = [
                    h1[h, pl.ds(at(row + r) + 4, INNER), :].reshape(4, 8, 128)
                    for r in range(rows)
                ]
                centre = [
                    jnp.stack(
                        [jnp.where(later, c[0], 0.0), c[1], c[2], jnp.where(later, 0.0, c[3])]
                    )
                    for c in centre
                ]
                visit = TapSums(gk2, h, centre)
            sums = joined(conv(dd2, h, start, INNER, rows, INNER, flip2, visit))
            total.append(sums + cots[h, pl.ds(pl.multiple_of(start, 8), rows * INNER), :])
        keep(g1, start, total)

    def third_mix(row, rows, local):
        start = inner(row)
        gain = gains(gain1)
        xhat = from_wide(xhat1, row, rows)
        scale = jnp.concatenate(
            [scale1[pl.ds(at(row + r) + 4, INNER), :] for r in range(rows)], 0
        )
        dp, both, dd = through_norm(
            get(g1, start, rows * INNER), from_wide(slope1, row, rows), xhat, scale, gain, turned1
        )
        keep(dd1, start, dd)
        if local is not None:
            spot = pl.ds(pl.multiple_of(local * 96, 96), 96)
            u = [local_part(xhat[h] * gain[h]) for h in (0, 1)]
            u1[spot] = jnp.concatenate(u, 1).astype(BF16)
            dp1[spot] = jnp.concatenate([local_part(v) for v in dp], 1).astype(BF16)
            gain_sums(gg1, both)
            result(local)

    def margin(k, carry):
        row = 6 + k * (ROWS + 2)
        third_conv(row, 2, False)
        third_mix(row, 2, None)
        return carry

    lax.fori_loop(0, 2, margin, 0)
    pipeline(
        ROWS // 4,
        lambda i: third_conv(HALO + 4 * i, 4, True),
        lambda i: third_mix(HALO + 4 * i, 4, i),
    )

    @pl.when(lat[0] == 0)
    def _():
        for h in (0, 1):
            dd1[h, inner(6) : inner(HALO)] = jnp.zeros((2 * INNER, 128), F32)

    @pl.when(lat[0] == lat_devices - 1)
    def _():
        for h in (0, 1):
            dd1[h, inner(HALO + ROWS) : inner(HALO + ROWS + 2)] = jnp.zeros(
                (2 * INNER, 128), F32
            )

    def fourth(i, carry):
        row = HALO + 4 * i
        for h in (0, 1):
            centre = [
                x0[h, pl.ds(pl.multiple_of(at(row + r) + HALO, 8), COLS), :].reshape(3, 8, 128)
                for r in range(4)
            ]
            sums = conv(dd1, h, inner(row) + 4, INNER, 4, COLS, flip1, TapSums(gk1, h, centre))
            for r in range(4):
                base = g1[h, pl.ds(inner(row + r) + 4, COLS), :]
                place = GROUP * (i // 2) + 4 * (i % 2) + r
                g0[h, pl.ds(place, COLS, stride=8), :] = sums[r].reshape(COLS, 128) + base
        return carry

    lax.fori_loop(0, ROWS // 4, fourth, 0)

    def pack(place, value):
        rows = value.shape[0]
        value = value.astype(BF16)
        for h in (0, 1):
            packed[place : place + rows // 8, h] = value[:, halves[h]].reshape(rows // 8, 8, 128)

    pack(0, across(u1[...], dp1[...]))
    pack(32, across(u2[...], dp2[...]))
    field = jnp.concatenate([g0[h] for h in (0, 1)], 1).astype(BF16)
    embedded = jnp.dot(high[...], field, preferred_element_type=F32)

    def gain_row(ref, gain):
        total = [jnp.sum(ref[h], 0, keepdims=True) for h in (0, 1)]
        return jnp.concatenate(total, 1) / gain[...]

    pack(
        64,
        jnp.concatenate(
            [embedded, gain_row(gg1, gain1), gain_row(gg2, gain2), jnp.zeros((1, CHANS), F32)], 0
        ),
    )
    for place, ref in ((73, gk1), (77, gk2)):
        total = jnp.concatenate([jnp.sum(ref[h], 1) for h in (0, 1)], 1)
        pack(place, jnp.concatenate([total, jnp.zeros((7, CHANS), F32)], 0))
    packed[81:TILES] = jnp.zeros((TILES - 81, 2, 8, 128), BF16)


def blocks(fields, weights, lat_devices):
    wide = pltpu.VMEM((2, FLAT, 128), F32)
    slim = pltpu.VMEM((2, SLIM, 128), F32)
    taps = pltpu.VMEM((2, 25, 8, 128), F32)
    square = pltpu.VMEM((CHANS, CHANS), BF16)
    local = pltpu.VMEM((ROWS * COLS, CHANS), BF16)
    eight = pltpu.VMEM((2, 8, 128), F32)
    lat = jnp.reshape(lax.axis_index("lat"), (1,)).astype(jnp.int32)
    operands = (*fields, *weights)
    vmem = pl.BlockSpec(memory_space=pltpu.VMEM)
    return pl.pallas_call(
        functools.partial(blocks_kernel, lat_devices=lat_devices),
        in_specs=[pl.BlockSpec(memory_space=pltpu.SMEM)] + [vmem] * len(operands),
        out_specs=[vmem, vmem],
        out_shape=[
            jax.ShapeDtypeStruct((ROWS, COLS, CHANS), BF16),
            jax.ShapeDtypeStruct((TILES, 2, 8, 128), BF16),
        ],
        scratch_shapes=[wide, slim, wide, wide, wide, pltpu.VMEM((FLAT, 128), F32), wide]
        + [slim] * 3
        + [taps] * 4
        + [square] * 2
        + [local] * 4
        + [pltpu.VMEM((2, ROWS * COLS, 128), F32)]
        + [taps] * 2
        + [eight] * 2
        + [pltpu.VMEM((2, PITCH * TALL, 128), F32)]
        + [pltpu.VMEM((2, LEAD + INNER * ROWS + 16, 128), F32)],
        compiler_params=pltpu.CompilerParams(vmem_limit_bytes=60 * 1024 * 1024),
        name="both_blocks",
    )(lat, *operands)


def unpack_kernel(packed, embed, kernel1, kernel2, point1, point2, gain1, gain2, *, factor):
    for h in (0, 1):
        lanes = slice(128 * h, 128 * h + 128)
        point1[:, lanes] = packed[0:32, h].astype(F32).reshape(CHANS, 128) * factor
        point2[:, lanes] = packed[32:64, h].astype(F32).reshape(CHANS, 128) * factor
        mixed = packed[64:73, h].astype(F32).reshape(72, 128) * factor
        embed[:, lanes] = mixed[:VARS]
        gain1[:, lanes] = mixed[VARS : VARS + 1]
        gain2[:, lanes] = mixed[VARS + 1 : VARS + 2]
        kernel1[:, lanes] = (packed[73:77, h].astype(F32).reshape(32, 128) * factor)[:25]
        kernel2[:, lanes] = (packed[77:81, h].astype(F32).reshape(32, 128) * factor)[:25]


def summed(packed, factor):
    devices = lax.axis_size(AXES)
    parts = lax.all_to_all(packed, AXES, 0, 0, tiled=True)
    mine = jnp.sum(parts.reshape(devices, -1, 2, 8, 128).astype(F32), 0).astype(BF16)
    total = lax.all_to_all(jnp.tile(mine, (devices, 1, 1, 1)), AXES, 0, 0, tiled=True)
    shapes = [(VARS, CHANS), (25, CHANS), (25, CHANS), (CHANS, CHANS), (CHANS, CHANS)]
    results = pl.pallas_call(
        functools.partial(unpack_kernel, factor=factor),
        out_shape=[jax.ShapeDtypeStruct(s, F32) for s in shapes + [(1, CHANS)] * 2],
        name="unpack",
    )(total)
    return (*results[:5], results[5].reshape(CHANS), results[6].reshape(CHANS))


def shifted(before, after, axis, wrap):
    devices = lax.axis_size(axis)
    up = [(i, (i + 1) % devices) for i in range(devices if wrap else devices - 1)]
    down = [(j, i) for i, j in up]
    return lax.ppermute(after, axis, up), lax.ppermute(before, axis, down)


def on_device(points, row_len, w_embed, kernel1, gain1, point1, kernel2, gain2, point2, cotangent):
    lon_total = COLS * lax.axis_size("lon")
    rows_total = ROWS * lax.axis_size("lat")
    cot_left, cot_right = shifted(
        cotangent[:, :4].reshape(ROWS // 2, 8, CHANS),
        cotangent[:, COLS - 4 :].reshape(ROWS // 2, 8, CHANS),
        "lon",
        True,
    )
    high, low, west, east = regrid(jnp.swapaxes(points, 0, 1), row_len, lon_total)
    left, right = shifted(west, east, "lon", True)

    def cot_band(rows, pairs):
        sides = [c[pairs].reshape(4, 4, CHANS) for c in (cot_left, cot_right)]
        return jnp.concatenate([sides[0], cotangent[rows], sides[1]], 1)

    cot_above, cot_below = shifted(
        cot_band(slice(0, 4), slice(0, 2)),
        cot_band(slice(ROWS - 4, ROWS), slice(ROWS // 2 - 2, ROWS // 2)),
        "lat",
        False,
    )
    above, below = shifted(
        jnp.concatenate([left[:, :STRIP], high[:, :GROUP], right[:, :STRIP]], 1),
        jnp.concatenate([left[:, -STRIP:], high[:, -GROUP:], right[:, -STRIP:]], 1),
        "lat",
        False,
    )
    fields = (
        high, low, left, right, above, below,
        cotangent, cot_left, cot_right, cot_above, cot_below,
    )
    weights = (
        w_embed, kernel1, gain1.reshape(1, CHANS), point1,
        kernel2, gain2.reshape(1, CHANS), point2,
    )
    out, packed = blocks(fields, weights, lax.axis_size("lat"))
    return (out, *summed(packed, float(rows_total * lon_total) ** (-0.5)))


def solution(mesh):
    in_specs = (
        P("lat", None, "lon"),
        P("lat"),
        P(),
        P(),
        P(),
        P(),
        P(),
        P(),
        P(),
        P("lat", "lon", None),
    )
    out_specs = (P("lat", "lon", None), P(), P(), P(), P(), P(), P(), P())
    return jax.shard_map(
        on_device, mesh=mesh, in_specs=in_specs, out_specs=out_specs, check_vma=False
    )
```

```python
import functools

import jax
import jax.numpy as jnp
from jax import lax
from jax.experimental import pallas as pl
from jax.experimental.pallas import tpu as pltpu
from jax.sharding import PartitionSpec as P

F32 = jnp.float32
BF16 = jnp.bfloat16
ROWS = 64
COLS = 24
HALO = 8
PITCH = COLS + 2 * HALO
TALL = ROWS + 2 * HALO
INNER = COLS + 8
LEAD = 16
FLAT = LEAD + PITCH * TALL + 16
SLIM = LEAD + INNER * TALL + 16
CHANS = 256
VARS = 69
TILES = 128
AXES = ("lon", "lat")


GROUP = 8 * COLS
STRIP = 8 * HALO


def regrid_kernel(row_len, sector, points, values, west, east, *, lon_total):
    first = (sector[0] * COLS).astype(F32)
    whole = lon_total // 4
    lane = lax.broadcasted_iota(jnp.int32, (8, GROUP), 1)
    row = lane % 8
    cell = first + (lane // 8).astype(F32)
    own = lax.broadcasted_iota(jnp.int32, (8, GROUP), 0) == row
    own = jnp.where(own, 1.0 / whole, 0.0)
    every8 = lax.broadcasted_iota(jnp.int32, (VARS, 8 * VARS), 1) // 8
    fold = jnp.where(every8 == lax.broadcasted_iota(jnp.int32, every8.shape, 0), 1.0, 0.0)
    fold = fold.astype(BF16)
    mark = lax.broadcasted_iota(jnp.int32, (points.shape[3], GROUP), 0).astype(F32)
    found = []
    for k in range(points.shape[1]):
        group = pl.program_id(0) * points.shape[1] + k
        count = jnp.zeros((8, GROUP), F32)
        for q in range(8):
            count = jnp.where(row == q, row_len[8 * group + q].astype(F32), count)
        product = cell * count
        lower = jnp.floor((product + 2.0) * (1.0 / lon_total))
        start = jnp.floor((first * count + 2.0) * (1.0 / lon_total))
        share = (product - lower * lon_total) * 0.25
        away = mark - (lower - start)[:1]
        mix = jnp.where(
            away == 0.0, whole - share[:1], jnp.where(away == 1.0, share[:1], 0.0)
        )
        rows = points[:, k].reshape(VARS * 8, points.shape[3])
        every = jnp.dot(rows, mix.astype(BF16), preferred_element_type=F32)
        kept = (every.reshape(VARS, 8, GROUP) * own[None]).reshape(VARS * 8, GROUP)
        found.append(jnp.dot(fold, kept.astype(BF16), preferred_element_type=F32))
    values[...] = jnp.concatenate(found, 1).astype(BF16)
    west[...] = jnp.concatenate([f[:, :STRIP] for f in found], 1).astype(BF16)
    east[...] = jnp.concatenate([f[:, GROUP - STRIP :] for f in found], 1).astype(BF16)


def regrid(points, row_len, lon_total):
    nvars, nrows, slots = points.shape
    groups = 2
    steps = nrows // (8 * groups)
    strips = jax.ShapeDtypeStruct((nvars, nrows * HALO), BF16)
    full = jax.ShapeDtypeStruct((nvars, nrows * COLS), BF16)
    return pl.pallas_call(
        functools.partial(regrid_kernel, lon_total=lon_total),
        grid_spec=pltpu.PrefetchScalarGridSpec(
            num_scalar_prefetch=2,
            grid=(steps,),
            in_specs=[pl.BlockSpec((nvars, groups, 8, slots), lambda i, *_: (0, i, 0, 0))],
            out_specs=[
                pl.BlockSpec((nvars, groups * GROUP), lambda i, *_: (0, i)),
                pl.BlockSpec((nvars, groups * STRIP), lambda i, *_: (0, i)),
                pl.BlockSpec((nvars, groups * STRIP), lambda i, *_: (0, i)),
            ],
        ),
        out_shape=[full, strips, strips],
        name="regrid",
    )(
        row_len,
        jnp.reshape(lax.axis_index("lon"), (1,)).astype(jnp.int32),
        points.reshape(nvars, nrows // 8, 8, slots),
    )


def at(row):
    return LEAD + PITCH * row


def inner(row):
    return LEAD + INNER * row


def conv(source, half, start, pitch, rows, cols, taps, visit=None):
    sums = [None] * rows
    for e in range(5):
        weights = [taps[half, 5 * a + e] for a in range(5)]
        for i in range(rows + 4):
            x = source[half, pl.ds(start + pitch * (i - 2) + e - 2, cols), :]
            x = x.reshape(cols // 8, 8, 128)
            for a in range(5):
                r = i - a
                if 0 <= r < rows:
                    term = x * weights[a]
                    sums[r] = term if sums[r] is None else sums[r] + term
                    if visit is not None:
                        visit(a, e, r, x)
        if visit is not None:
            visit(None, e, None, None)
    return sums


def own_tiles(x):
    later = lax.broadcasted_iota(jnp.int32, (8, 128), 0) >= 4
    return jnp.stack([jnp.where(later, x[0], x[3]), x[1], x[2]])


class TapSums:
    def __init__(self, store, half, centre):
        self.store, self.half, self.centre, self.live = store, half, centre, {}
        self.seen = self.own = None

    def __call__(self, a, e, r, x):
        if a is None:
            for tap, value in self.live.items():
                self.store[self.half, tap] += value
            self.live = {}
            return
        tap = 24 - (5 * a + e)
        if x.shape[0] == 4:
            if self.seen is not x:
                self.seen, self.own = x, own_tiles(x)
            x = self.own
        term = jnp.sum(self.centre[r] * x, 0)
        self.live[tap] = term if tap not in self.live else self.live[tap] + term


def blocks_kernel(
    lat, regridded, left, right, above, below, cot, cot_left, cot_right,
    w_embed, kernel1, gain1, point1, kernel2, gain2, point2,
    out, packed,
    x0, cots, d, h1, xhat1, scale1, slope1, dd2, g1, dd1,
    taps1, taps2, flip1, flip2, half1, half2, turned1, turned2,
    u1, dp1, u2, dp2, g0, gk1, gk2, gg1, gg2, swap, lifted,
    *, lat_devices,
):
    halves = (slice(0, 128), slice(128, 256))

    for k in range(25):
        for h in (0, 1):
            one = jnp.broadcast_to(kernel1[k : k + 1, halves[h]].astype(F32), (8, 128))
            two = jnp.broadcast_to(kernel2[k : k + 1, halves[h]].astype(F32), (8, 128))
            taps1[h, k] = one
            flip1[h, 24 - k] = one
            taps2[h, k] = two
            flip2[h, 24 - k] = two
    for point, half, turned in ((point1, half1, turned1), (point2, half2, turned2)):
        value = point[...].astype(F32) * 0.5
        half[...] = value.astype(BF16)
        turned[...] = jnp.transpose(value).astype(BF16)
    zeros = jnp.zeros((8, 128), F32)
    for h in (0, 1):
        for ref in (gg1, gg2):
            ref[h] = zeros
        for ref in (gk1, gk2):
            ref[h] = jnp.zeros((25, 8, 128), F32)
        for ref, size in ((x0, FLAT), (h1, FLAT), (dd2, SLIM), (dd1, SLIM)):
            ref[h, 0:LEAD] = jnp.zeros((LEAD, 128), F32)
            ref[h, size - 16 : size] = jnp.zeros((16, 128), F32)

    weight = w_embed[...]

    def across(a, b):
        return lax.dot_general(a, b, (((0,), (0,)), ((), ())), preferred_element_type=F32)

    def embed(spot, values):
        values = values.astype(BF16).astype(F32)
        for h in (0, 1):
            swap[h, pl.ds(pl.multiple_of(spot, 64), values.shape[0]), :] = values[:, halves[h]]

    def spread(spot, row):
        for k in range(8):
            for h in (0, 1):
                x0[h, pl.ds(pl.multiple_of(at(row + k), 8), PITCH), :] = swap[
                    h, pl.ds(spot + k, PITCH, stride=8), :
                ]

    for i in range(ROWS // 16):
        edge = slice(2 * STRIP * i, 2 * STRIP * (i + 1))
        middle = slice(2 * GROUP * i, 2 * GROUP * (i + 1))
        west = across(left[:, edge], weight)
        east = across(right[:, edge], weight)
        centre = across(regridded[:, middle], weight)
        for k in (0, 1):
            spot = 8 * PITCH * (2 * i + k)
            embed(spot, west[STRIP * k : STRIP * (k + 1)])
            embed(spot + STRIP, centre[GROUP * k : GROUP * (k + 1)])
            embed(spot + STRIP + GROUP, east[STRIP * k : STRIP * (k + 1)])
    for k, given in ((0, above), (1, below)):
        spot = 8 * PITCH * (ROWS // 8 + k)
        embed(spot, across(given[128 : 128 + VARS], weight))
        embed(spot + CHANS, across(given[208 : 208 + VARS, : 8 * PITCH - CHANS], weight))

    def unravel(i, carry):
        spread(8 * PITCH * i, HALO + 8 * i)
        return carry

    lax.fori_loop(0, ROWS // 8, unravel, 0)
    spread(8 * PITCH * (ROWS // 8), 0)
    spread(8 * PITCH * (ROWS // 8 + 1), HALO + ROWS)

    later = lax.broadcasted_iota(jnp.int32, (8, 128), 0) >= 4

    def put(row, value):
        for h in (0, 1):
            cots[h, pl.ds(pl.multiple_of(inner(row), 8), INNER), :] = value[:, halves[h]]

    def fill(pair, carry):
        sides = [cot_left[pair].astype(F32), cot_right[pair].astype(F32)]
        for odd in (0, 1):
            row = 2 * pair + odd
            edges = [s[4 * odd : 4 * odd + 4] for s in sides]
            put(
                row + HALO, jnp.concatenate([edges[0], cot[row].astype(F32), edges[1]], 0)
            )
        return carry

    lax.fori_loop(0, ROWS // 2, fill, 0)
    for k in range(4):
        rows = slice(INNER * k, INNER * (k + 1))
        put(k + 4, above[rows].astype(F32))
        put(k + HALO + ROWS, below[rows].astype(F32))

    def get(ref, start, count):
        return [ref[h, pl.ds(pl.multiple_of(start, 8), count), :] for h in (0, 1)]

    def keep(ref, start, values):
        for h in (0, 1):
            ref[h, pl.ds(pl.multiple_of(start, 8), values[h].shape[0]), :] = values[h]

    def from_wide(ref, row, rows):
        return [
            jnp.concatenate(
                [ref[h, pl.ds(at(row + r) + 4, INNER), :] for r in range(rows)], 0
            )
            for h in (0, 1)
        ]

    def joined(sums):
        return jnp.concatenate(sums, 0).reshape(-1, 128)

    def local_part(x):
        x = x.reshape(-1, 4, 8, 128)
        ends = jnp.where(later, x[:, 0], x[:, 3])
        return jnp.stack([ends, x[:, 1], x[:, 2]], 1).reshape(-1, 128)

    def gains(ref):
        return [ref[:, halves[h]] for h in (0, 1)]

    def normalised(raw):
        mean = jnp.sum(raw[0] * raw[0] + raw[1] * raw[1], -1, keepdims=True) * (1.0 / CHANS)
        scale = lax.rsqrt(mean + 1e-06)
        return scale, [raw[h] * scale for h in (0, 1)]

    def activated(xhat, gain, point):
        u = [xhat[h] * gain[h] for h in (0, 1)]
        p = jnp.dot(
            jnp.concatenate(u, 1).astype(BF16), point[...], preferred_element_type=F32
        )
        p = [p[:, s] for s in halves]
        rise = [jnp.tanh(v) + 1.0 for v in p]
        silu = [p[h] * rise[h] for h in (0, 1)]
        slope = [rise[h] + silu[h] * (2.0 - rise[h]) for h in (0, 1)]
        return u, silu, slope

    def through_norm(grad, slope, xhat, scale, gain, turned):
        dp = [grad[h] * slope[h] for h in (0, 1)]
        du = jnp.dot(
            jnp.concatenate(dp, 1).astype(BF16), turned[...], preferred_element_type=F32
        )
        gained = [du[:, halves[h]] * gain[h] for h in (0, 1)]
        both = [gained[h] * xhat[h] for h in (0, 1)]
        mean = jnp.sum(both[0] + both[1], -1, keepdims=True) * (1.0 / CHANS)
        dd = [
            (scale * (gained[h] - xhat[h] * mean)).astype(BF16).astype(F32) for h in (0, 1)
        ]
        return dp, both, dd

    def gain_sums(store, both):
        for h in (0, 1):
            store[h] += jnp.sum(local_part(both[h]).reshape(-1, 8, 128), 0)

    def pipeline(blocks, first, second):
        first(0)

        def step(i, carry):
            second(i - 1)
            first(i)
            return carry

        lax.fori_loop(1, blocks, step, 0)
        second(blocks - 1)

    size = 4 * PITCH

    def first_conv(i):
        start = at(2) + i * size
        keep(d, start, [joined(conv(x0, h, start, PITCH, 4, PITCH, taps1)) for h in (0, 1)])

    def first_mix(i):
        start = at(2) + i * size
        scale, xhat = normalised(get(d, start, size))
        _, silu, slope = activated(xhat, gains(gain1), half1)
        x = get(x0, start, size)
        keep(h1, start, [(x[h] + silu[h]).astype(BF16).astype(F32) for h in (0, 1)])
        keep(xhat1, start, xhat)
        keep(slope1, start, slope)
        scale1[pl.ds(pl.multiple_of(start, 8), size), :] = jnp.broadcast_to(scale, (size, 128))

    pipeline((TALL - 4) // 4, first_conv, first_mix)

    @pl.when(lat[0] == 0)
    def _():
        for h in (0, 1):
            h1[h, at(2) : at(HALO)] = jnp.zeros((6 * PITCH, 128), F32)

    @pl.when(lat[0] == lat_devices - 1)
    def _():
        for h in (0, 1):
            h1[h, at(HALO + ROWS) : at(HALO + ROWS + 6)] = jnp.zeros((6 * PITCH, 128), F32)

    def second_conv(row):
        keep(
            d,
            inner(row),
            [joined(conv(h1, h, at(row) + 4, PITCH, 4, INNER, taps2)) for h in (0, 1)],
        )

    def second_mix(row, local):
        start = inner(row)
        scale, xhat = normalised(get(d, start, 4 * INNER))
        gain = gains(gain2)
        u, silu, slope = activated(xhat, gain, half2)
        dp, both, dd = through_norm(
            get(cots, start, 4 * INNER), slope, xhat, scale, gain, turned2
        )
        keep(dd2, start, dd)
        if local is not None:
            keep(lifted, LEAD + 4 * INNER * local, silu)
            spot = pl.ds(pl.multiple_of(local * 96, 96), 96)
            u2[spot] = jnp.concatenate([local_part(v) for v in u], 1).astype(BF16)
            dp2[spot] = jnp.concatenate([local_part(v) for v in dp], 1).astype(BF16)
            gain_sums(gg2, both)

    def result(i):
        total = []
        for h in (0, 1):
            rows = []
            for r in range(4):
                place = LEAD + INNER * (4 * i + r) + 4
                base = h1[h, pl.ds(pl.multiple_of(at(HALO + 4 * i + r) + HALO, 8), COLS), :]
                rows.append(base + lifted[h, pl.ds(place, COLS), :])
            total.append(jnp.concatenate(rows, 0))
        out[pl.ds(i * 4, 4)] = jnp.concatenate(total, 1).reshape(4, COLS, CHANS).astype(BF16)

    for row in (4, HALO + ROWS):
        second_conv(row)
    for row in (4, HALO + ROWS):
        second_mix(row, None)
    pipeline(
        ROWS // 4,
        lambda i: second_conv(HALO + 4 * i),
        lambda i: second_mix(HALO + 4 * i, i),
    )

    def third_conv(row, rows, local):
        start = inner(row)
        total = []
        for h in (0, 1):
            visit = None
            if local:
                centre = [
                    own_tiles(h1[h, pl.ds(at(row + r) + 4, INNER), :].reshape(4, 8, 128))
                    for r in range(rows)
                ]
                visit = TapSums(gk2, h, centre)
            sums = joined(conv(dd2, h, start, INNER, rows, INNER, flip2, visit))
            total.append(sums + cots[h, pl.ds(pl.multiple_of(start, 8), rows * INNER), :])
        keep(g1, start, total)

    def third_mix(row, rows, local):
        start = inner(row)
        gain = gains(gain1)
        xhat = from_wide(xhat1, row, rows)
        scale = jnp.concatenate(
            [scale1[pl.ds(at(row + r) + 4, INNER), :] for r in range(rows)], 0
        )
        dp, both, dd = through_norm(
            get(g1, start, rows * INNER), from_wide(slope1, row, rows), xhat, scale, gain, turned1
        )
        keep(dd1, start, dd)
        if local is not None:
            spot = pl.ds(pl.multiple_of(local * 96, 96), 96)
            u = [local_part(xhat[h] * gain[h]) for h in (0, 1)]
            u1[spot] = jnp.concatenate(u, 1).astype(BF16)
            dp1[spot] = jnp.concatenate([local_part(v) for v in dp], 1).astype(BF16)
            gain_sums(gg1, both)
            result(local)

    for row in (6, HALO + ROWS):
        third_conv(row, 2, False)
    for row in (6, HALO + ROWS):
        third_mix(row, 2, None)
    pipeline(
        ROWS // 4,
        lambda i: third_conv(HALO + 4 * i, 4, True),
        lambda i: third_mix(HALO + 4 * i, 4, i),
    )

    @pl.when(lat[0] == 0)
    def _():
        for h in (0, 1):
            dd1[h, inner(6) : inner(HALO)] = jnp.zeros((2 * INNER, 128), F32)

    @pl.when(lat[0] == lat_devices - 1)
    def _():
        for h in (0, 1):
            dd1[h, inner(HALO + ROWS) : inner(HALO + ROWS + 2)] = jnp.zeros(
                (2 * INNER, 128), F32
            )

    def fourth(i, carry):
        row = HALO + 4 * i
        for h in (0, 1):
            centre = [
                x0[h, pl.ds(pl.multiple_of(at(row + r) + HALO, 8), COLS), :].reshape(3, 8, 128)
                for r in range(4)
            ]
            sums = conv(dd1, h, inner(row) + 4, INNER, 4, COLS, flip1, TapSums(gk1, h, centre))
            for r in range(4):
                base = g1[h, pl.ds(inner(row + r) + 4, COLS), :]
                place = GROUP * (i // 2) + 4 * (i % 2) + r
                g0[h, pl.ds(place, COLS, stride=8), :] = sums[r].reshape(COLS, 128) + base
        return carry

    lax.fori_loop(0, ROWS // 4, fourth, 0)

    def pack(place, value):
        rows = value.shape[0]
        value = value.astype(BF16)
        for h in (0, 1):
            packed[place : place + rows // 8, h] = value[:, halves[h]].reshape(rows // 8, 8, 128)

    pack(0, across(u1[...], dp1[...]) * 0.5)
    pack(32, across(u2[...], dp2[...]) * 0.5)
    field = jnp.concatenate([g0[h] for h in (0, 1)], 1).astype(BF16)
    embedded = jnp.dot(regridded[...], field, preferred_element_type=F32)

    def gain_row(ref, gain):
        total = [jnp.sum(ref[h], 0, keepdims=True) for h in (0, 1)]
        return jnp.concatenate(total, 1) / gain[...]

    pack(
        64,
        jnp.concatenate(
            [embedded, gain_row(gg1, gain1), gain_row(gg2, gain2), jnp.zeros((1, CHANS), F32)], 0
        ),
    )
    for place, ref in ((73, gk1), (77, gk2)):
        total = jnp.concatenate([jnp.sum(ref[h], 1) for h in (0, 1)], 1)
        pack(place, jnp.concatenate([total, jnp.zeros((7, CHANS), F32)], 0))
    packed[81:TILES] = jnp.zeros((TILES - 81, 2, 8, 128), BF16)


def blocks(fields, weights, lat_devices):
    wide = pltpu.VMEM((2, FLAT, 128), F32)
    slim = pltpu.VMEM((2, SLIM, 128), F32)
    taps = pltpu.VMEM((2, 25, 8, 128), F32)
    square = pltpu.VMEM((CHANS, CHANS), BF16)
    local = pltpu.VMEM((ROWS * COLS, CHANS), BF16)
    eight = pltpu.VMEM((2, 8, 128), F32)
    lat = jnp.reshape(lax.axis_index("lat"), (1,)).astype(jnp.int32)
    operands = (*fields, *weights)
    vmem = pl.BlockSpec(memory_space=pltpu.VMEM)
    return pl.pallas_call(
        functools.partial(blocks_kernel, lat_devices=lat_devices),
        in_specs=[pl.BlockSpec(memory_space=pltpu.SMEM)] + [vmem] * len(operands),
        out_specs=[vmem, vmem],
        out_shape=[
            jax.ShapeDtypeStruct((ROWS, COLS, CHANS), BF16),
            jax.ShapeDtypeStruct((TILES, 2, 8, 128), BF16),
        ],
        scratch_shapes=[wide, slim, wide, wide, wide, pltpu.VMEM((FLAT, 128), F32), wide]
        + [slim] * 3
        + [taps] * 4
        + [square] * 4
        + [local] * 4
        + [pltpu.VMEM((2, ROWS * COLS, 128), F32)]
        + [taps] * 2
        + [eight] * 2
        + [pltpu.VMEM((2, PITCH * TALL, 128), F32)]
        + [pltpu.VMEM((2, LEAD + INNER * ROWS + 16, 128), F32)],
        compiler_params=pltpu.CompilerParams(vmem_limit_bytes=60 * 1024 * 1024),
        name="both_blocks",
    )(lat, *operands)


def unpack_kernel(packed, embed, kernel1, kernel2, point1, point2, gain1, gain2, *, factor):
    for h in (0, 1):
        lanes = slice(128 * h, 128 * h + 128)
        point1[:, lanes] = packed[0:32, h].astype(F32).reshape(CHANS, 128) * factor
        point2[:, lanes] = packed[32:64, h].astype(F32).reshape(CHANS, 128) * factor
        mixed = packed[64:73, h].astype(F32).reshape(72, 128) * factor
        embed[:, lanes] = mixed[:VARS]
        gain1[:, lanes] = mixed[VARS : VARS + 1]
        gain2[:, lanes] = mixed[VARS + 1 : VARS + 2]
        kernel1[:, lanes] = (packed[73:77, h].astype(F32).reshape(32, 128) * factor)[:25]
        kernel2[:, lanes] = (packed[77:81, h].astype(F32).reshape(32, 128) * factor)[:25]


def summed(packed, factor):
    devices = lax.axis_size(AXES)
    parts = lax.all_to_all(packed, AXES, 0, 0, tiled=True)
    mine = jnp.sum(parts.reshape(devices, -1, 2, 8, 128).astype(F32), 0).astype(BF16)
    total = lax.all_to_all(jnp.tile(mine, (devices, 1, 1, 1)), AXES, 0, 0, tiled=True)
    shapes = [(VARS, CHANS), (25, CHANS), (25, CHANS), (CHANS, CHANS), (CHANS, CHANS)]
    results = pl.pallas_call(
        functools.partial(unpack_kernel, factor=factor),
        out_shape=[jax.ShapeDtypeStruct(s, F32) for s in shapes + [(1, CHANS)] * 2],
        name="unpack",
    )(total)
    return (*results[:5], results[5].reshape(CHANS), results[6].reshape(CHANS))


def shifted(before, after, axis, wrap):
    devices = lax.axis_size(axis)
    up = [(i, (i + 1) % devices) for i in range(devices if wrap else devices - 1)]
    down = [(j, i) for i, j in up]
    return lax.ppermute(after, axis, up), lax.ppermute(before, axis, down)


def on_device(points, row_len, w_embed, kernel1, gain1, point1, kernel2, gain2, point2, cotangent):
    lon_total = COLS * lax.axis_size("lon")
    rows_total = ROWS * lax.axis_size("lat")
    cot_left, cot_right = shifted(
        cotangent[:, :4].reshape(ROWS // 2, 8, CHANS),
        cotangent[:, COLS - 4 :].reshape(ROWS // 2, 8, CHANS),
        "lon",
        True,
    )
    values, west, east = regrid(jnp.swapaxes(points, 0, 1), row_len, lon_total)
    left, right = shifted(west, east, "lon", True)

    def band(rows, pairs, lanes, edge):
        sides = [c[pairs].reshape(4, 4, CHANS) for c in (cot_left, cot_right)]
        given = jnp.concatenate([sides[0], cotangent[rows], sides[1]], 1).reshape(-1, CHANS)
        field = jnp.concatenate([left[:, edge], values[:, lanes], right[:, edge]], 1)
        pieces = [field[:, :CHANS], field[:, CHANS:]]
        pieces = [
            jnp.pad(x, ((0, 80 - VARS), (0, CHANS - x.shape[1]))) for x in pieces
        ]
        return jnp.concatenate([given, *pieces], 0)

    above, below = shifted(
        band(slice(0, 4), slice(0, 2), slice(0, GROUP), slice(0, STRIP)),
        band(
            slice(ROWS - 4, ROWS),
            slice(ROWS // 2 - 2, ROWS // 2),
            slice(GROUP * (ROWS // 8 - 1), GROUP * (ROWS // 8)),
            slice(STRIP * (ROWS // 8 - 1), STRIP * (ROWS // 8)),
        ),
        "lat",
        False,
    )
    fields = (values, left, right, above, below, cotangent, cot_left, cot_right)
    weights = (
        w_embed, kernel1, gain1.reshape(1, CHANS), point1,
        kernel2, gain2.reshape(1, CHANS), point2,
    )
    out, packed = blocks(fields, weights, lax.axis_size("lat"))
    return (out, *summed(packed, float(rows_total * lon_total) ** (-0.5)))


def solution(mesh):
    in_specs = (
        P("lat", None, "lon"),
        P("lat"),
        P(),
        P(),
        P(),
        P(),
        P(),
        P(),
        P(),
        P("lat", "lon", None),
    )
    out_specs = (P("lat", "lon", None), P(), P(), P(), P(), P(), P(), P())
    return jax.shard_map(
        on_device, mesh=mesh, in_specs=in_specs, out_specs=out_specs, check_vma=False
    )
```

```python
import functools

import jax
import jax.numpy as jnp
from jax import lax
from jax.experimental import pallas as pl
from jax.experimental.pallas import tpu as pltpu
from jax.sharding import PartitionSpec as P

F32 = jnp.float32
BF16 = jnp.bfloat16
ROWS = 64
COLS = 24
HALO = 8
PITCH = COLS + 2 * HALO
TALL = ROWS + 2 * HALO
INNER = COLS + 8
LEAD = 16
FLAT = LEAD + PITCH * TALL + 16
SLIM = LEAD + INNER * TALL + 16
CHANS = 256
VARS = 69
TILES = 128
AXES = ("lon", "lat")


GROUP = 8 * COLS
STRIP = 8 * HALO


def regrid_kernel(row_len, sector, points, values, west, east, held, arrived, *, lon_total):
    batch = held.shape[2]
    copies = [
        pltpu.make_async_copy(
            points.at[:, batch * i : batch * (i + 1)], held.at[i], arrived.at[i]
        )
        for i in range(held.shape[0])
    ]
    for copy in copies:
        copy.start()
    first = (sector[0] * COLS).astype(F32)
    whole = lon_total // 4
    lane = lax.broadcasted_iota(jnp.int32, (8, GROUP), 1)
    row = lane % 8
    cell = first + (lane // 8).astype(F32)
    own = lax.broadcasted_iota(jnp.int32, (8, GROUP), 0) == row
    own = jnp.where(own, 1.0 / whole, 0.0)
    every8 = lax.broadcasted_iota(jnp.int32, (VARS, 8 * VARS), 1) // 8
    fold = jnp.where(every8 == lax.broadcasted_iota(jnp.int32, every8.shape, 0), 1.0, 0.0)
    fold = fold.astype(BF16)
    slots = points.shape[3]
    mark = lax.broadcasted_iota(jnp.int32, (slots, GROUP), 0).astype(F32)
    for i, copy in enumerate(copies):
        found = []
        copy.wait()
        for k in range(batch):
            count = jnp.zeros((8, GROUP), F32)
            for q in range(8):
                length = row_len[8 * (batch * i + k) + q]
                count = jnp.where(row == q, length.astype(F32), count)
            product = cell * count
            lower = jnp.floor((product + 2.0) * (1.0 / lon_total))
            start = jnp.floor((first * count + 2.0) * (1.0 / lon_total))
            share = (product - lower * lon_total) * 0.25
            away = mark - (lower - start)[:1]
            mix = jnp.where(
                away == 0.0, whole - share[:1], jnp.where(away == 1.0, share[:1], 0.0)
            )
            rows = held[i, :, k].reshape(VARS * 8, slots)
            every = jnp.dot(rows, mix.astype(BF16), preferred_element_type=F32)
            kept = (every.reshape(VARS, 8, GROUP) * own[None]).reshape(VARS * 8, GROUP)
            found.append(jnp.dot(fold, kept.astype(BF16), preferred_element_type=F32))
        lanes = slice(batch * GROUP * i, batch * GROUP * (i + 1))
        edge = slice(batch * STRIP * i, batch * STRIP * (i + 1))
        values[:, lanes] = jnp.concatenate(found, 1).astype(BF16)
        west[:, edge] = jnp.concatenate([f[:, :STRIP] for f in found], 1).astype(BF16)
        east[:, edge] = jnp.concatenate([f[:, GROUP - STRIP :] for f in found], 1).astype(BF16)


def regrid(points, row_len, lon_total):
    nvars, nrows, slots = points.shape
    batches = 2
    strips = jax.ShapeDtypeStruct((nvars, nrows * HALO), BF16)
    full = jax.ShapeDtypeStruct((nvars, nrows * COLS), BF16)
    smem = pl.BlockSpec(memory_space=pltpu.SMEM)
    vmem = pl.BlockSpec(memory_space=pltpu.VMEM)
    return pl.pallas_call(
        functools.partial(regrid_kernel, lon_total=lon_total),
        in_specs=[smem, smem, pl.BlockSpec(memory_space=pl.ANY)],
        out_specs=[vmem] * 3,
        out_shape=[full, strips, strips],
        scratch_shapes=[
            pltpu.VMEM((batches, nvars, nrows // (8 * batches), 8, slots), BF16),
            pltpu.SemaphoreType.DMA((batches,)),
        ],
        name="regrid",
    )(
        row_len,
        jnp.reshape(lax.axis_index("lon"), (1,)).astype(jnp.int32),
        points.reshape(nvars, nrows // 8, 8, slots),
    )


BAND = 288


def bands_kernel(*refs):
    for k, band in ((0, refs[12]), (1, refs[13])):
        values, left, right, cot, cot_left, cot_right = (ref[...] for ref in refs[k:12:2])
        for row in range(4):
            edge = slice(4 * (row % 2), 4 * (row % 2) + 4)
            whole = [cot_left[row // 2].astype(F32)[edge], cot[row].astype(F32)]
            whole.append(cot_right[row // 2].astype(F32)[edge])
            band[INNER * row : INNER * (row + 1)] = jnp.concatenate(whole, 0).astype(BF16)
        edge = slice(STRIP * k, STRIP * (k + 1))
        lanes = slice(GROUP * k, GROUP * (k + 1))
        field = [x.astype(F32) for x in (left[:, edge], values[:, lanes], right[:, edge])]
        field = jnp.concatenate(field, 1).astype(BF16)
        band[128 : 128 + VARS] = field[:, :CHANS]
        band[208 : 208 + VARS, : 8 * PITCH - CHANS] = field[:, CHANS:]


def bands(values, left, right, cot, cot_left, cot_right):
    def ends(array, dim, size):
        shape = tuple(size if i == dim else n for i, n in enumerate(array.shape))
        last = array.shape[dim] // size - 1

        def spec(place):
            index = tuple(place if i == dim else 0 for i in range(len(shape)))
            return pl.BlockSpec(shape, lambda _: index)

        return [spec(0), spec(last)]

    kinds = (
        (values, 1, 2 * GROUP), (left, 1, 2 * STRIP), (right, 1, 2 * STRIP),
        (cot, 0, 4), (cot_left, 0, 2), (cot_right, 0, 2),
    )
    band = jax.ShapeDtypeStruct((BAND, CHANS), BF16)
    full = pl.BlockSpec((BAND, CHANS), lambda _: (0, 0))
    return pl.pallas_call(
        bands_kernel,
        grid=(1,),
        in_specs=[spec for kind in kinds for spec in ends(*kind)],
        out_specs=[full, full],
        out_shape=[band, band],
        name="bands",
    )(*[kind[0] for kind in kinds for _ in (0, 1)])


def at(row):
    return LEAD + PITCH * row


def inner(row):
    return LEAD + INNER * row


def conv(source, half, start, pitch, rows, cols, taps, visit=None):
    sums = [None] * rows
    for e in range(5):
        weights = [taps[half, 5 * a + e] for a in range(5)]
        for i in range(rows + 4):
            x = source[half, pl.ds(start + pitch * (i - 2) + e - 2, cols), :]
            x = x.reshape(cols // 8, 8, 128)
            for a in range(5):
                r = i - a
                if 0 <= r < rows:
                    term = x * weights[a]
                    sums[r] = term if sums[r] is None else sums[r] + term
                    if visit is not None:
                        visit(a, e, r, x)
        if visit is not None:
            visit(None, e, None, None)
    return sums


def own_tiles(x):
    later = lax.broadcasted_iota(jnp.int32, (8, 128), 0) >= 4
    return jnp.stack([jnp.where(later, x[0], x[3]), x[1], x[2]])


class TapSums:
    def __init__(self, store, half, centre):
        self.store, self.half, self.centre, self.live = store, half, centre, {}
        self.seen = self.own = None

    def __call__(self, a, e, r, x):
        if a is None:
            for tap, value in self.live.items():
                self.store[self.half, tap] += value
            self.live = {}
            return
        tap = 24 - (5 * a + e)
        if x.shape[0] == 4:
            if self.seen is not x:
                self.seen, self.own = x, own_tiles(x)
            x = self.own
        term = jnp.sum(self.centre[r] * x, 0)
        self.live[tap] = term if tap not in self.live else self.live[tap] + term


def blocks_kernel(
    lat, regridded, left, right, above, below, cot, cot_left, cot_right,
    w_embed, kernel1, gain1, point1, kernel2, gain2, point2,
    out, packed,
    x0, cots, d, h1, xhat1, scale1, slope1, dd2, g1, dd1,
    taps1, taps2, flip1, flip2, half1, half2, turned1, turned2,
    u1, dp1, u2, dp2, g0, gk1, gk2, gg1, gg2, swap, lifted,
    *, lat_devices,
):
    halves = (slice(0, 128), slice(128, 256))

    for k in range(25):
        for h in (0, 1):
            one = jnp.broadcast_to(kernel1[k : k + 1, halves[h]].astype(F32), (8, 128))
            two = jnp.broadcast_to(kernel2[k : k + 1, halves[h]].astype(F32), (8, 128))
            taps1[h, k] = one
            flip1[h, 24 - k] = one
            taps2[h, k] = two
            flip2[h, 24 - k] = two
    for point, half, turned in ((point1, half1, turned1), (point2, half2, turned2)):
        value = point[...].astype(F32) * 0.5
        half[...] = value.astype(BF16)
        turned[...] = jnp.transpose(value).astype(BF16)
    zeros = jnp.zeros((8, 128), F32)
    for h in (0, 1):
        for ref in (gg1, gg2):
            ref[h] = zeros
        for ref in (gk1, gk2):
            ref[h] = jnp.zeros((25, 8, 128), F32)
        for ref, size in ((x0, FLAT), (h1, FLAT), (dd2, SLIM), (dd1, SLIM)):
            ref[h, 0:LEAD] = jnp.zeros((LEAD, 128), F32)
            ref[h, size - 16 : size] = jnp.zeros((16, 128), F32)

    weight = w_embed[...]

    def across(a, b):
        return lax.dot_general(a, b, (((0,), (0,)), ((), ())), preferred_element_type=F32)

    def embed(spot, values):
        values = values.astype(BF16).astype(F32)
        for h in (0, 1):
            swap[h, pl.ds(pl.multiple_of(spot, 64), values.shape[0]), :] = values[:, halves[h]]

    def spread(spot, row):
        for k in range(8):
            for h in (0, 1):
                x0[h, pl.ds(pl.multiple_of(at(row + k), 8), PITCH), :] = swap[
                    h, pl.ds(spot + k, PITCH, stride=8), :
                ]

    for i in range(ROWS // 16):
        edge = slice(2 * STRIP * i, 2 * STRIP * (i + 1))
        middle = slice(2 * GROUP * i, 2 * GROUP * (i + 1))
        west = across(left[:, edge], weight)
        east = across(right[:, edge], weight)
        centre = across(regridded[:, middle], weight)
        for k in (0, 1):
            spot = 8 * PITCH * (2 * i + k)
            embed(spot, west[STRIP * k : STRIP * (k + 1)])
            embed(spot + STRIP, centre[GROUP * k : GROUP * (k + 1)])
            embed(spot + STRIP + GROUP, east[STRIP * k : STRIP * (k + 1)])
    for k, given in ((0, above), (1, below)):
        spot = 8 * PITCH * (ROWS // 8 + k)
        embed(spot, across(given[128 : 128 + VARS], weight))
        embed(spot + CHANS, across(given[208 : 208 + VARS, : 8 * PITCH - CHANS], weight))

    def unravel(i, carry):
        spread(8 * PITCH * i, HALO + 8 * i)
        return carry

    lax.fori_loop(0, ROWS // 8, unravel, 0)
    spread(8 * PITCH * (ROWS // 8), 0)
    spread(8 * PITCH * (ROWS // 8 + 1), HALO + ROWS)

    later = lax.broadcasted_iota(jnp.int32, (8, 128), 0) >= 4

    def put(row, value):
        for h in (0, 1):
            cots[h, pl.ds(pl.multiple_of(inner(row), 8), INNER), :] = value[:, halves[h]]

    def fill(pair, carry):
        sides = [cot_left[pair].astype(F32), cot_right[pair].astype(F32)]
        for odd in (0, 1):
            row = 2 * pair + odd
            edges = [s[4 * odd : 4 * odd + 4] for s in sides]
            put(
                row + HALO, jnp.concatenate([edges[0], cot[row].astype(F32), edges[1]], 0)
            )
        return carry

    lax.fori_loop(0, ROWS // 2, fill, 0)
    for k in range(4):
        rows = slice(INNER * k, INNER * (k + 1))
        put(k + 4, above[rows].astype(F32))
        put(k + HALO + ROWS, below[rows].astype(F32))

    def get(ref, start, count):
        return [ref[h, pl.ds(pl.multiple_of(start, 8), count), :] for h in (0, 1)]

    def keep(ref, start, values):
        for h in (0, 1):
            ref[h, pl.ds(pl.multiple_of(start, 8), values[h].shape[0]), :] = values[h]

    def from_wide(ref, row, rows):
        return [
            jnp.concatenate(
                [ref[h, pl.ds(at(row + r) + 4, INNER), :] for r in range(rows)], 0
            )
            for h in (0, 1)
        ]

    def joined(sums):
        return jnp.concatenate(sums, 0).reshape(-1, 128)

    def local_part(x):
        x = x.reshape(-1, 4, 8, 128)
        ends = jnp.where(later, x[:, 0], x[:, 3])
        return jnp.stack([ends, x[:, 1], x[:, 2]], 1).reshape(-1, 128)

    def gains(ref):
        return [ref[:, halves[h]] for h in (0, 1)]

    def normalised(raw):
        mean = jnp.sum(raw[0] * raw[0] + raw[1] * raw[1], -1, keepdims=True) * (1.0 / CHANS)
        scale = lax.rsqrt(mean + 1e-06)
        return scale, [raw[h] * scale for h in (0, 1)]

    def activated(xhat, gain, point):
        u = [xhat[h] * gain[h] for h in (0, 1)]
        p = jnp.dot(
            jnp.concatenate(u, 1).astype(BF16), point[...], preferred_element_type=F32
        )
        p = [p[:, s] for s in halves]
        rise = [jnp.tanh(v) + 1.0 for v in p]
        silu = [p[h] * rise[h] for h in (0, 1)]
        slope = [rise[h] + silu[h] * (2.0 - rise[h]) for h in (0, 1)]
        return u, silu, slope

    def through_norm(grad, slope, xhat, scale, gain, turned):
        dp = [grad[h] * slope[h] for h in (0, 1)]
        du = jnp.dot(
            jnp.concatenate(dp, 1).astype(BF16), turned[...], preferred_element_type=F32
        )
        gained = [du[:, halves[h]] * gain[h] for h in (0, 1)]
        both = [gained[h] * xhat[h] for h in (0, 1)]
        mean = jnp.sum(both[0] + both[1], -1, keepdims=True) * (1.0 / CHANS)
        dd = [
            (scale * (gained[h] - xhat[h] * mean)).astype(BF16).astype(F32) for h in (0, 1)
        ]
        return dp, both, dd

    def gain_sums(store, both):
        for h in (0, 1):
            store[h] += jnp.sum(local_part(both[h]).reshape(-1, 8, 128), 0)

    def pipeline(blocks, first, second):
        first(0)

        def step(i, carry):
            second(i - 1)
            first(i)
            return carry

        lax.fori_loop(1, blocks, step, 0)
        second(blocks - 1)

    size = 4 * PITCH

    def first_conv(i):
        start = at(2) + i * size
        keep(d, start, [joined(conv(x0, h, start, PITCH, 4, PITCH, taps1)) for h in (0, 1)])

    def first_mix(i):
        start = at(2) + i * size
        scale, xhat = normalised(get(d, start, size))
        _, silu, slope = activated(xhat, gains(gain1), half1)
        x = get(x0, start, size)
        keep(h1, start, [(x[h] + silu[h]).astype(BF16).astype(F32) for h in (0, 1)])
        keep(xhat1, start, xhat)
        keep(slope1, start, slope)
        scale1[pl.ds(pl.multiple_of(start, 8), size), :] = jnp.broadcast_to(scale, (size, 128))

    pipeline((TALL - 4) // 4, first_conv, first_mix)

    @pl.when(lat[0] == 0)
    def _():
        for h in (0, 1):
            h1[h, at(2) : at(HALO)] = jnp.zeros((6 * PITCH, 128), F32)

    @pl.when(lat[0] == lat_devices - 1)
    def _():
        for h in (0, 1):
            h1[h, at(HALO + ROWS) : at(HALO + ROWS + 6)] = jnp.zeros((6 * PITCH, 128), F32)

    def second_conv(row):
        keep(
            d,
            inner(row),
            [joined(conv(h1, h, at(row) + 4, PITCH, 4, INNER, taps2)) for h in (0, 1)],
        )

    def second_mix(row, local):
        start = inner(row)
        scale, xhat = normalised(get(d, start, 4 * INNER))
        gain = gains(gain2)
        u, silu, slope = activated(xhat, gain, half2)
        dp, both, dd = through_norm(
            get(cots, start, 4 * INNER), slope, xhat, scale, gain, turned2
        )
        keep(dd2, start, dd)
        if local is not None:
            keep(lifted, LEAD + 4 * INNER * local, silu)
            spot = pl.ds(pl.multiple_of(local * 96, 96), 96)
            u2[spot] = jnp.concatenate([local_part(v) for v in u], 1).astype(BF16)
            dp2[spot] = jnp.concatenate([local_part(v) for v in dp], 1).astype(BF16)
            gain_sums(gg2, both)

    def result(i):
        total = []
        for h in (0, 1):
            rows = []
            for r in range(4):
                place = LEAD + INNER * (4 * i + r) + 4
                base = h1[h, pl.ds(pl.multiple_of(at(HALO + 4 * i + r) + HALO, 8), COLS), :]
                rows.append(base + lifted[h, pl.ds(place, COLS), :])
            total.append(jnp.concatenate(rows, 0))
        out[pl.ds(i * 4, 4)] = jnp.concatenate(total, 1).reshape(4, COLS, CHANS).astype(BF16)

    for row in (4, HALO + ROWS):
        second_conv(row)
    for row in (4, HALO + ROWS):
        second_mix(row, None)
    pipeline(
        ROWS // 4,
        lambda i: second_conv(HALO + 4 * i),
        lambda i: second_mix(HALO + 4 * i, i),
    )

    def third_conv(row, rows, local):
        start = inner(row)
        total = []
        for h in (0, 1):
            visit = None
            if local:
                centre = [
                    own_tiles(h1[h, pl.ds(at(row + r) + 4, INNER), :].reshape(4, 8, 128))
                    for r in range(rows)
                ]
                visit = TapSums(gk2, h, centre)
            sums = joined(conv(dd2, h, start, INNER, rows, INNER, flip2, visit))
            total.append(sums + cots[h, pl.ds(pl.multiple_of(start, 8), rows * INNER), :])
        keep(g1, start, total)

    def third_mix(row, rows, local):
        start = inner(row)
        gain = gains(gain1)
        xhat = from_wide(xhat1, row, rows)
        scale = jnp.concatenate(
            [scale1[pl.ds(at(row + r) + 4, INNER), :] for r in range(rows)], 0
        )
        dp, both, dd = through_norm(
            get(g1, start, rows * INNER), from_wide(slope1, row, rows), xhat, scale, gain, turned1
        )
        keep(dd1, start, dd)
        if local is not None:
            spot = pl.ds(pl.multiple_of(local * 96, 96), 96)
            u = [local_part(xhat[h] * gain[h]) for h in (0, 1)]
            u1[spot] = jnp.concatenate(u, 1).astype(BF16)
            dp1[spot] = jnp.concatenate([local_part(v) for v in dp], 1).astype(BF16)
            gain_sums(gg1, both)
            result(local)

    for row in (6, HALO + ROWS):
        third_conv(row, 2, False)
    for row in (6, HALO + ROWS):
        third_mix(row, 2, None)
    pipeline(
        ROWS // 4,
        lambda i: third_conv(HALO + 4 * i, 4, True),
        lambda i: third_mix(HALO + 4 * i, 4, i),
    )

    @pl.when(lat[0] == 0)
    def _():
        for h in (0, 1):
            dd1[h, inner(6) : inner(HALO)] = jnp.zeros((2 * INNER, 128), F32)

    @pl.when(lat[0] == lat_devices - 1)
    def _():
        for h in (0, 1):
            dd1[h, inner(HALO + ROWS) : inner(HALO + ROWS + 2)] = jnp.zeros(
                (2 * INNER, 128), F32
            )

    def fourth(i, carry):
        row = HALO + 4 * i
        for h in (0, 1):
            centre = [
                x0[h, pl.ds(pl.multiple_of(at(row + r) + HALO, 8), COLS), :].reshape(3, 8, 128)
                for r in range(4)
            ]
            sums = conv(dd1, h, inner(row) + 4, INNER, 4, COLS, flip1, TapSums(gk1, h, centre))
            for r in range(4):
                base = g1[h, pl.ds(inner(row + r) + 4, COLS), :]
                place = GROUP * (i // 2) + 4 * (i % 2) + r
                g0[h, pl.ds(place, COLS, stride=8), :] = sums[r].reshape(COLS, 128) + base
        return carry

    lax.fori_loop(0, ROWS // 4, fourth, 0)

    def pack(place, value):
        rows = value.shape[0]
        value = value.astype(BF16)
        for h in (0, 1):
            packed[place : place + rows // 8, h] = value[:, halves[h]].reshape(rows // 8, 8, 128)

    pack(0, across(u1[...], dp1[...]) * 0.5)
    pack(32, across(u2[...], dp2[...]) * 0.5)
    field = jnp.concatenate([g0[h] for h in (0, 1)], 1).astype(BF16)
    embedded = jnp.dot(regridded[...], field, preferred_element_type=F32)

    def gain_row(ref, gain):
        total = [jnp.sum(ref[h], 0, keepdims=True) for h in (0, 1)]
        return jnp.concatenate(total, 1) / gain[...]

    pack(
        64,
        jnp.concatenate(
            [embedded, gain_row(gg1, gain1), gain_row(gg2, gain2), jnp.zeros((1, CHANS), F32)], 0
        ),
    )
    for place, ref in ((73, gk1), (77, gk2)):
        total = jnp.concatenate([jnp.sum(ref[h], 1) for h in (0, 1)], 1)
        pack(place, jnp.concatenate([total, jnp.zeros((7, CHANS), F32)], 0))
    packed[81:TILES] = jnp.zeros((TILES - 81, 2, 8, 128), BF16)


def blocks(fields, weights, lat_devices):
    wide = pltpu.VMEM((2, FLAT, 128), F32)
    slim = pltpu.VMEM((2, SLIM, 128), F32)
    taps = pltpu.VMEM((2, 25, 8, 128), F32)
    square = pltpu.VMEM((CHANS, CHANS), BF16)
    local = pltpu.VMEM((ROWS * COLS, CHANS), BF16)
    eight = pltpu.VMEM((2, 8, 128), F32)
    lat = jnp.reshape(lax.axis_index("lat"), (1,)).astype(jnp.int32)
    operands = (*fields, *weights)
    vmem = pl.BlockSpec(memory_space=pltpu.VMEM)
    return pl.pallas_call(
        functools.partial(blocks_kernel, lat_devices=lat_devices),
        in_specs=[pl.BlockSpec(memory_space=pltpu.SMEM)] + [vmem] * len(operands),
        out_specs=[vmem, vmem],
        out_shape=[
            jax.ShapeDtypeStruct((ROWS, COLS, CHANS), BF16),
            jax.ShapeDtypeStruct((TILES, 2, 8, 128), BF16),
        ],
        scratch_shapes=[wide, slim, wide, wide, wide, pltpu.VMEM((FLAT, 128), F32), wide]
        + [slim] * 3
        + [taps] * 4
        + [square] * 4
        + [local] * 4
        + [pltpu.VMEM((2, ROWS * COLS, 128), F32)]
        + [taps] * 2
        + [eight] * 2
        + [pltpu.VMEM((2, PITCH * TALL, 128), F32)]
        + [pltpu.VMEM((2, LEAD + INNER * ROWS + 16, 128), F32)],
        compiler_params=pltpu.CompilerParams(vmem_limit_bytes=60 * 1024 * 1024),
        name="both_blocks",
    )(lat, *operands)


def unpack_kernel(packed, embed, kernel1, kernel2, point1, point2, gain1, gain2, *, factor):
    for h in (0, 1):
        lanes = slice(128 * h, 128 * h + 128)
        point1[:, lanes] = packed[0:32, h].astype(F32).reshape(CHANS, 128) * factor
        point2[:, lanes] = packed[32:64, h].astype(F32).reshape(CHANS, 128) * factor
        mixed = packed[64:73, h].astype(F32).reshape(72, 128) * factor
        embed[:, lanes] = mixed[:VARS]
        gain1[:, lanes] = mixed[VARS : VARS + 1]
        gain2[:, lanes] = mixed[VARS + 1 : VARS + 2]
        kernel1[:, lanes] = (packed[73:77, h].astype(F32).reshape(32, 128) * factor)[:25]
        kernel2[:, lanes] = (packed[77:81, h].astype(F32).reshape(32, 128) * factor)[:25]


def summed(packed, factor):
    devices = lax.axis_size(AXES)
    parts = lax.all_to_all(packed, AXES, 0, 0, tiled=True)
    mine = jnp.sum(parts.reshape(devices, -1, 2, 8, 128).astype(F32), 0).astype(BF16)
    total = lax.all_to_all(jnp.tile(mine, (devices, 1, 1, 1)), AXES, 0, 0, tiled=True)
    shapes = [(VARS, CHANS), (25, CHANS), (25, CHANS), (CHANS, CHANS), (CHANS, CHANS)]
    results = pl.pallas_call(
        functools.partial(unpack_kernel, factor=factor),
        out_shape=[jax.ShapeDtypeStruct(s, F32) for s in shapes + [(1, CHANS)] * 2],
        name="unpack",
    )(total)
    return (*results[:5], results[5].reshape(CHANS), results[6].reshape(CHANS))


def shifted(before, after, axis, wrap):
    devices = lax.axis_size(axis)
    up = [(i, (i + 1) % devices) for i in range(devices if wrap else devices - 1)]
    down = [(j, i) for i, j in up]
    return lax.ppermute(after, axis, up), lax.ppermute(before, axis, down)


def whole_step(points, row_len, w_embed, kernel1, gain1, point1, kernel2, gain2, point2, cotangent):
    lon_total = COLS * lax.axis_size("lon")
    rows_total = ROWS * lax.axis_size("lat")
    values, west, east = regrid(jnp.swapaxes(points, 0, 1), row_len, lon_total)
    left, right = shifted(west, east, "lon", True)
    cot_left, cot_right = shifted(
        cotangent[:, :4].reshape(ROWS // 2, 8, CHANS),
        cotangent[:, COLS - 4 :].reshape(ROWS // 2, 8, CHANS),
        "lon",
        True,
    )
    before, after = bands(values, left, right, cotangent, cot_left, cot_right)
    above, below = shifted(before, after, "lat", False)
    fields = (values, left, right, above, below, cotangent, cot_left, cot_right)
    weights = (
        w_embed, kernel1, gain1.reshape(1, CHANS), point1,
        kernel2, gain2.reshape(1, CHANS), point2,
    )
    out, packed = blocks(fields, weights, lax.axis_size("lat"))
    return (out, *summed(packed, float(rows_total * lon_total) ** (-0.5)))


def solution(mesh):
    in_specs = (
        P("lat", None, "lon"),
        P("lat"),
        P(),
        P(),
        P(),
        P(),
        P(),
        P(),
        P(),
        P("lat", "lon", None),
    )
    out_specs = (P("lat", "lon", None), P(), P(), P(), P(), P(), P(), P())
    return jax.shard_map(
        whole_step, mesh=mesh, in_specs=in_specs, out_specs=out_specs, check_vma=False
    )
```

```python
import functools

import jax
import jax.numpy as jnp
from jax import lax
from jax.experimental import pallas as pl
from jax.experimental.pallas import tpu as pltpu
from jax.sharding import PartitionSpec as P

F32 = jnp.float32
BF16 = jnp.bfloat16
ROWS = 64
COLS = 24
HALO = 8
PITCH = COLS + 2 * HALO
TALL = ROWS + 2 * HALO
INNER = COLS + 8
LEAD = 16
FLAT = LEAD + PITCH * TALL + 16
SLIM = LEAD + INNER * TALL + 16
CHANS = 256
VARS = 69
TILES = 128
AXES = ("lon", "lat")


GROUP = 8 * COLS
STRIP = 8 * HALO


def regrid_kernel(row_len, sector, points, *refs, lon_total, skipped):
    values, west, east = refs[-3:]
    first = (sector[0] * COLS).astype(F32)
    whole = lon_total // 4
    lane = lax.broadcasted_iota(jnp.int32, (8, GROUP), 1)
    row = lane % 8
    cell = first + (lane // 8).astype(F32)
    own = lax.broadcasted_iota(jnp.int32, (8, GROUP), 0) == row
    own = jnp.where(own, 1.0 / whole, 0.0)
    every8 = lax.broadcasted_iota(jnp.int32, (VARS, 8 * VARS), 1) // 8
    fold = jnp.where(every8 == lax.broadcasted_iota(jnp.int32, every8.shape, 0), 1.0, 0.0)
    fold = fold.astype(BF16)
    mark = lax.broadcasted_iota(jnp.int32, (points.shape[3], GROUP), 0).astype(F32)
    found = []
    for k in range(points.shape[1]):
        group = (pl.program_id(0) + skipped) * points.shape[1] + k
        count = jnp.zeros((8, GROUP), F32)
        for q in range(8):
            count = jnp.where(row == q, row_len[8 * group + q].astype(F32), count)
        product = cell * count
        lower = jnp.floor((product + 2.0) * (1.0 / lon_total))
        start = jnp.floor((first * count + 2.0) * (1.0 / lon_total))
        share = (product - lower * lon_total) * 0.25
        away = mark - (lower - start)[:1]
        mix = jnp.where(
            away == 0.0, whole - share[:1], jnp.where(away == 1.0, share[:1], 0.0)
        )
        rows = points[:, k].reshape(VARS * 8, points.shape[3])
        every = jnp.dot(rows, mix.astype(BF16), preferred_element_type=F32)
        kept = (every.reshape(VARS, 8, GROUP) * own[None]).reshape(VARS * 8, GROUP)
        found.append(jnp.dot(fold, kept.astype(BF16), preferred_element_type=F32))
    values[...] = jnp.concatenate(found, 1).astype(BF16)
    west[...] = jnp.concatenate([f[:, :STRIP] for f in found], 1).astype(BF16)
    east[...] = jnp.concatenate([f[:, GROUP - STRIP :] for f in found], 1).astype(BF16)


def regrid(points, row_len, lon_total, part, earlier):
    nvars, nrows, slots = points.shape
    groups = 2
    steps = nrows // (16 * groups)
    skipped = steps * part
    strips = jax.ShapeDtypeStruct((nvars, nrows * HALO), BF16)
    full = jax.ShapeDtypeStruct((nvars, nrows * COLS), BF16)
    return pl.pallas_call(
        functools.partial(regrid_kernel, lon_total=lon_total, skipped=skipped),
        grid_spec=pltpu.PrefetchScalarGridSpec(
            num_scalar_prefetch=2,
            grid=(steps,),
            in_specs=[
                pl.BlockSpec((nvars, groups, 8, slots), lambda i, *_: (0, i + skipped, 0, 0))
            ]
            + [pl.BlockSpec(memory_space=pl.ANY)] * len(earlier),
            out_specs=[
                pl.BlockSpec((nvars, groups * GROUP), lambda i, *_: (0, i + skipped)),
                pl.BlockSpec((nvars, groups * STRIP), lambda i, *_: (0, i + skipped)),
                pl.BlockSpec((nvars, groups * STRIP), lambda i, *_: (0, i + skipped)),
            ],
        ),
        out_shape=[full, strips, strips],
        input_output_aliases={3 + i: i for i in range(len(earlier))},
        name="regrid",
    )(
        row_len,
        jnp.reshape(lax.axis_index("lon"), (1,)).astype(jnp.int32),
        points.reshape(nvars, nrows // 8, 8, slots),
        *earlier,
    )


def at(row):
    return LEAD + PITCH * row


def inner(row):
    return LEAD + INNER * row


def conv(source, half, start, pitch, rows, cols, taps, visit=None):
    sums = [None] * rows
    for e in range(5):
        weights = [taps[half, 5 * a + e] for a in range(5)]
        for i in range(rows + 4):
            x = source[half, pl.ds(start + pitch * (i - 2) + e - 2, cols), :]
            x = x.reshape(cols // 8, 8, 128)
            for a in range(5):
                r = i - a
                if 0 <= r < rows:
                    term = x * weights[a]
                    sums[r] = term if sums[r] is None else sums[r] + term
                    if visit is not None:
                        visit(a, e, r, x)
        if visit is not None:
            visit(None, e, None, None)
    return sums


def own_tiles(x):
    later = lax.broadcasted_iota(jnp.int32, (8, 128), 0) >= 4
    return jnp.stack([jnp.where(later, x[0], x[3]), x[1], x[2]])


class TapSums:
    def __init__(self, store, half, centre):
        self.store, self.half, self.centre, self.live = store, half, centre, {}
        self.seen = self.own = None

    def __call__(self, a, e, r, x):
        if a is None:
            for tap, value in self.live.items():
                self.store[self.half, tap] += value
            self.live = {}
            return
        tap = 24 - (5 * a + e)
        if x.shape[0] == 4:
            if self.seen is not x:
                self.seen, self.own = x, own_tiles(x)
            x = self.own
        term = jnp.sum(self.centre[r] * x, 0)
        self.live[tap] = term if tap not in self.live else self.live[tap] + term


def blocks_kernel(
    lat, regridded, left, right, above, below, cot, cot_left, cot_right,
    w_embed, kernel1, gain1, point1, kernel2, gain2, point2,
    out, packed,
    x0, cots, d, h1, xhat1, scale1, slope1, dd2, g1, dd1,
    taps1, taps2, flip1, flip2, half1, half2, turned1, turned2,
    u1, dp1, u2, dp2, g0, gk1, gk2, gg1, gg2, swap, lifted,
    *, lat_devices,
):
    halves = (slice(0, 128), slice(128, 256))

    for k in range(25):
        for h in (0, 1):
            one = jnp.broadcast_to(kernel1[k : k + 1, halves[h]].astype(F32), (8, 128))
            two = jnp.broadcast_to(kernel2[k : k + 1, halves[h]].astype(F32), (8, 128))
            taps1[h, k] = one
            flip1[h, 24 - k] = one
            taps2[h, k] = two
            flip2[h, 24 - k] = two
    for point, half, turned in ((point1, half1, turned1), (point2, half2, turned2)):
        value = point[...].astype(F32) * 0.5
        half[...] = value.astype(BF16)
        turned[...] = jnp.transpose(value).astype(BF16)
    zeros = jnp.zeros((8, 128), F32)
    for h in (0, 1):
        for ref in (gg1, gg2):
            ref[h] = zeros
        for ref in (gk1, gk2):
            ref[h] = jnp.zeros((25, 8, 128), F32)
        for ref, size in ((x0, FLAT), (h1, FLAT), (dd2, SLIM), (dd1, SLIM)):
            ref[h, 0:LEAD] = jnp.zeros((LEAD, 128), F32)
            ref[h, size - 16 : size] = jnp.zeros((16, 128), F32)

    weight = w_embed[...]

    def across(a, b):
        return lax.dot_general(a, b, (((0,), (0,)), ((), ())), preferred_element_type=F32)

    def embed(spot, values):
        values = values.astype(BF16).astype(F32)
        for h in (0, 1):
            swap[h, pl.ds(pl.multiple_of(spot, 64), values.shape[0]), :] = values[:, halves[h]]

    def spread(spot, row):
        for k in range(8):
            for h in (0, 1):
                x0[h, pl.ds(pl.multiple_of(at(row + k), 8), PITCH), :] = swap[
                    h, pl.ds(spot + k, PITCH, stride=8), :
                ]

    for i in range(ROWS // 16):
        edge = slice(2 * STRIP * i, 2 * STRIP * (i + 1))
        middle = slice(2 * GROUP * i, 2 * GROUP * (i + 1))
        west = across(left[:, edge], weight)
        east = across(right[:, edge], weight)
        centre = across(regridded[:, middle], weight)
        for k in (0, 1):
            spot = 8 * PITCH * (2 * i + k)
            embed(spot, west[STRIP * k : STRIP * (k + 1)])
            embed(spot + STRIP, centre[GROUP * k : GROUP * (k + 1)])
            embed(spot + STRIP + GROUP, east[STRIP * k : STRIP * (k + 1)])
    for k, given in ((0, above), (1, below)):
        spot = 8 * PITCH * (ROWS // 8 + k)
        embed(spot, across(given[128 : 128 + VARS], weight))
        embed(spot + CHANS, across(given[208 : 208 + VARS, : 8 * PITCH - CHANS], weight))

    def unravel(i, carry):
        spread(8 * PITCH * i, HALO + 8 * i)
        return carry

    lax.fori_loop(0, ROWS // 8, unravel, 0)
    spread(8 * PITCH * (ROWS // 8), 0)
    spread(8 * PITCH * (ROWS // 8 + 1), HALO + ROWS)

    later = lax.broadcasted_iota(jnp.int32, (8, 128), 0) >= 4

    def put(row, value):
        for h in (0, 1):
            cots[h, pl.ds(pl.multiple_of(inner(row), 8), INNER), :] = value[:, halves[h]]

    def fill(pair, carry):
        sides = [cot_left[pair].astype(F32), cot_right[pair].astype(F32)]
        for odd in (0, 1):
            row = 2 * pair + odd
            edges = [s[4 * odd : 4 * odd + 4] for s in sides]
            put(
                row + HALO, jnp.concatenate([edges[0], cot[row].astype(F32), edges[1]], 0)
            )
        return carry

    lax.fori_loop(0, ROWS // 2, fill, 0)
    for k in range(4):
        rows = slice(INNER * k, INNER * (k + 1))
        put(k + 4, above[rows].astype(F32))
        put(k + HALO + ROWS, below[rows].astype(F32))

    def get(ref, start, count):
        return [ref[h, pl.ds(pl.multiple_of(start, 8), count), :] for h in (0, 1)]

    def keep(ref, start, values):
        for h in (0, 1):
            ref[h, pl.ds(pl.multiple_of(start, 8), values[h].shape[0]), :] = values[h]

    def from_wide(ref, row, rows):
        return [
            jnp.concatenate(
                [ref[h, pl.ds(at(row + r) + 4, INNER), :] for r in range(rows)], 0
            )
            for h in (0, 1)
        ]

    def joined(sums):
        return jnp.concatenate(sums, 0).reshape(-1, 128)

    def local_part(x):
        x = x.reshape(-1, 4, 8, 128)
        ends = jnp.where(later, x[:, 0], x[:, 3])
        return jnp.stack([ends, x[:, 1], x[:, 2]], 1).reshape(-1, 128)

    def gains(ref):
        return [ref[:, halves[h]] for h in (0, 1)]

    def normalised(raw):
        mean = jnp.sum(raw[0] * raw[0] + raw[1] * raw[1], -1, keepdims=True) * (1.0 / CHANS)
        scale = lax.rsqrt(mean + 1e-06)
        return scale, [raw[h] * scale for h in (0, 1)]

    def activated(xhat, gain, point):
        u = [xhat[h] * gain[h] for h in (0, 1)]
        p = jnp.dot(
            jnp.concatenate(u, 1).astype(BF16), point[...], preferred_element_type=F32
        )
        p = [p[:, s] for s in halves]
        rise = [jnp.tanh(v) + 1.0 for v in p]
        silu = [p[h] * rise[h] for h in (0, 1)]
        slope = [rise[h] + silu[h] * (2.0 - rise[h]) for h in (0, 1)]
        return u, silu, slope

    def through_norm(grad, slope, xhat, scale, gain, turned):
        dp = [grad[h] * slope[h] for h in (0, 1)]
        du = jnp.dot(
            jnp.concatenate(dp, 1).astype(BF16), turned[...], preferred_element_type=F32
        )
        gained = [du[:, halves[h]] * gain[h] for h in (0, 1)]
        both = [gained[h] * xhat[h] for h in (0, 1)]
        mean = jnp.sum(both[0] + both[1], -1, keepdims=True) * (1.0 / CHANS)
        dd = [
            (scale * (gained[h] - xhat[h] * mean)).astype(BF16).astype(F32) for h in (0, 1)
        ]
        return dp, both, dd

    def gain_sums(store, both):
        for h in (0, 1):
            store[h] += jnp.sum(local_part(both[h]).reshape(-1, 8, 128), 0)

    def pipeline(blocks, first, second):
        first(0)

        def step(i, carry):
            second(i - 1)
            first(i)
            return carry

        lax.fori_loop(1, blocks, step, 0)
        second(blocks - 1)

    size = 4 * PITCH

    def first_conv(i):
        start = at(2) + i * size
        keep(d, start, [joined(conv(x0, h, start, PITCH, 4, PITCH, taps1)) for h in (0, 1)])

    def first_mix(i):
        start = at(2) + i * size
        scale, xhat = normalised(get(d, start, size))
        _, silu, slope = activated(xhat, gains(gain1), half1)
        x = get(x0, start, size)
        keep(h1, start, [(x[h] + silu[h]).astype(BF16).astype(F32) for h in (0, 1)])
        keep(xhat1, start, xhat)
        keep(slope1, start, slope)
        scale1[pl.ds(pl.multiple_of(start, 8), size), :] = jnp.broadcast_to(scale, (size, 128))

    pipeline((TALL - 4) // 4, first_conv, first_mix)

    @pl.when(lat[0] == 0)
    def _():
        for h in (0, 1):
            h1[h, at(2) : at(HALO)] = jnp.zeros((6 * PITCH, 128), F32)

    @pl.when(lat[0] == lat_devices - 1)
    def _():
        for h in (0, 1):
            h1[h, at(HALO + ROWS) : at(HALO + ROWS + 6)] = jnp.zeros((6 * PITCH, 128), F32)

    def second_conv(row):
        keep(
            d,
            inner(row),
            [joined(conv(h1, h, at(row) + 4, PITCH, 4, INNER, taps2)) for h in (0, 1)],
        )

    def second_mix(row, local):
        start = inner(row)
        scale, xhat = normalised(get(d, start, 4 * INNER))
        gain = gains(gain2)
        u, silu, slope = activated(xhat, gain, half2)
        dp, both, dd = through_norm(
            get(cots, start, 4 * INNER), slope, xhat, scale, gain, turned2
        )
        keep(dd2, start, dd)
        if local is not None:
            keep(lifted, LEAD + 4 * INNER * local, silu)
            spot = pl.ds(pl.multiple_of(local * 96, 96), 96)
            u2[spot] = jnp.concatenate([local_part(v) for v in u], 1).astype(BF16)
            dp2[spot] = jnp.concatenate([local_part(v) for v in dp], 1).astype(BF16)
            gain_sums(gg2, both)

    def result(i):
        total = []
        for h in (0, 1):
            rows = []
            for r in range(4):
                place = LEAD + INNER * (4 * i + r) + 4
                base = h1[h, pl.ds(pl.multiple_of(at(HALO + 4 * i + r) + HALO, 8), COLS), :]
                rows.append(base + lifted[h, pl.ds(place, COLS), :])
            total.append(jnp.concatenate(rows, 0))
        out[pl.ds(i * 4, 4)] = jnp.concatenate(total, 1).reshape(4, COLS, CHANS).astype(BF16)

    for row in (4, HALO + ROWS):
        second_conv(row)
    for row in (4, HALO + ROWS):
        second_mix(row, None)
    pipeline(
        ROWS // 4,
        lambda i: second_conv(HALO + 4 * i),
        lambda i: second_mix(HALO + 4 * i, i),
    )

    def third_conv(row, rows, local):
        start = inner(row)
        total = []
        for h in (0, 1):
            visit = None
            if local:
                centre = [
                    own_tiles(h1[h, pl.ds(at(row + r) + 4, INNER), :].reshape(4, 8, 128))
                    for r in range(rows)
                ]
                visit = TapSums(gk2, h, centre)
            sums = joined(conv(dd2, h, start, INNER, rows, INNER, flip2, visit))
            total.append(sums + cots[h, pl.ds(pl.multiple_of(start, 8), rows * INNER), :])
        keep(g1, start, total)

    def third_mix(row, rows, local):
        start = inner(row)
        gain = gains(gain1)
        xhat = from_wide(xhat1, row, rows)
        scale = jnp.concatenate(
            [scale1[pl.ds(at(row + r) + 4, INNER), :] for r in range(rows)], 0
        )
        dp, both, dd = through_norm(
            get(g1, start, rows * INNER), from_wide(slope1, row, rows), xhat, scale, gain, turned1
        )
        keep(dd1, start, dd)
        if local is not None:
            spot = pl.ds(pl.multiple_of(local * 96, 96), 96)
            u = [local_part(xhat[h] * gain[h]) for h in (0, 1)]
            u1[spot] = jnp.concatenate(u, 1).astype(BF16)
            dp1[spot] = jnp.concatenate([local_part(v) for v in dp], 1).astype(BF16)
            gain_sums(gg1, both)
            result(local)

    for row in (6, HALO + ROWS):
        third_conv(row, 2, False)
    for row in (6, HALO + ROWS):
        third_mix(row, 2, None)
    pipeline(
        ROWS // 4,
        lambda i: third_conv(HALO + 4 * i, 4, True),
        lambda i: third_mix(HALO + 4 * i, 4, i),
    )

    @pl.when(lat[0] == 0)
    def _():
        for h in (0, 1):
            dd1[h, inner(6) : inner(HALO)] = jnp.zeros((2 * INNER, 128), F32)

    @pl.when(lat[0] == lat_devices - 1)
    def _():
        for h in (0, 1):
            dd1[h, inner(HALO + ROWS) : inner(HALO + ROWS + 2)] = jnp.zeros(
                (2 * INNER, 128), F32
            )

    def fourth(i, carry):
        row = HALO + 4 * i
        for h in (0, 1):
            centre = [
                x0[h, pl.ds(pl.multiple_of(at(row + r) + HALO, 8), COLS), :].reshape(3, 8, 128)
                for r in range(4)
            ]
            sums = conv(dd1, h, inner(row) + 4, INNER, 4, COLS, flip1, TapSums(gk1, h, centre))
            for r in range(4):
                base = g1[h, pl.ds(inner(row + r) + 4, COLS), :]
                place = GROUP * (i // 2) + 4 * (i % 2) + r
                g0[h, pl.ds(place, COLS, stride=8), :] = sums[r].reshape(COLS, 128) + base
        return carry

    lax.fori_loop(0, ROWS // 4, fourth, 0)

    def pack(place, value):
        rows = value.shape[0]
        value = value.astype(BF16)
        for h in (0, 1):
            packed[place : place + rows // 8, h] = value[:, halves[h]].reshape(rows // 8, 8, 128)

    pack(0, across(u1[...], dp1[...]) * 0.5)
    pack(32, across(u2[...], dp2[...]) * 0.5)
    field = jnp.concatenate([g0[h] for h in (0, 1)], 1).astype(BF16)
    embedded = jnp.dot(regridded[...], field, preferred_element_type=F32)

    def gain_row(ref, gain):
        total = [jnp.sum(ref[h], 0, keepdims=True) for h in (0, 1)]
        return jnp.concatenate(total, 1) / gain[...]

    pack(
        64,
        jnp.concatenate(
            [embedded, gain_row(gg1, gain1), gain_row(gg2, gain2), jnp.zeros((1, CHANS), F32)], 0
        ),
    )
    for place, ref in ((73, gk1), (77, gk2)):
        total = jnp.concatenate([jnp.sum(ref[h], 1) for h in (0, 1)], 1)
        pack(place, jnp.concatenate([total, jnp.zeros((7, CHANS), F32)], 0))
    packed[81:TILES] = jnp.zeros((TILES - 81, 2, 8, 128), BF16)


def blocks(fields, weights, lat_devices):
    wide = pltpu.VMEM((2, FLAT, 128), F32)
    slim = pltpu.VMEM((2, SLIM, 128), F32)
    taps = pltpu.VMEM((2, 25, 8, 128), F32)
    square = pltpu.VMEM((CHANS, CHANS), BF16)
    local = pltpu.VMEM((ROWS * COLS, CHANS), BF16)
    eight = pltpu.VMEM((2, 8, 128), F32)
    lat = jnp.reshape(lax.axis_index("lat"), (1,)).astype(jnp.int32)
    operands = (*fields, *weights)
    vmem = pl.BlockSpec(memory_space=pltpu.VMEM)
    return pl.pallas_call(
        functools.partial(blocks_kernel, lat_devices=lat_devices),
        in_specs=[pl.BlockSpec(memory_space=pltpu.SMEM)] + [vmem] * len(operands),
        out_specs=[vmem, vmem],
        out_shape=[
            jax.ShapeDtypeStruct((ROWS, COLS, CHANS), BF16),
            jax.ShapeDtypeStruct((TILES, 2, 8, 128), BF16),
        ],
        scratch_shapes=[wide, slim, wide, wide, wide, pltpu.VMEM((FLAT, 128), F32), wide]
        + [slim] * 3
        + [taps] * 4
        + [square] * 4
        + [local] * 4
        + [pltpu.VMEM((2, ROWS * COLS, 128), F32)]
        + [taps] * 2
        + [eight] * 2
        + [pltpu.VMEM((2, PITCH * TALL, 128), F32)]
        + [pltpu.VMEM((2, LEAD + INNER * ROWS + 16, 128), F32)],
        compiler_params=pltpu.CompilerParams(vmem_limit_bytes=60 * 1024 * 1024),
        name="both_blocks",
    )(lat, *operands)


def unpack_kernel(packed, embed, kernel1, kernel2, point1, point2, gain1, gain2, *, factor):
    for h in (0, 1):
        lanes = slice(128 * h, 128 * h + 128)
        point1[:, lanes] = packed[0:32, h].astype(F32).reshape(CHANS, 128) * factor
        point2[:, lanes] = packed[32:64, h].astype(F32).reshape(CHANS, 128) * factor
        mixed = packed[64:73, h].astype(F32).reshape(72, 128) * factor
        embed[:, lanes] = mixed[:VARS]
        gain1[:, lanes] = mixed[VARS : VARS + 1]
        gain2[:, lanes] = mixed[VARS + 1 : VARS + 2]
        kernel1[:, lanes] = (packed[73:77, h].astype(F32).reshape(32, 128) * factor)[:25]
        kernel2[:, lanes] = (packed[77:81, h].astype(F32).reshape(32, 128) * factor)[:25]


def summed(packed, factor):
    devices = lax.axis_size(AXES)
    parts = lax.all_to_all(packed, AXES, 0, 0, tiled=True)
    mine = jnp.sum(parts.reshape(devices, -1, 2, 8, 128).astype(F32), 0).astype(BF16)
    total = lax.all_to_all(jnp.tile(mine, (devices, 1, 1, 1)), AXES, 0, 0, tiled=True)
    shapes = [(VARS, CHANS), (25, CHANS), (25, CHANS), (CHANS, CHANS), (CHANS, CHANS)]
    results = pl.pallas_call(
        functools.partial(unpack_kernel, factor=factor),
        out_shape=[jax.ShapeDtypeStruct(s, F32) for s in shapes + [(1, CHANS)] * 2],
        name="unpack",
    )(total)
    return (*results[:5], results[5].reshape(CHANS), results[6].reshape(CHANS))


def shifted(before, after, axis, wrap):
    devices = lax.axis_size(axis)
    up = [(i, (i + 1) % devices) for i in range(devices if wrap else devices - 1)]
    down = [(j, i) for i, j in up]
    return lax.ppermute(after, axis, up), lax.ppermute(before, axis, down)


def whole_step(points, row_len, w_embed, kernel1, gain1, point1, kernel2, gain2, point2, cotangent):
    lon_total = COLS * lax.axis_size("lon")
    rows_total = ROWS * lax.axis_size("lat")
    devices = lax.axis_size("lon")
    up = [(i, (i + 1) % devices) for i in range(devices)]
    columns = [
        x.reshape(ROWS // 2, 8, CHANS) for x in (cotangent[:, COLS - 4 :], cotangent[:, :4])
    ]
    swapped = jnp.swapaxes(points, 0, 1)
    cot_left = lax.ppermute(columns[0], "lon", up)
    early = regrid(swapped, row_len, lon_total, 0, ())
    cot_right = lax.ppermute(columns[1], "lon", [(j, i) for i, j in up])
    values, west, east = regrid(swapped, row_len, lon_total, 1, early)
    left, right = shifted(west, east, "lon", True)

    def band(rows, pairs, lanes, edge):
        sides = [c[pairs].reshape(4, 4, CHANS) for c in (cot_left, cot_right)]
        given = jnp.concatenate([sides[0], cotangent[rows], sides[1]], 1).reshape(-1, CHANS)
        field = jnp.concatenate([left[:, edge], values[:, lanes], right[:, edge]], 1)
        pieces = [field[:, :CHANS], field[:, CHANS:]]
        pieces = [
            jnp.pad(x, ((0, 80 - VARS), (0, CHANS - x.shape[1]))) for x in pieces
        ]
        return jnp.concatenate([given, *pieces], 0)

    above, below = shifted(
        band(slice(0, 4), slice(0, 2), slice(0, GROUP), slice(0, STRIP)),
        band(
            slice(ROWS - 4, ROWS),
            slice(ROWS // 2 - 2, ROWS // 2),
            slice(GROUP * (ROWS // 8 - 1), GROUP * (ROWS // 8)),
            slice(STRIP * (ROWS // 8 - 1), STRIP * (ROWS // 8)),
        ),
        "lat",
        False,
    )
    fields = (values, left, right, above, below, cotangent, cot_left, cot_right)
    weights = (
        w_embed, kernel1, gain1.reshape(1, CHANS), point1,
        kernel2, gain2.reshape(1, CHANS), point2,
    )
    out, packed = blocks(fields, weights, lax.axis_size("lat"))
    return (out, *summed(packed, float(rows_total * lon_total) ** (-0.5)))


def solution(mesh):
    in_specs = (
        P("lat", None, "lon"),
        P("lat"),
        P(),
        P(),
        P(),
        P(),
        P(),
        P(),
        P(),
        P("lat", "lon", None),
    )
    out_specs = (P("lat", "lon", None), P(), P(), P(), P(), P(), P(), P())
    return jax.shard_map(
        whole_step, mesh=mesh, in_specs=in_specs, out_specs=out_specs, check_vma=False
    )
```

```python
import functools

import jax
import jax.numpy as jnp
from jax import lax
from jax.experimental import pallas as pl
from jax.experimental.pallas import tpu as pltpu
from jax.sharding import PartitionSpec as P

F32 = jnp.float32
BF16 = jnp.bfloat16
ROWS = 64
COLS = 24
HALO = 8
PITCH = COLS + 2 * HALO
TALL = ROWS + 2 * HALO
INNER = COLS + 8
LEAD = 16
FLAT = LEAD + PITCH * TALL + 16
SLIM = LEAD + INNER * TALL + 16
CHANS = 256
VARS = 69
TILES = 128
AXES = ("lon", "lat")


GROUP = 8 * COLS
STRIP = 8 * HALO


def regrid_kernel(
    row_len, sector, points, high, low, west, east, held, arrived, *, lon_total
):
    batch = held.shape[2]
    copies = [
        pltpu.make_async_copy(
            points.at[:, batch * i : batch * (i + 1)], held.at[i], arrived.at[i]
        )
        for i in range(held.shape[0])
    ]
    for copy in copies:
        copy.start()
    slots = points.shape[3]
    first = (sector[0] * COLS).astype(F32)
    whole = lon_total // 4
    lane = lax.broadcasted_iota(jnp.int32, (8, GROUP), 1)
    row = lane % 8
    cell = first + (lane // 8).astype(F32)
    own = lax.broadcasted_iota(jnp.int32, (8, GROUP), 0) == row
    mark = lax.broadcasted_iota(jnp.int32, (slots, GROUP), 0).astype(F32)
    for i, copy in enumerate(copies):
        found = []
        copy.wait()
        for k in range(batch):
            count = jnp.zeros((8, GROUP), F32)
            for q in range(8):
                length = row_len[8 * (batch * i + k) + q]
                count = jnp.where(row == q, length.astype(F32), count)
            product = cell * count
            lower = jnp.floor((product + 2.0) * (1.0 / lon_total))
            start = jnp.floor((first * count + 2.0) * (1.0 / lon_total))
            share = (product - lower * lon_total) * 0.25
            away = mark - (lower - start)[:1]
            mix = jnp.where(
                away == 0.0, whole - share[:1], jnp.where(away == 1.0, share[:1], 0.0)
            )
            rows = held[i, :, k].reshape(VARS * 8, slots)
            every = jnp.dot(rows, mix.astype(BF16), preferred_element_type=F32)
            kept = jnp.where(own[None], every.reshape(VARS, 8, GROUP), 0.0)
            found.append(jnp.sum(kept, 1) * (1.0 / whole))
        lanes = slice(batch * GROUP * i, batch * GROUP * (i + 1))
        edge = slice(batch * STRIP * i, batch * STRIP * (i + 1))
        values = jnp.concatenate(found, 1)
        rounded = values.astype(BF16)
        high[:, lanes] = rounded
        low[:, lanes] = (values - rounded.astype(F32)).astype(BF16)
        west[:, edge] = jnp.concatenate([f[:, :STRIP] for f in found], 1).astype(BF16)
        east[:, edge] = jnp.concatenate([f[:, GROUP - STRIP :] for f in found], 1).astype(BF16)


def regrid(points, row_len, lon_total):
    nvars, nrows, slots = points.shape
    batches = 4
    strips = jax.ShapeDtypeStruct((nvars, nrows * HALO), BF16)
    full = jax.ShapeDtypeStruct((nvars, nrows * COLS), BF16)
    smem = pl.BlockSpec(memory_space=pltpu.SMEM)
    vmem = pl.BlockSpec(memory_space=pltpu.VMEM)
    return pl.pallas_call(
        functools.partial(regrid_kernel, lon_total=lon_total),
        in_specs=[smem, smem, pl.BlockSpec(memory_space=pl.ANY)],
        out_specs=[vmem] * 4,
        out_shape=[full, full, strips, strips],
        scratch_shapes=[
            pltpu.VMEM((batches, nvars, nrows // (8 * batches), 8, slots), BF16),
            pltpu.SemaphoreType.DMA((batches,)),
        ],
        name="regrid",
    )(
        row_len,
        jnp.reshape(lax.axis_index("lon"), (1,)).astype(jnp.int32),
        points.reshape(nvars, nrows // 8, 8, slots),
    )


def at(row):
    return LEAD + PITCH * row


def inner(row):
    return LEAD + INNER * row


def conv(source, half, start, pitch, rows, cols, taps, visit=None):
    sums = [None] * rows
    for e in range(5):
        weights = [taps[half, 5 * a + e] for a in range(5)]
        for i in range(rows + 4):
            x = source[half, pl.ds(start + pitch * (i - 2) + e - 2, cols), :]
            x = x.reshape(cols // 8, 8, 128)
            for a in range(5):
                r = i - a
                if 0 <= r < rows:
                    term = x * weights[a]
                    sums[r] = term if sums[r] is None else sums[r] + term
                    if visit is not None:
                        visit(a, e, r, x)
        if visit is not None:
            visit(None, e, None, None)
    return sums


def own_tiles(x):
    later = lax.broadcasted_iota(jnp.int32, (8, 128), 0) >= 4
    return jnp.stack([jnp.where(later, x[0], x[3]), x[1], x[2]])


class TapSums:
    def __init__(self, store, half, centre):
        self.store, self.half, self.centre, self.live = store, half, centre, {}
        self.seen = self.own = None

    def __call__(self, a, e, r, x):
        if a is None:
            for tap, value in self.live.items():
                self.store[self.half, tap] += value
            self.live = {}
            return
        tap = 24 - (5 * a + e)
        if x.shape[0] == 4:
            if self.seen is not x:
                self.seen, self.own = x, own_tiles(x)
            x = self.own
        term = jnp.sum(self.centre[r] * x, 0)
        self.live[tap] = term if tap not in self.live else self.live[tap] + term


def blocks_kernel(
    lat, high, low, left, right, above, below, cot, cot_left, cot_right,
    w_embed, kernel1, gain1, point1, kernel2, gain2, point2,
    out, packed,
    x0, cots, d, h1, xhat1, scale1, slope1, dd2, g1, dd1,
    taps1, taps2, flip1, flip2, half1, half2, turned1, turned2,
    u1, dp1, u2, dp2, g0, gk1, gk2, gg1, gg2, swap, lifted,
    *, lat_devices,
):
    halves = (slice(0, 128), slice(128, 256))

    for k in range(25):
        for h in (0, 1):
            one = jnp.broadcast_to(kernel1[k : k + 1, halves[h]].astype(F32), (8, 128))
            two = jnp.broadcast_to(kernel2[k : k + 1, halves[h]].astype(F32), (8, 128))
            taps1[h, k] = one
            flip1[h, 24 - k] = one
            taps2[h, k] = two
            flip2[h, 24 - k] = two
    for point, half, turned in ((point1, half1, turned1), (point2, half2, turned2)):
        value = point[...].astype(F32) * 0.5
        half[...] = value.astype(BF16)
        turned[...] = jnp.transpose(value).astype(BF16)
    zeros = jnp.zeros((8, 128), F32)
    for h in (0, 1):
        for ref in (gg1, gg2):
            ref[h] = zeros
        for ref in (gk1, gk2):
            ref[h] = jnp.zeros((25, 8, 128), F32)
        for ref, size in ((x0, FLAT), (h1, FLAT), (dd2, SLIM), (dd1, SLIM)):
            ref[h, 0:LEAD] = jnp.zeros((LEAD, 128), F32)
            ref[h, size - 16 : size] = jnp.zeros((16, 128), F32)

    weight = w_embed[...]

    def across(a, b):
        return lax.dot_general(a, b, (((0,), (0,)), ((), ())), preferred_element_type=F32)

    def embed(spot, values):
        values = values.astype(BF16).astype(F32)
        for h in (0, 1):
            swap[h, pl.ds(pl.multiple_of(spot, 64), values.shape[0]), :] = values[:, halves[h]]

    def spread(spot, row):
        for k in range(8):
            for h in (0, 1):
                x0[h, pl.ds(pl.multiple_of(at(row + k), 8), PITCH), :] = swap[
                    h, pl.ds(spot + k, PITCH, stride=8), :
                ]

    for i in range(ROWS // 16):
        edge = slice(2 * STRIP * i, 2 * STRIP * (i + 1))
        middle = slice(2 * GROUP * i, 2 * GROUP * (i + 1))
        west = across(left[:, edge], weight)
        east = across(right[:, edge], weight)
        centre = across(high[:, middle], weight) + across(low[:, middle], weight)
        for k in (0, 1):
            spot = 8 * PITCH * (2 * i + k)
            embed(spot, west[STRIP * k : STRIP * (k + 1)])
            embed(spot + STRIP, centre[GROUP * k : GROUP * (k + 1)])
            embed(spot + STRIP + GROUP, east[STRIP * k : STRIP * (k + 1)])
    for k, given in ((0, above), (1, below)):
        spot = 8 * PITCH * (ROWS // 8 + k)
        embed(spot, across(given[128 : 128 + VARS], weight))
        embed(spot + CHANS, across(given[208 : 208 + VARS, : 8 * PITCH - CHANS], weight))

    def unravel(i, carry):
        spread(8 * PITCH * i, HALO + 8 * i)
        return carry

    lax.fori_loop(0, ROWS // 8, unravel, 0)
    spread(8 * PITCH * (ROWS // 8), 0)
    spread(8 * PITCH * (ROWS // 8 + 1), HALO + ROWS)

    later = lax.broadcasted_iota(jnp.int32, (8, 128), 0) >= 4

    def put(row, value):
        for h in (0, 1):
            cots[h, pl.ds(pl.multiple_of(inner(row), 8), INNER), :] = value[:, halves[h]]

    def fill(pair, carry):
        sides = [cot_left[pair].astype(F32), cot_right[pair].astype(F32)]
        for odd in (0, 1):
            row = 2 * pair + odd
            edges = [s[4 * odd : 4 * odd + 4] for s in sides]
            put(
                row + HALO, jnp.concatenate([edges[0], cot[row].astype(F32), edges[1]], 0)
            )
        return carry

    lax.fori_loop(0, ROWS // 2, fill, 0)
    for k in range(4):
        rows = slice(INNER * k, INNER * (k + 1))
        put(k + 4, above[rows].astype(F32))
        put(k + HALO + ROWS, below[rows].astype(F32))

    def get(ref, start, count):
        return [ref[h, pl.ds(pl.multiple_of(start, 8), count), :] for h in (0, 1)]

    def keep(ref, start, values):
        for h in (0, 1):
            ref[h, pl.ds(pl.multiple_of(start, 8), values[h].shape[0]), :] = values[h]

    def from_wide(ref, row, rows):
        return [
            jnp.concatenate(
                [ref[h, pl.ds(at(row + r) + 4, INNER), :] for r in range(rows)], 0
            )
            for h in (0, 1)
        ]

    def joined(sums):
        return jnp.concatenate(sums, 0).reshape(-1, 128)

    def local_part(x):
        x = x.reshape(-1, 4, 8, 128)
        ends = jnp.where(later, x[:, 0], x[:, 3])
        return jnp.stack([ends, x[:, 1], x[:, 2]], 1).reshape(-1, 128)

    def gains(ref):
        return [ref[:, halves[h]] for h in (0, 1)]

    def normalised(raw):
        mean = jnp.sum(raw[0] * raw[0] + raw[1] * raw[1], -1, keepdims=True) * (1.0 / CHANS)
        scale = lax.rsqrt(mean + 1e-06)
        return scale, [raw[h] * scale for h in (0, 1)]

    def activated(xhat, gain, point):
        u = [xhat[h] * gain[h] for h in (0, 1)]
        p = jnp.dot(
            jnp.concatenate(u, 1).astype(BF16), point[...], preferred_element_type=F32
        )
        p = [p[:, s] for s in halves]
        rise = [jnp.tanh(v) + 1.0 for v in p]
        silu = [p[h] * rise[h] for h in (0, 1)]
        slope = [rise[h] + silu[h] * (2.0 - rise[h]) for h in (0, 1)]
        return u, silu, slope

    def through_norm(grad, slope, xhat, scale, gain, turned):
        dp = [grad[h] * slope[h] for h in (0, 1)]
        du = jnp.dot(
            jnp.concatenate(dp, 1).astype(BF16), turned[...], preferred_element_type=F32
        )
        gained = [du[:, halves[h]] * gain[h] for h in (0, 1)]
        both = [gained[h] * xhat[h] for h in (0, 1)]
        mean = jnp.sum(both[0] + both[1], -1, keepdims=True) * (1.0 / CHANS)
        dd = [
            (scale * (gained[h] - xhat[h] * mean)).astype(BF16).astype(F32) for h in (0, 1)
        ]
        return dp, both, dd

    def gain_sums(store, both):
        for h in (0, 1):
            store[h] += jnp.sum(local_part(both[h]).reshape(-1, 8, 128), 0)

    def pipeline(blocks, first, second):
        first(0)

        def step(i, carry):
            second(i - 1)
            first(i)
            return carry

        lax.fori_loop(1, blocks, step, 0)
        second(blocks - 1)

    size = 4 * PITCH

    def first_conv(i):
        start = at(2) + i * size
        keep(d, start, [joined(conv(x0, h, start, PITCH, 4, PITCH, taps1)) for h in (0, 1)])

    def first_mix(i):
        start = at(2) + i * size
        scale, xhat = normalised(get(d, start, size))
        _, silu, slope = activated(xhat, gains(gain1), half1)
        x = get(x0, start, size)
        keep(h1, start, [(x[h] + silu[h]).astype(BF16).astype(F32) for h in (0, 1)])
        keep(xhat1, start, xhat)
        keep(slope1, start, slope)
        scale1[pl.ds(pl.multiple_of(start, 8), size), :] = jnp.broadcast_to(scale, (size, 128))

    pipeline((TALL - 4) // 4, first_conv, first_mix)

    @pl.when(lat[0] == 0)
    def _():
        for h in (0, 1):
            h1[h, at(2) : at(HALO)] = jnp.zeros((6 * PITCH, 128), F32)

    @pl.when(lat[0] == lat_devices - 1)
    def _():
        for h in (0, 1):
            h1[h, at(HALO + ROWS) : at(HALO + ROWS + 6)] = jnp.zeros((6 * PITCH, 128), F32)

    def second_conv(row):
        keep(
            d,
            inner(row),
            [joined(conv(h1, h, at(row) + 4, PITCH, 4, INNER, taps2)) for h in (0, 1)],
        )

    def second_mix(row, local):
        start = inner(row)
        scale, xhat = normalised(get(d, start, 4 * INNER))
        gain = gains(gain2)
        u, silu, slope = activated(xhat, gain, half2)
        dp, both, dd = through_norm(
            get(cots, start, 4 * INNER), slope, xhat, scale, gain, turned2
        )
        keep(dd2, start, dd)
        if local is not None:
            keep(lifted, LEAD + 4 * INNER * local, silu)
            spot = pl.ds(pl.multiple_of(local * 96, 96), 96)
            u2[spot] = jnp.concatenate([local_part(v) for v in u], 1).astype(BF16)
            dp2[spot] = jnp.concatenate([local_part(v) for v in dp], 1).astype(BF16)
            gain_sums(gg2, both)

    def result(i):
        total = []
        for h in (0, 1):
            rows = []
            for r in range(4):
                place = LEAD + INNER * (4 * i + r) + 4
                base = h1[h, pl.ds(pl.multiple_of(at(HALO + 4 * i + r) + HALO, 8), COLS), :]
                rows.append(base + lifted[h, pl.ds(place, COLS), :])
            total.append(jnp.concatenate(rows, 0))
        out[pl.ds(i * 4, 4)] = jnp.concatenate(total, 1).reshape(4, COLS, CHANS).astype(BF16)

    for row in (4, HALO + ROWS):
        second_conv(row)
    for row in (4, HALO + ROWS):
        second_mix(row, None)
    pipeline(
        ROWS // 4,
        lambda i: second_conv(HALO + 4 * i),
        lambda i: second_mix(HALO + 4 * i, i),
    )

    def third_conv(row, rows, local):
        start = inner(row)
        total = []
        for h in (0, 1):
            visit = None
            if local:
                centre = [
                    own_tiles(h1[h, pl.ds(at(row + r) + 4, INNER), :].reshape(4, 8, 128))
                    for r in range(rows)
                ]
                visit = TapSums(gk2, h, centre)
            sums = joined(conv(dd2, h, start, INNER, rows, INNER, flip2, visit))
            total.append(sums + cots[h, pl.ds(pl.multiple_of(start, 8), rows * INNER), :])
        keep(g1, start, total)

    def third_mix(row, rows, local):
        start = inner(row)
        gain = gains(gain1)
        xhat = from_wide(xhat1, row, rows)
        scale = jnp.concatenate(
            [scale1[pl.ds(at(row + r) + 4, INNER), :] for r in range(rows)], 0
        )
        dp, both, dd = through_norm(
            get(g1, start, rows * INNER), from_wide(slope1, row, rows), xhat, scale, gain, turned1
        )
        keep(dd1, start, dd)
        if local is not None:
            spot = pl.ds(pl.multiple_of(local * 96, 96), 96)
            u = [local_part(xhat[h] * gain[h]) for h in (0, 1)]
            u1[spot] = jnp.concatenate(u, 1).astype(BF16)
            dp1[spot] = jnp.concatenate([local_part(v) for v in dp], 1).astype(BF16)
            gain_sums(gg1, both)
            result(local)

    for row in (6, HALO + ROWS):
        third_conv(row, 2, False)
    for row in (6, HALO + ROWS):
        third_mix(row, 2, None)
    pipeline(
        ROWS // 4,
        lambda i: third_conv(HALO + 4 * i, 4, True),
        lambda i: third_mix(HALO + 4 * i, 4, i),
    )

    @pl.when(lat[0] == 0)
    def _():
        for h in (0, 1):
            dd1[h, inner(6) : inner(HALO)] = jnp.zeros((2 * INNER, 128), F32)

    @pl.when(lat[0] == lat_devices - 1)
    def _():
        for h in (0, 1):
            dd1[h, inner(HALO + ROWS) : inner(HALO + ROWS + 2)] = jnp.zeros(
                (2 * INNER, 128), F32
            )

    def fourth(i, carry):
        row = HALO + 4 * i
        for h in (0, 1):
            centre = [
                x0[h, pl.ds(pl.multiple_of(at(row + r) + HALO, 8), COLS), :].reshape(3, 8, 128)
                for r in range(4)
            ]
            sums = conv(dd1, h, inner(row) + 4, INNER, 4, COLS, flip1, TapSums(gk1, h, centre))
            for r in range(4):
                base = g1[h, pl.ds(inner(row + r) + 4, COLS), :]
                place = GROUP * (i // 2) + 4 * (i % 2) + r
                g0[h, pl.ds(place, COLS, stride=8), :] = sums[r].reshape(COLS, 128) + base
        return carry

    lax.fori_loop(0, ROWS // 4, fourth, 0)

    def pack(place, value):
        rows = value.shape[0]
        value = value.astype(BF16)
        for h in (0, 1):
            packed[place : place + rows // 8, h] = value[:, halves[h]].reshape(rows // 8, 8, 128)

    pack(0, across(u1[...], dp1[...]) * 0.5)
    pack(32, across(u2[...], dp2[...]) * 0.5)
    field = jnp.concatenate([g0[h] for h in (0, 1)], 1).astype(BF16)
    embedded = jnp.dot(high[...], field, preferred_element_type=F32)

    def gain_row(ref, gain):
        total = [jnp.sum(ref[h], 0, keepdims=True) for h in (0, 1)]
        return jnp.concatenate(total, 1) / gain[...]

    pack(
        64,
        jnp.concatenate(
            [embedded, gain_row(gg1, gain1), gain_row(gg2, gain2), jnp.zeros((1, CHANS), F32)], 0
        ),
    )
    for place, ref in ((73, gk1), (77, gk2)):
        total = jnp.concatenate([jnp.sum(ref[h], 1) for h in (0, 1)], 1)
        pack(place, jnp.concatenate([total, jnp.zeros((7, CHANS), F32)], 0))
    packed[81:TILES] = jnp.zeros((TILES - 81, 2, 8, 128), BF16)


def blocks(fields, weights, lat_devices):
    wide = pltpu.VMEM((2, FLAT, 128), F32)
    slim = pltpu.VMEM((2, SLIM, 128), F32)
    taps = pltpu.VMEM((2, 25, 8, 128), F32)
    square = pltpu.VMEM((CHANS, CHANS), BF16)
    local = pltpu.VMEM((ROWS * COLS, CHANS), BF16)
    eight = pltpu.VMEM((2, 8, 128), F32)
    lat = jnp.reshape(lax.axis_index("lat"), (1,)).astype(jnp.int32)
    operands = (*fields, *weights)
    vmem = pl.BlockSpec(memory_space=pltpu.VMEM)
    return pl.pallas_call(
        functools.partial(blocks_kernel, lat_devices=lat_devices),
        in_specs=[pl.BlockSpec(memory_space=pltpu.SMEM)] + [vmem] * len(operands),
        out_specs=[vmem, vmem],
        out_shape=[
            jax.ShapeDtypeStruct((ROWS, COLS, CHANS), BF16),
            jax.ShapeDtypeStruct((TILES, 2, 8, 128), BF16),
        ],
        scratch_shapes=[wide, slim, wide, wide, wide, pltpu.VMEM((FLAT, 128), F32), wide]
        + [slim] * 3
        + [taps] * 4
        + [square] * 4
        + [local] * 4
        + [pltpu.VMEM((2, ROWS * COLS, 128), F32)]
        + [taps] * 2
        + [eight] * 2
        + [pltpu.VMEM((2, PITCH * TALL, 128), F32)]
        + [pltpu.VMEM((2, LEAD + INNER * ROWS + 16, 128), F32)],
        compiler_params=pltpu.CompilerParams(
            vmem_limit_bytes=60 * 1024 * 1024,
        ),
        name="both_blocks",
    )(lat, *operands)


def unpack_kernel(packed, embed, kernel1, kernel2, point1, point2, gain1, gain2, *, factor):
    for h in (0, 1):
        lanes = slice(128 * h, 128 * h + 128)
        point1[:, lanes] = packed[0:32, h].astype(F32).reshape(CHANS, 128) * factor
        point2[:, lanes] = packed[32:64, h].astype(F32).reshape(CHANS, 128) * factor
        mixed = packed[64:73, h].astype(F32).reshape(72, 128) * factor
        embed[:, lanes] = mixed[:VARS]
        gain1[:, lanes] = mixed[VARS : VARS + 1]
        gain2[:, lanes] = mixed[VARS + 1 : VARS + 2]
        kernel1[:, lanes] = (packed[73:77, h].astype(F32).reshape(32, 128) * factor)[:25]
        kernel2[:, lanes] = (packed[77:81, h].astype(F32).reshape(32, 128) * factor)[:25]


def summed(packed, factor):
    devices = lax.axis_size(AXES)
    parts = lax.all_to_all(packed, AXES, 0, 0, tiled=True)
    mine = jnp.sum(parts.reshape(devices, -1, 2, 8, 128).astype(F32), 0).astype(BF16)
    total = lax.all_to_all(jnp.tile(mine, (devices, 1, 1, 1)), AXES, 0, 0, tiled=True)
    shapes = [(VARS, CHANS), (25, CHANS), (25, CHANS), (CHANS, CHANS), (CHANS, CHANS)]
    results = pl.pallas_call(
        functools.partial(unpack_kernel, factor=factor),
        out_shape=[jax.ShapeDtypeStruct(s, F32) for s in shapes + [(1, CHANS)] * 2],
        name="unpack",
    )(total)
    return (*results[:5], results[5].reshape(CHANS), results[6].reshape(CHANS))


def shifted(before, after, axis, wrap):
    devices = lax.axis_size(axis)
    up = [(i, (i + 1) % devices) for i in range(devices if wrap else devices - 1)]
    down = [(j, i) for i, j in up]
    return lax.ppermute(after, axis, up), lax.ppermute(before, axis, down)


def on_device(points, row_len, w_embed, kernel1, gain1, point1, kernel2, gain2, point2, cotangent):
    lon_total = COLS * lax.axis_size("lon")
    rows_total = ROWS * lax.axis_size("lat")
    cot_left, cot_right = shifted(
        cotangent[:, :4].reshape(ROWS // 2, 8, CHANS),
        cotangent[:, COLS - 4 :].reshape(ROWS // 2, 8, CHANS),
        "lon",
        True,
    )
    high, low, west, east = regrid(jnp.swapaxes(points, 0, 1), row_len, lon_total)
    left, right = shifted(west, east, "lon", True)

    def band(rows, pairs, lanes, edge):
        sides = [c[pairs].reshape(4, 4, CHANS) for c in (cot_left, cot_right)]
        given = jnp.concatenate([sides[0], cotangent[rows], sides[1]], 1).reshape(-1, CHANS)
        field = jnp.concatenate([left[:, edge], high[:, lanes], right[:, edge]], 1)
        pieces = [field[:, :CHANS], field[:, CHANS:]]
        pieces = [
            jnp.pad(x, ((0, 80 - VARS), (0, CHANS - x.shape[1]))) for x in pieces
        ]
        return jnp.concatenate([given, *pieces], 0)

    above, below = shifted(
        band(slice(0, 4), slice(0, 2), slice(0, GROUP), slice(0, STRIP)),
        band(
            slice(ROWS - 4, ROWS),
            slice(ROWS // 2 - 2, ROWS // 2),
            slice(GROUP * (ROWS // 8 - 1), GROUP * (ROWS // 8)),
            slice(STRIP * (ROWS // 8 - 1), STRIP * (ROWS // 8)),
        ),
        "lat",
        False,
    )
    fields = (high, low, left, right, above, below, cotangent, cot_left, cot_right)
    weights = (
        w_embed, kernel1, gain1.reshape(1, CHANS), point1,
        kernel2, gain2.reshape(1, CHANS), point2,
    )
    out, packed = blocks(fields, weights, lax.axis_size("lat"))
    return (out, *summed(packed, float(rows_total * lon_total) ** (-0.5)))


def solution(mesh):
    in_specs = (
        P("lat", None, "lon"),
        P("lat"),
        P(),
        P(),
        P(),
        P(),
        P(),
        P(),
        P(),
        P("lat", "lon", None),
    )
    out_specs = (P("lat", "lon", None), P(), P(), P(), P(), P(), P(), P())
    return jax.shard_map(
        on_device, mesh=mesh, in_specs=in_specs, out_specs=out_specs, check_vma=False
    )
```

```python
import functools

import jax
import jax.numpy as jnp
from jax import lax
from jax.experimental import pallas as pl
from jax.experimental.pallas import tpu as pltpu
from jax.sharding import PartitionSpec as P

F32 = jnp.float32
BF16 = jnp.bfloat16
ROWS = 64
COLS = 24
HALO = 8
PITCH = COLS + 2 * HALO
TALL = ROWS + 2 * HALO
INNER = COLS + 8
LEAD = 16
FLAT = LEAD + PITCH * TALL + 16
SLIM = LEAD + INNER * TALL + 16
CHANS = 256
VARS = 69
TILES = 128
AXES = ("lon", "lat")


GROUP = 8 * COLS
STRIP = 8 * HALO


def regrid_kernel(
    row_len, sector, points, high, low, west, east, held, arrived, *, lon_total
):
    batch = held.shape[2]
    copies = [
        pltpu.make_async_copy(
            points.at[:, batch * i : batch * (i + 1)], held.at[i], arrived.at[i]
        )
        for i in range(held.shape[0])
    ]
    for copy in copies:
        copy.start()
    slots = points.shape[3]
    first = (sector[0] * COLS).astype(F32)
    whole = lon_total // 4
    lane = lax.broadcasted_iota(jnp.int32, (8, GROUP), 1)
    row = lane % 8
    cell = first + (lane // 8).astype(F32)
    own = lax.broadcasted_iota(jnp.int32, (8, GROUP), 0) == row
    mark = lax.broadcasted_iota(jnp.int32, (slots, GROUP), 0).astype(F32)
    for i, copy in enumerate(copies):
        found = []
        copy.wait()
        for k in range(batch):
            count = jnp.zeros((8, GROUP), F32)
            for q in range(8):
                length = row_len[8 * (batch * i + k) + q]
                count = jnp.where(row == q, length.astype(F32), count)
            product = cell * count
            lower = jnp.floor((product + 2.0) * (1.0 / lon_total))
            start = jnp.floor((first * count + 2.0) * (1.0 / lon_total))
            share = (product - lower * lon_total) * 0.25
            away = mark - (lower - start)[:1]
            mix = jnp.where(
                away == 0.0, whole - share[:1], jnp.where(away == 1.0, share[:1], 0.0)
            )
            rows = held[i, :, k].reshape(VARS * 8, slots)
            every = jnp.dot(rows, mix.astype(BF16), preferred_element_type=F32)
            kept = jnp.where(own[None], every.reshape(VARS, 8, GROUP), 0.0)
            found.append(jnp.sum(kept, 1) * (1.0 / whole))
        lanes = slice(batch * GROUP * i, batch * GROUP * (i + 1))
        edge = slice(batch * STRIP * i, batch * STRIP * (i + 1))
        values = jnp.concatenate(found, 1)
        rounded = values.astype(BF16)
        high[:, lanes] = rounded
        low[:, lanes] = (values - rounded.astype(F32)).astype(BF16)
        west[:, edge] = jnp.concatenate([f[:, :STRIP] for f in found], 1).astype(BF16)
        east[:, edge] = jnp.concatenate([f[:, GROUP - STRIP :] for f in found], 1).astype(BF16)


def regrid(points, row_len, lon_total):
    nvars, nrows, slots = points.shape
    batches = 4
    strips = jax.ShapeDtypeStruct((nvars, nrows * HALO), BF16)
    full = jax.ShapeDtypeStruct((nvars, nrows * COLS), BF16)
    smem = pl.BlockSpec(memory_space=pltpu.SMEM)
    vmem = pl.BlockSpec(memory_space=pltpu.VMEM)
    return pl.pallas_call(
        functools.partial(regrid_kernel, lon_total=lon_total),
        in_specs=[smem, smem, pl.BlockSpec(memory_space=pl.ANY)],
        out_specs=[vmem] * 4,
        out_shape=[full, full, strips, strips],
        scratch_shapes=[
            pltpu.VMEM((batches, nvars, nrows // (8 * batches), 8, slots), BF16),
            pltpu.SemaphoreType.DMA((batches,)),
        ],
        name="regrid",
    )(
        row_len,
        jnp.reshape(lax.axis_index("lon"), (1,)).astype(jnp.int32),
        points.reshape(nvars, nrows // 8, 8, slots),
    )


def at(row):
    return LEAD + PITCH * row


def inner(row):
    return LEAD + INNER * row


def conv(source, half, start, pitch, rows, cols, taps, visit=None):
    sums = [None] * rows
    for e in range(5):
        weights = [taps[half, 5 * a + e] for a in range(5)]
        for i in range(rows + 4):
            x = source[half, pl.ds(start + pitch * (i - 2) + e - 2, cols), :]
            x = x.reshape(cols // 8, 8, 128)
            for a in range(5):
                r = i - a
                if 0 <= r < rows:
                    term = x * weights[a]
                    sums[r] = term if sums[r] is None else sums[r] + term
                    if visit is not None:
                        visit(a, e, r, x)
        if visit is not None:
            visit(None, e, None, None)
    return sums


def own_tiles(x):
    later = lax.broadcasted_iota(jnp.int32, (8, 128), 0) >= 4
    return jnp.stack([jnp.where(later, x[0], x[3]), x[1], x[2]])


class TapSums:
    def __init__(self, store, half, centre):
        self.store, self.half, self.centre, self.live = store, half, centre, {}
        self.seen = self.own = None

    def __call__(self, a, e, r, x):
        if a is None:
            for tap, value in self.live.items():
                self.store[self.half, tap] += value
            self.live = {}
            return
        tap = 24 - (5 * a + e)
        if x.shape[0] == 4:
            if self.seen is not x:
                self.seen, self.own = x, own_tiles(x)
            x = self.own
        term = jnp.sum(self.centre[r] * x, 0)
        self.live[tap] = term if tap not in self.live else self.live[tap] + term


def blocks_kernel(
    lat, high, low, left, right, near, far, cot, cot_left, cot_right,
    w_embed, kernel1, gain1, point1, kernel2, gain2, point2,
    out, packed,
    x0, cots, d, h1, xhat1, scale1, slope1, dd2, g1, dd1,
    taps1, taps2, flip1, flip2, half1, half2, turned1, turned2,
    u1, dp1, u2, dp2, g0, gk1, gk2, gg1, gg2, swap, lifted,
    *, lat_devices,
):
    halves = (slice(0, 128), slice(128, 256))

    for k in range(25):
        for h in (0, 1):
            one = jnp.broadcast_to(kernel1[k : k + 1, halves[h]].astype(F32), (8, 128))
            two = jnp.broadcast_to(kernel2[k : k + 1, halves[h]].astype(F32), (8, 128))
            taps1[h, k] = one
            flip1[h, 24 - k] = one
            taps2[h, k] = two
            flip2[h, 24 - k] = two
    for point, half, turned in ((point1, half1, turned1), (point2, half2, turned2)):
        value = point[...].astype(F32) * 0.5
        half[...] = value.astype(BF16)
        turned[...] = jnp.transpose(value).astype(BF16)
    zeros = jnp.zeros((8, 128), F32)
    for h in (0, 1):
        for ref in (gg1, gg2):
            ref[h] = zeros
        for ref in (gk1, gk2):
            ref[h] = jnp.zeros((25, 8, 128), F32)
        for ref, size in ((x0, FLAT), (h1, FLAT), (dd2, SLIM), (dd1, SLIM)):
            ref[h, 0:LEAD] = jnp.zeros((LEAD, 128), F32)
            ref[h, size - 16 : size] = jnp.zeros((16, 128), F32)

    weight = w_embed[...]

    def across(a, b):
        return lax.dot_general(a, b, (((0,), (0,)), ((), ())), preferred_element_type=F32)

    def embed(spot, values):
        values = values.astype(BF16).astype(F32)
        for h in (0, 1):
            swap[h, pl.ds(pl.multiple_of(spot, 64), values.shape[0]), :] = values[:, halves[h]]

    def spread(spot, row):
        for k in range(8):
            for h in (0, 1):
                x0[h, pl.ds(pl.multiple_of(at(row + k), 8), PITCH), :] = swap[
                    h, pl.ds(spot + k, PITCH, stride=8), :
                ]

    for i in range(ROWS // 16):
        edge = slice(2 * STRIP * i, 2 * STRIP * (i + 1))
        middle = slice(2 * GROUP * i, 2 * GROUP * (i + 1))
        west = across(left[:, edge], weight)
        east = across(right[:, edge], weight)
        centre = across(high[:, middle], weight) + across(low[:, middle], weight)
        for k in (0, 1):
            spot = 8 * PITCH * (2 * i + k)
            embed(spot, west[STRIP * k : STRIP * (k + 1)])
            embed(spot + STRIP, centre[GROUP * k : GROUP * (k + 1)])
            embed(spot + STRIP + GROUP, east[STRIP * k : STRIP * (k + 1)])
    odd = lat[0] % 2 == 1

    def beyond(k, rows, lanes=slice(None)):
        one, two = near[rows, lanes].astype(F32), far[rows, lanes].astype(F32)
        return jnp.where(odd, two, one) if k else jnp.where(odd, one, two)

    for k in (0, 1):
        spot = 8 * PITCH * (ROWS // 8 + k)
        main = beyond(k, slice(128, 128 + VARS)).astype(BF16)
        rest = beyond(k, slice(208, 208 + VARS), slice(0, 8 * PITCH - CHANS)).astype(BF16)
        embed(spot, across(main, weight))
        embed(spot + CHANS, across(rest, weight))

    def unravel(i, carry):
        spread(8 * PITCH * i, HALO + 8 * i)
        return carry

    lax.fori_loop(0, ROWS // 8, unravel, 0)
    spread(8 * PITCH * (ROWS // 8), 0)
    spread(8 * PITCH * (ROWS // 8 + 1), HALO + ROWS)

    later = lax.broadcasted_iota(jnp.int32, (8, 128), 0) >= 4

    def put(row, value):
        for h in (0, 1):
            cots[h, pl.ds(pl.multiple_of(inner(row), 8), INNER), :] = value[:, halves[h]]

    def fill(pair, carry):
        sides = [cot_left[pair].astype(F32), cot_right[pair].astype(F32)]
        for odd in (0, 1):
            row = 2 * pair + odd
            edges = [s[4 * odd : 4 * odd + 4] for s in sides]
            put(
                row + HALO, jnp.concatenate([edges[0], cot[row].astype(F32), edges[1]], 0)
            )
        return carry

    lax.fori_loop(0, ROWS // 2, fill, 0)
    for k in range(4):
        rows = slice(INNER * k, INNER * (k + 1))
        put(k + 4, beyond(0, rows))
        put(k + HALO + ROWS, beyond(1, rows))

    def get(ref, start, count):
        return [ref[h, pl.ds(pl.multiple_of(start, 8), count), :] for h in (0, 1)]

    def keep(ref, start, values):
        for h in (0, 1):
            ref[h, pl.ds(pl.multiple_of(start, 8), values[h].shape[0]), :] = values[h]

    def from_wide(ref, row, rows):
        return [
            jnp.concatenate(
                [ref[h, pl.ds(at(row + r) + 4, INNER), :] for r in range(rows)], 0
            )
            for h in (0, 1)
        ]

    def joined(sums):
        return jnp.concatenate(sums, 0).reshape(-1, 128)

    def local_part(x):
        x = x.reshape(-1, 4, 8, 128)
        ends = jnp.where(later, x[:, 0], x[:, 3])
        return jnp.stack([ends, x[:, 1], x[:, 2]], 1).reshape(-1, 128)

    def gains(ref):
        return [ref[:, halves[h]] for h in (0, 1)]

    def normalised(raw):
        mean = jnp.sum(raw[0] * raw[0] + raw[1] * raw[1], -1, keepdims=True) * (1.0 / CHANS)
        scale = lax.rsqrt(mean + 1e-06)
        return scale, [raw[h] * scale for h in (0, 1)]

    def activated(xhat, gain, point):
        u = [xhat[h] * gain[h] for h in (0, 1)]
        p = jnp.dot(
            jnp.concatenate(u, 1).astype(BF16), point[...], preferred_element_type=F32
        )
        p = [p[:, s] for s in halves]
        rise = [jnp.tanh(v) + 1.0 for v in p]
        silu = [p[h] * rise[h] for h in (0, 1)]
        slope = [rise[h] + silu[h] * (2.0 - rise[h]) for h in (0, 1)]
        return u, silu, slope

    def through_norm(grad, slope, xhat, scale, gain, turned):
        dp = [grad[h] * slope[h] for h in (0, 1)]
        du = jnp.dot(
            jnp.concatenate(dp, 1).astype(BF16), turned[...], preferred_element_type=F32
        )
        gained = [du[:, halves[h]] * gain[h] for h in (0, 1)]
        both = [gained[h] * xhat[h] for h in (0, 1)]
        mean = jnp.sum(both[0] + both[1], -1, keepdims=True) * (1.0 / CHANS)
        dd = [
            (scale * (gained[h] - xhat[h] * mean)).astype(BF16).astype(F32) for h in (0, 1)
        ]
        return dp, both, dd

    def gain_sums(store, both):
        for h in (0, 1):
            store[h] += jnp.sum(local_part(both[h]).reshape(-1, 8, 128), 0)

    def pipeline(blocks, first, second):
        first(0)

        def step(i, carry):
            second(i - 1)
            first(i)
            return carry

        lax.fori_loop(1, blocks, step, 0)
        second(blocks - 1)

    size = 4 * PITCH

    def first_conv(i):
        start = at(2) + i * size
        keep(d, start, [joined(conv(x0, h, start, PITCH, 4, PITCH, taps1)) for h in (0, 1)])

    def first_mix(i):
        start = at(2) + i * size
        scale, xhat = normalised(get(d, start, size))
        _, silu, slope = activated(xhat, gains(gain1), half1)
        x = get(x0, start, size)
        keep(h1, start, [(x[h] + silu[h]).astype(BF16).astype(F32) for h in (0, 1)])
        keep(xhat1, start, xhat)
        keep(slope1, start, slope)
        scale1[pl.ds(pl.multiple_of(start, 8), size), :] = jnp.broadcast_to(scale, (size, 128))

    pipeline((TALL - 4) // 4, first_conv, first_mix)

    @pl.when(lat[0] == 0)
    def _():
        for h in (0, 1):
            h1[h, at(2) : at(HALO)] = jnp.zeros((6 * PITCH, 128), F32)

    @pl.when(lat[0] == lat_devices - 1)
    def _():
        for h in (0, 1):
            h1[h, at(HALO + ROWS) : at(HALO + ROWS + 6)] = jnp.zeros((6 * PITCH, 128), F32)

    def second_conv(row):
        keep(
            d,
            inner(row),
            [joined(conv(h1, h, at(row) + 4, PITCH, 4, INNER, taps2)) for h in (0, 1)],
        )

    def second_mix(row, local):
        start = inner(row)
        scale, xhat = normalised(get(d, start, 4 * INNER))
        gain = gains(gain2)
        u, silu, slope = activated(xhat, gain, half2)
        dp, both, dd = through_norm(
            get(cots, start, 4 * INNER), slope, xhat, scale, gain, turned2
        )
        keep(dd2, start, dd)
        if local is not None:
            keep(lifted, LEAD + 4 * INNER * local, silu)
            spot = pl.ds(pl.multiple_of(local * 96, 96), 96)
            u2[spot] = jnp.concatenate([local_part(v) for v in u], 1).astype(BF16)
            dp2[spot] = jnp.concatenate([local_part(v) for v in dp], 1).astype(BF16)
            gain_sums(gg2, both)

    def result(i):
        total = []
        for h in (0, 1):
            rows = []
            for r in range(4):
                place = LEAD + INNER * (4 * i + r) + 4
                base = h1[h, pl.ds(pl.multiple_of(at(HALO + 4 * i + r) + HALO, 8), COLS), :]
                rows.append(base + lifted[h, pl.ds(place, COLS), :])
            total.append(jnp.concatenate(rows, 0))
        out[pl.ds(i * 4, 4)] = jnp.concatenate(total, 1).reshape(4, COLS, CHANS).astype(BF16)

    for row in (4, HALO + ROWS):
        second_conv(row)
    for row in (4, HALO + ROWS):
        second_mix(row, None)
    pipeline(
        ROWS // 4,
        lambda i: second_conv(HALO + 4 * i),
        lambda i: second_mix(HALO + 4 * i, i),
    )

    def third_conv(row, rows, local):
        start = inner(row)
        total = []
        for h in (0, 1):
            visit = None
            if local:
                centre = [
                    own_tiles(h1[h, pl.ds(at(row + r) + 4, INNER), :].reshape(4, 8, 128))
                    for r in range(rows)
                ]
                visit = TapSums(gk2, h, centre)
            sums = joined(conv(dd2, h, start, INNER, rows, INNER, flip2, visit))
            total.append(sums + cots[h, pl.ds(pl.multiple_of(start, 8), rows * INNER), :])
        keep(g1, start, total)

    def third_mix(row, rows, local):
        start = inner(row)
        gain = gains(gain1)
        xhat = from_wide(xhat1, row, rows)
        scale = jnp.concatenate(
            [scale1[pl.ds(at(row + r) + 4, INNER), :] for r in range(rows)], 0
        )
        dp, both, dd = through_norm(
            get(g1, start, rows * INNER), from_wide(slope1, row, rows), xhat, scale, gain, turned1
        )
        keep(dd1, start, dd)
        if local is not None:
            spot = pl.ds(pl.multiple_of(local * 96, 96), 96)
            u = [local_part(xhat[h] * gain[h]) for h in (0, 1)]
            u1[spot] = jnp.concatenate(u, 1).astype(BF16)
            dp1[spot] = jnp.concatenate([local_part(v) for v in dp], 1).astype(BF16)
            gain_sums(gg1, both)
            result(local)

    for row in (6, HALO + ROWS):
        third_conv(row, 2, False)
    for row in (6, HALO + ROWS):
        third_mix(row, 2, None)
    pipeline(
        ROWS // 4,
        lambda i: third_conv(HALO + 4 * i, 4, True),
        lambda i: third_mix(HALO + 4 * i, 4, i),
    )

    @pl.when(lat[0] == 0)
    def _():
        for h in (0, 1):
            dd1[h, inner(6) : inner(HALO)] = jnp.zeros((2 * INNER, 128), F32)

    @pl.when(lat[0] == lat_devices - 1)
    def _():
        for h in (0, 1):
            dd1[h, inner(HALO + ROWS) : inner(HALO + ROWS + 2)] = jnp.zeros(
                (2 * INNER, 128), F32
            )

    def fourth(i, carry):
        row = HALO + 4 * i
        for h in (0, 1):
            centre = [
                x0[h, pl.ds(pl.multiple_of(at(row + r) + HALO, 8), COLS), :].reshape(3, 8, 128)
                for r in range(4)
            ]
            sums = conv(dd1, h, inner(row) + 4, INNER, 4, COLS, flip1, TapSums(gk1, h, centre))
            for r in range(4):
                base = g1[h, pl.ds(inner(row + r) + 4, COLS), :]
                place = GROUP * (i // 2) + 4 * (i % 2) + r
                g0[h, pl.ds(place, COLS, stride=8), :] = sums[r].reshape(COLS, 128) + base
        return carry

    lax.fori_loop(0, ROWS // 4, fourth, 0)

    def pack(place, value):
        rows = value.shape[0]
        value = value.astype(BF16)
        for h in (0, 1):
            packed[place : place + rows // 8, h] = value[:, halves[h]].reshape(rows // 8, 8, 128)

    pack(0, across(u1[...], dp1[...]) * 0.5)
    pack(32, across(u2[...], dp2[...]) * 0.5)
    field = jnp.concatenate([g0[h] for h in (0, 1)], 1).astype(BF16)
    embedded = jnp.dot(high[...], field, preferred_element_type=F32)

    def gain_row(ref, gain):
        total = [jnp.sum(ref[h], 0, keepdims=True) for h in (0, 1)]
        return jnp.concatenate(total, 1) / gain[...]

    pack(
        64,
        jnp.concatenate(
            [embedded, gain_row(gg1, gain1), gain_row(gg2, gain2), jnp.zeros((1, CHANS), F32)], 0
        ),
    )
    for place, ref in ((73, gk1), (77, gk2)):
        total = jnp.concatenate([jnp.sum(ref[h], 1) for h in (0, 1)], 1)
        pack(place, jnp.concatenate([total, jnp.zeros((7, CHANS), F32)], 0))
    packed[81:TILES] = jnp.zeros((TILES - 81, 2, 8, 128), BF16)


def blocks(fields, weights, lat_devices):
    wide = pltpu.VMEM((2, FLAT, 128), F32)
    slim = pltpu.VMEM((2, SLIM, 128), F32)
    taps = pltpu.VMEM((2, 25, 8, 128), F32)
    square = pltpu.VMEM((CHANS, CHANS), BF16)
    local = pltpu.VMEM((ROWS * COLS, CHANS), BF16)
    eight = pltpu.VMEM((2, 8, 128), F32)
    lat = jnp.reshape(lax.axis_index("lat"), (1,)).astype(jnp.int32)
    operands = (*fields, *weights)
    vmem = pl.BlockSpec(memory_space=pltpu.VMEM)
    return pl.pallas_call(
        functools.partial(blocks_kernel, lat_devices=lat_devices),
        in_specs=[pl.BlockSpec(memory_space=pltpu.SMEM)] + [vmem] * len(operands),
        out_specs=[vmem, vmem],
        out_shape=[
            jax.ShapeDtypeStruct((ROWS, COLS, CHANS), BF16),
            jax.ShapeDtypeStruct((TILES, 2, 8, 128), BF16),
        ],
        scratch_shapes=[wide, slim, wide, wide, wide, pltpu.VMEM((FLAT, 128), F32), wide]
        + [slim] * 3
        + [taps] * 4
        + [square] * 4
        + [local] * 4
        + [pltpu.VMEM((2, ROWS * COLS, 128), F32)]
        + [taps] * 2
        + [eight] * 2
        + [pltpu.VMEM((2, PITCH * TALL, 128), F32)]
        + [pltpu.VMEM((2, LEAD + INNER * ROWS + 16, 128), F32)],
        compiler_params=pltpu.CompilerParams(vmem_limit_bytes=60 * 1024 * 1024),
        name="both_blocks",
    )(lat, *operands)


def unpack_kernel(packed, embed, kernel1, kernel2, point1, point2, gain1, gain2, *, factor):
    for h in (0, 1):
        lanes = slice(128 * h, 128 * h + 128)
        point1[:, lanes] = packed[0:32, h].astype(F32).reshape(CHANS, 128) * factor
        point2[:, lanes] = packed[32:64, h].astype(F32).reshape(CHANS, 128) * factor
        mixed = packed[64:73, h].astype(F32).reshape(72, 128) * factor
        embed[:, lanes] = mixed[:VARS]
        gain1[:, lanes] = mixed[VARS : VARS + 1]
        gain2[:, lanes] = mixed[VARS + 1 : VARS + 2]
        kernel1[:, lanes] = (packed[73:77, h].astype(F32).reshape(32, 128) * factor)[:25]
        kernel2[:, lanes] = (packed[77:81, h].astype(F32).reshape(32, 128) * factor)[:25]


def summed(packed, factor):
    devices = lax.axis_size(AXES)
    parts = lax.all_to_all(packed, AXES, 0, 0, tiled=True)
    mine = jnp.sum(parts.reshape(devices, -1, 2, 8, 128).astype(F32), 0).astype(BF16)
    total = lax.all_to_all(jnp.tile(mine, (devices, 1, 1, 1)), AXES, 0, 0, tiled=True)
    shapes = [(VARS, CHANS), (25, CHANS), (25, CHANS), (CHANS, CHANS), (CHANS, CHANS)]
    results = pl.pallas_call(
        functools.partial(unpack_kernel, factor=factor),
        out_shape=[jax.ShapeDtypeStruct(s, F32) for s in shapes + [(1, CHANS)] * 2],
        name="unpack",
    )(total)
    return (*results[:5], results[5].reshape(CHANS), results[6].reshape(CHANS))


def shifted(before, after, axis, wrap):
    devices = lax.axis_size(axis)
    up = [(i, (i + 1) % devices) for i in range(devices if wrap else devices - 1)]
    down = [(j, i) for i, j in up]
    return lax.ppermute(after, axis, up), lax.ppermute(before, axis, down)


def on_device(points, row_len, w_embed, kernel1, gain1, point1, kernel2, gain2, point2, cotangent):
    lon_total = COLS * lax.axis_size("lon")
    rows_total = ROWS * lax.axis_size("lat")
    cot_left, cot_right = shifted(
        cotangent[:, :4].reshape(ROWS // 2, 8, CHANS),
        cotangent[:, COLS - 4 :].reshape(ROWS // 2, 8, CHANS),
        "lon",
        True,
    )
    high, low, west, east = regrid(jnp.swapaxes(points, 0, 1), row_len, lon_total)
    left, right = shifted(west, east, "lon", True)

    def band(rows, pairs, lanes, edge):
        sides = [c[pairs].reshape(4, 4, CHANS) for c in (cot_left, cot_right)]
        given = jnp.concatenate([sides[0], cotangent[rows], sides[1]], 1).reshape(-1, CHANS)
        field = jnp.concatenate([left[:, edge], high[:, lanes], right[:, edge]], 1)
        pieces = [field[:, :CHANS], field[:, CHANS:]]
        pieces = [
            jnp.pad(x, ((0, 80 - VARS), (0, CHANS - x.shape[1]))) for x in pieces
        ]
        return jnp.concatenate([given, *pieces], 0)

    first_band = band(slice(0, 4), slice(0, 2), slice(0, GROUP), slice(0, STRIP))
    last_band = band(
        slice(ROWS - 4, ROWS),
        slice(ROWS // 2 - 2, ROWS // 2),
        slice(GROUP * (ROWS // 8 - 1), GROUP * (ROWS // 8)),
        slice(STRIP * (ROWS // 8 - 1), STRIP * (ROWS // 8)),
    )
    odd = lax.axis_index("lat") % 2 == 1
    sent = (jnp.where(odd, first_band, last_band), jnp.where(odd, last_band, first_band))
    swaps = []
    for start in (0, 1):
        pairs = [(i, i + 1) for i in range(start, lax.axis_size("lat") - 1, 2)]
        swaps.append(lax.ppermute(sent[start], "lat", pairs + [(j, i) for i, j in pairs]))
    above, below = swaps
    fields = (high, low, left, right, above, below, cotangent, cot_left, cot_right)
    weights = (
        w_embed, kernel1, gain1.reshape(1, CHANS), point1,
        kernel2, gain2.reshape(1, CHANS), point2,
    )
    out, packed = blocks(fields, weights, lax.axis_size("lat"))
    return (out, *summed(packed, float(rows_total * lon_total) ** (-0.5)))


def solution(mesh):
    in_specs = (
        P("lat", None, "lon"),
        P("lat"),
        P(),
        P(),
        P(),
        P(),
        P(),
        P(),
        P(),
        P("lat", "lon", None),
    )
    out_specs = (P("lat", "lon", None), P(), P(), P(), P(), P(), P(), P())
    return jax.shard_map(
        on_device, mesh=mesh, in_specs=in_specs, out_specs=out_specs, check_vma=False
    )
```

```python
import functools

import jax
import jax.numpy as jnp
from jax import lax
from jax.experimental import pallas as pl
from jax.experimental.pallas import tpu as pltpu
from jax.sharding import PartitionSpec as P

F32 = jnp.float32
BF16 = jnp.bfloat16
ROWS = 64
COLS = 24
HALO = 8
PITCH = COLS + 2 * HALO
TALL = ROWS + 2 * HALO
INNER = COLS + 8
LEAD = 16
FLAT = LEAD + PITCH * TALL + 16
SLIM = LEAD + INNER * TALL + 16
CHANS = 256
VARS = 69
TILES = 128
AXES = ("lon", "lat")


GROUP = 8 * COLS
STRIP = 8 * HALO


def regrid_kernel(
    row_len, sector, points, high, low, west, east, held, arrived, *, lon_total
):
    batch = held.shape[2]
    copies = [
        pltpu.make_async_copy(
            points.at[:, batch * i : batch * (i + 1)], held.at[i], arrived.at[i]
        )
        for i in range(held.shape[0])
    ]
    for copy in copies:
        copy.start()
    slots = points.shape[3]
    first = (sector[0] * COLS).astype(F32)
    whole = lon_total // 4
    lane = lax.broadcasted_iota(jnp.int32, (8, GROUP), 1)
    row = lane % 8
    cell = first + (lane // 8).astype(F32)
    own = lax.broadcasted_iota(jnp.int32, (8, GROUP), 0) == row
    mark = lax.broadcasted_iota(jnp.int32, (slots, GROUP), 0).astype(F32)
    for i, copy in enumerate(copies):
        found = []
        copy.wait()
        for k in range(batch):
            count = jnp.zeros((8, GROUP), F32)
            for q in range(8):
                length = row_len[8 * (batch * i + k) + q]
                count = jnp.where(row == q, length.astype(F32), count)
            product = cell * count
            lower = jnp.floor((product + 2.0) * (1.0 / lon_total))
            start = jnp.floor((first * count + 2.0) * (1.0 / lon_total))
            share = (product - lower * lon_total) * 0.25
            away = mark - (lower - start)[:1]
            mix = jnp.where(
                away == 0.0, whole - share[:1], jnp.where(away == 1.0, share[:1], 0.0)
            )
            rows = held[i, :, k].reshape(VARS * 8, slots)
            every = jnp.dot(rows, mix.astype(BF16), preferred_element_type=F32)
            kept = jnp.where(own[None], every.reshape(VARS, 8, GROUP), 0.0)
            found.append(jnp.sum(kept, 1) * (1.0 / whole))
        lanes = slice(batch * GROUP * i, batch * GROUP * (i + 1))
        edge = slice(batch * STRIP * i, batch * STRIP * (i + 1))
        values = jnp.concatenate(found, 1)
        rounded = values.astype(BF16)
        high[:, lanes] = rounded
        low[:, lanes] = (values - rounded.astype(F32)).astype(BF16)
        west[:, edge] = jnp.concatenate([f[:, :STRIP] for f in found], 1).astype(BF16)
        east[:, edge] = jnp.concatenate([f[:, GROUP - STRIP :] for f in found], 1).astype(BF16)


def regrid(points, row_len, lon_total):
    nvars, nrows, slots = points.shape
    batches = 4
    strips = jax.ShapeDtypeStruct((nvars, nrows * HALO), BF16)
    full = jax.ShapeDtypeStruct((nvars, nrows * COLS), BF16)
    smem = pl.BlockSpec(memory_space=pltpu.SMEM)
    vmem = pl.BlockSpec(memory_space=pltpu.VMEM)
    return pl.pallas_call(
        functools.partial(regrid_kernel, lon_total=lon_total),
        in_specs=[smem, smem, pl.BlockSpec(memory_space=pl.ANY)],
        out_specs=[vmem] * 4,
        out_shape=[full, full, strips, strips],
        scratch_shapes=[
            pltpu.VMEM((batches, nvars, nrows // (8 * batches), 8, slots), BF16),
            pltpu.SemaphoreType.DMA((batches,)),
        ],
        name="regrid",
    )(
        row_len,
        jnp.reshape(lax.axis_index("lon"), (1,)).astype(jnp.int32),
        points.reshape(nvars, nrows // 8, 8, slots),
    )


def at(row):
    return LEAD + PITCH * row


def inner(row):
    return LEAD + INNER * row


def conv(source, half, start, pitch, rows, cols, taps, visit=None):
    sums = [None] * rows
    for e in range(5):
        weights = [taps[half, 5 * a + e] for a in range(5)]
        for i in range(rows + 4):
            x = source[half, pl.ds(start + pitch * (i - 2) + e - 2, cols), :]
            x = x.reshape(cols // 8, 8, 128)
            for a in range(5):
                r = i - a
                if 0 <= r < rows:
                    term = x * weights[a]
                    sums[r] = term if sums[r] is None else sums[r] + term
                    if visit is not None:
                        visit(a, e, r, x)
        if visit is not None:
            visit(None, e, None, None)
    return sums


def own_tiles(x):
    later = lax.broadcasted_iota(jnp.int32, (8, 128), 0) >= 4
    return jnp.stack([jnp.where(later, x[0], x[3]), x[1], x[2]])


class TapSums:
    def __init__(self, store, half, centre):
        self.store, self.half, self.centre, self.live = store, half, centre, {}
        self.seen = self.own = None

    def __call__(self, a, e, r, x):
        if a is None:
            for tap, value in self.live.items():
                self.store[self.half, tap] += value
            self.live = {}
            return
        tap = 24 - (5 * a + e)
        if x.shape[0] == 4:
            if self.seen is not x:
                self.seen, self.own = x, own_tiles(x)
            x = self.own
        term = jnp.sum(self.centre[r] * x, 0)
        self.live[tap] = term if tap not in self.live else self.live[tap] + term


def blocks_kernel(
    lat, high, low, left, right, near, far, cot, cot_left, cot_right,
    w_embed, kernel1, gain1, point1, kernel2, gain2, point2,
    out, packed,
    x0, cots, d, h1, xhat1, scale1, slope1, dd2, g1, dd1,
    taps1, taps2, flip1, flip2, half1, half2, turned1, turned2,
    u1, dp1, u2, dp2, g0, gk1, gk2, gg1, gg2, swap, lifted,
    *, lat_devices,
):
    halves = (slice(0, 128), slice(128, 256))

    for k in range(25):
        for h in (0, 1):
            one = jnp.broadcast_to(kernel1[k : k + 1, halves[h]].astype(F32), (8, 128))
            two = jnp.broadcast_to(kernel2[k : k + 1, halves[h]].astype(F32), (8, 128))
            taps1[h, k] = one
            flip1[h, 24 - k] = one
            taps2[h, k] = two
            flip2[h, 24 - k] = two
    for point, half, turned in ((point1, half1, turned1), (point2, half2, turned2)):
        value = point[...].astype(F32) * 0.5
        half[...] = value.astype(BF16)
        turned[...] = jnp.transpose(value).astype(BF16)
    zeros = jnp.zeros((8, 128), F32)
    for h in (0, 1):
        for ref in (gg1, gg2):
            ref[h] = zeros
        for ref in (gk1, gk2):
            ref[h] = jnp.zeros((25, 8, 128), F32)
        for ref, size in ((x0, FLAT), (h1, FLAT), (dd2, SLIM), (dd1, SLIM)):
            ref[h, 0:LEAD] = jnp.zeros((LEAD, 128), F32)
            ref[h, size - 16 : size] = jnp.zeros((16, 128), F32)

    weight = w_embed[...]

    def across(a, b):
        return lax.dot_general(a, b, (((0,), (0,)), ((), ())), preferred_element_type=F32)

    def embed(spot, values):
        values = values.astype(BF16).astype(F32)
        for h in (0, 1):
            swap[h, pl.ds(pl.multiple_of(spot, 64), values.shape[0]), :] = values[:, halves[h]]

    def spread(spot, row):
        for k in range(8):
            for h in (0, 1):
                x0[h, pl.ds(pl.multiple_of(at(row + k), 8), PITCH), :] = swap[
                    h, pl.ds(spot + k, PITCH, stride=8), :
                ]

    for i in range(ROWS // 16):
        edge = slice(2 * STRIP * i, 2 * STRIP * (i + 1))
        middle = slice(2 * GROUP * i, 2 * GROUP * (i + 1))
        west = across(left[:, edge], weight)
        east = across(right[:, edge], weight)
        centre = across(high[:, middle], weight) + across(low[:, middle], weight)
        for k in (0, 1):
            spot = 8 * PITCH * (2 * i + k)
            embed(spot, west[STRIP * k : STRIP * (k + 1)])
            embed(spot + STRIP, centre[GROUP * k : GROUP * (k + 1)])
            embed(spot + STRIP + GROUP, east[STRIP * k : STRIP * (k + 1)])
    odd = lat[0] % 2 == 1

    def beyond(k, rows, lanes=slice(None)):
        one, two = near[rows, lanes].astype(F32), far[rows, lanes].astype(F32)
        return jnp.where(odd, two, one) if k else jnp.where(odd, one, two)

    for k in (0, 1):
        spot = 8 * PITCH * (ROWS // 8 + k)
        main = beyond(k, slice(128, 128 + VARS)).astype(BF16)
        rest = beyond(k, slice(208, 208 + VARS), slice(0, 8 * PITCH - CHANS)).astype(BF16)
        embed(spot, across(main, weight))
        embed(spot + CHANS, across(rest, weight))

    def unravel(i, carry):
        spread(8 * PITCH * i, HALO + 8 * i)
        return carry

    lax.fori_loop(0, ROWS // 8, unravel, 0)
    spread(8 * PITCH * (ROWS // 8), 0)
    spread(8 * PITCH * (ROWS // 8 + 1), HALO + ROWS)

    later = lax.broadcasted_iota(jnp.int32, (8, 128), 0) >= 4

    def put(row, value):
        for h in (0, 1):
            cots[h, pl.ds(pl.multiple_of(inner(row), 8), INNER), :] = value[:, halves[h]]

    def fill(pair, carry):
        sides = [cot_left[pair].astype(F32), cot_right[pair].astype(F32)]
        for odd in (0, 1):
            row = 2 * pair + odd
            edges = [s[4 * odd : 4 * odd + 4] for s in sides]
            put(
                row + HALO, jnp.concatenate([edges[0], cot[row].astype(F32), edges[1]], 0)
            )
        return carry

    lax.fori_loop(0, ROWS // 2, fill, 0)
    for k in range(4):
        rows = slice(INNER * k, INNER * (k + 1))
        put(k + 4, beyond(0, rows))
        put(k + HALO + ROWS, beyond(1, rows))

    def get(ref, start, count):
        return [ref[h, pl.ds(pl.multiple_of(start, 8), count), :] for h in (0, 1)]

    def keep(ref, start, values):
        for h in (0, 1):
            ref[h, pl.ds(pl.multiple_of(start, 8), values[h].shape[0]), :] = values[h]

    def from_wide(ref, row, rows):
        return [
            jnp.concatenate(
                [ref[h, pl.ds(at(row + r) + 4, INNER), :] for r in range(rows)], 0
            )
            for h in (0, 1)
        ]

    def joined(sums):
        return jnp.concatenate(sums, 0).reshape(-1, 128)

    def local_part(x):
        x = x.reshape(-1, 4, 8, 128)
        ends = jnp.where(later, x[:, 0], x[:, 3])
        return jnp.stack([ends, x[:, 1], x[:, 2]], 1).reshape(-1, 128)

    def gains(ref):
        return [ref[:, halves[h]] for h in (0, 1)]

    def normalised(raw):
        mean = jnp.sum(raw[0] * raw[0] + raw[1] * raw[1], -1, keepdims=True) * (1.0 / CHANS)
        scale = lax.rsqrt(mean + 1e-06)
        return scale, [raw[h] * scale for h in (0, 1)]

    def activated(xhat, gain, point):
        u = [xhat[h] * gain[h] for h in (0, 1)]
        p = jnp.dot(
            jnp.concatenate(u, 1).astype(BF16), point[...], preferred_element_type=F32
        )
        p = [p[:, s] for s in halves]
        rise = [jnp.tanh(v) + 1.0 for v in p]
        silu = [p[h] * rise[h] for h in (0, 1)]
        slope = [rise[h] + silu[h] * (2.0 - rise[h]) for h in (0, 1)]
        return u, silu, slope

    def through_norm(grad, slope, xhat, scale, gain, turned):
        dp = [grad[h] * slope[h] for h in (0, 1)]
        du = jnp.dot(
            jnp.concatenate(dp, 1).astype(BF16), turned[...], preferred_element_type=F32
        )
        gained = [du[:, halves[h]] * gain[h] for h in (0, 1)]
        both = [gained[h] * xhat[h] for h in (0, 1)]
        mean = jnp.sum(both[0] + both[1], -1, keepdims=True) * (1.0 / CHANS)
        dd = [
            (scale * (gained[h] - xhat[h] * mean)).astype(BF16).astype(F32) for h in (0, 1)
        ]
        return dp, both, dd

    def gain_sums(store, both):
        for h in (0, 1):
            store[h] += jnp.sum(local_part(both[h]).reshape(-1, 8, 128), 0)

    def pipeline(blocks, first, second):
        first(0)

        def step(i, carry):
            second(i - 1)
            first(i)
            return carry

        lax.fori_loop(1, blocks, step, 0)
        second(blocks - 1)

    size = 4 * PITCH

    def first_conv(i):
        start = at(2) + i * size
        keep(d, start, [joined(conv(x0, h, start, PITCH, 4, PITCH, taps1)) for h in (0, 1)])

    def first_mix(i):
        start = at(2) + i * size
        scale, xhat = normalised(get(d, start, size))
        _, silu, slope = activated(xhat, gains(gain1), half1)
        x = get(x0, start, size)
        keep(h1, start, [(x[h] + silu[h]).astype(BF16).astype(F32) for h in (0, 1)])
        keep(xhat1, start, xhat)
        keep(slope1, start, slope)
        scale1[pl.ds(pl.multiple_of(start, 8), size), :] = jnp.broadcast_to(scale, (size, 128))

    pipeline((TALL - 4) // 4, first_conv, first_mix)

    @pl.when(lat[0] == 0)
    def _():
        for h in (0, 1):
            h1[h, at(2) : at(HALO)] = jnp.zeros((6 * PITCH, 128), F32)

    @pl.when(lat[0] == lat_devices - 1)
    def _():
        for h in (0, 1):
            h1[h, at(HALO + ROWS) : at(HALO + ROWS + 6)] = jnp.zeros((6 * PITCH, 128), F32)

    def second_conv(row):
        keep(
            d,
            inner(row),
            [joined(conv(h1, h, at(row) + 4, PITCH, 4, INNER, taps2)) for h in (0, 1)],
        )

    def second_mix(row, local):
        start = inner(row)
        scale, xhat = normalised(get(d, start, 4 * INNER))
        gain = gains(gain2)
        u, silu, slope = activated(xhat, gain, half2)
        dp, both, dd = through_norm(
            get(cots, start, 4 * INNER), slope, xhat, scale, gain, turned2
        )
        keep(dd2, start, dd)
        if local is not None:
            keep(lifted, LEAD + 4 * INNER * local, silu)
            spot = pl.ds(pl.multiple_of(local * 96, 96), 96)
            u2[spot] = jnp.concatenate([local_part(v) for v in u], 1).astype(BF16)
            dp2[spot] = jnp.concatenate([local_part(v) for v in dp], 1).astype(BF16)
            gain_sums(gg2, both)

    def result(i):
        total = []
        for h in (0, 1):
            rows = []
            for r in range(4):
                place = LEAD + INNER * (4 * i + r) + 4
                base = h1[h, pl.ds(pl.multiple_of(at(HALO + 4 * i + r) + HALO, 8), COLS), :]
                rows.append(base + lifted[h, pl.ds(place, COLS), :])
            total.append(jnp.concatenate(rows, 0))
        out[pl.ds(i * 4, 4)] = jnp.concatenate(total, 1).reshape(4, COLS, CHANS).astype(BF16)

    for row in (4, HALO + ROWS):
        second_conv(row)
    for row in (4, HALO + ROWS):
        second_mix(row, None)
    pipeline(
        ROWS // 4,
        lambda i: second_conv(HALO + 4 * i),
        lambda i: second_mix(HALO + 4 * i, i),
    )

    def third_conv(row, rows, local):
        start = inner(row)
        total = []
        for h in (0, 1):
            visit = None
            if local:
                centre = [
                    own_tiles(h1[h, pl.ds(at(row + r) + 4, INNER), :].reshape(4, 8, 128))
                    for r in range(rows)
                ]
                visit = TapSums(gk2, h, centre)
            sums = joined(conv(dd2, h, start, INNER, rows, INNER, flip2, visit))
            total.append(sums + cots[h, pl.ds(pl.multiple_of(start, 8), rows * INNER), :])
        keep(g1, start, total)

    def third_mix(row, rows, local):
        start = inner(row)
        gain = gains(gain1)
        xhat = from_wide(xhat1, row, rows)
        scale = jnp.concatenate(
            [scale1[pl.ds(at(row + r) + 4, INNER), :] for r in range(rows)], 0
        )
        dp, both, dd = through_norm(
            get(g1, start, rows * INNER), from_wide(slope1, row, rows), xhat, scale, gain, turned1
        )
        keep(dd1, start, dd)
        if local is not None:
            spot = pl.ds(pl.multiple_of(local * 96, 96), 96)
            u = [local_part(xhat[h] * gain[h]) for h in (0, 1)]
            u1[spot] = jnp.concatenate(u, 1).astype(BF16)
            dp1[spot] = jnp.concatenate([local_part(v) for v in dp], 1).astype(BF16)
            gain_sums(gg1, both)
            result(local)

    for row in (6, HALO + ROWS):
        third_conv(row, 2, False)
    for row in (6, HALO + ROWS):
        third_mix(row, 2, None)
    pipeline(
        ROWS // 4,
        lambda i: third_conv(HALO + 4 * i, 4, True),
        lambda i: third_mix(HALO + 4 * i, 4, i),
    )

    @pl.when(lat[0] == 0)
    def _():
        for h in (0, 1):
            dd1[h, inner(6) : inner(HALO)] = jnp.zeros((2 * INNER, 128), F32)

    @pl.when(lat[0] == lat_devices - 1)
    def _():
        for h in (0, 1):
            dd1[h, inner(HALO + ROWS) : inner(HALO + ROWS + 2)] = jnp.zeros(
                (2 * INNER, 128), F32
            )

    def fourth(i, carry):
        row = HALO + 4 * i
        for h in (0, 1):
            centre = [
                x0[h, pl.ds(pl.multiple_of(at(row + r) + HALO, 8), COLS), :].reshape(3, 8, 128)
                for r in range(4)
            ]
            sums = conv(dd1, h, inner(row) + 4, INNER, 4, COLS, flip1, TapSums(gk1, h, centre))
            for r in range(4):
                base = g1[h, pl.ds(inner(row + r) + 4, COLS), :]
                place = GROUP * (i // 2) + 4 * (i % 2) + r
                g0[h, pl.ds(place, COLS, stride=8), :] = sums[r].reshape(COLS, 128) + base
        return carry

    lax.fori_loop(0, ROWS // 4, fourth, 0)

    def pack(place, value):
        rows = value.shape[0]
        value = value.astype(BF16)
        for h in (0, 1):
            packed[place : place + rows // 8, h] = value[:, halves[h]].reshape(rows // 8, 8, 128)

    pack(0, across(u1[...], dp1[...]) * 0.5)
    pack(32, across(u2[...], dp2[...]) * 0.5)
    field = jnp.concatenate([g0[h] for h in (0, 1)], 1).astype(BF16)
    embedded = jnp.dot(high[...], field, preferred_element_type=F32)

    def gain_row(ref, gain):
        total = [jnp.sum(ref[h], 0, keepdims=True) for h in (0, 1)]
        return jnp.concatenate(total, 1) / gain[...]

    pack(
        64,
        jnp.concatenate(
            [embedded, gain_row(gg1, gain1), gain_row(gg2, gain2), jnp.zeros((1, CHANS), F32)], 0
        ),
    )
    for place, ref in ((73, gk1), (77, gk2)):
        total = jnp.concatenate([jnp.sum(ref[h], 1) for h in (0, 1)], 1)
        pack(place, jnp.concatenate([total, jnp.zeros((7, CHANS), F32)], 0))
    packed[81:TILES] = jnp.zeros((TILES - 81, 2, 8, 128), BF16)


def blocks(fields, weights, lat_devices):
    wide = pltpu.VMEM((2, FLAT, 128), F32)
    slim = pltpu.VMEM((2, SLIM, 128), F32)
    taps = pltpu.VMEM((2, 25, 8, 128), F32)
    square = pltpu.VMEM((CHANS, CHANS), BF16)
    local = pltpu.VMEM((ROWS * COLS, CHANS), BF16)
    eight = pltpu.VMEM((2, 8, 128), F32)
    lat = jnp.reshape(lax.axis_index("lat"), (1,)).astype(jnp.int32)
    operands = (*fields, *weights)
    vmem = pl.BlockSpec(memory_space=pltpu.VMEM)
    return pl.pallas_call(
        functools.partial(blocks_kernel, lat_devices=lat_devices),
        in_specs=[pl.BlockSpec(memory_space=pltpu.SMEM)] + [vmem] * len(operands),
        out_specs=[vmem, vmem],
        out_shape=[
            jax.ShapeDtypeStruct((ROWS, COLS, CHANS), BF16),
            jax.ShapeDtypeStruct((TILES, 2, 8, 128), BF16),
        ],
        scratch_shapes=[wide, slim, wide, wide, wide, pltpu.VMEM((FLAT, 128), F32), wide]
        + [slim] * 3
        + [taps] * 4
        + [square] * 4
        + [local] * 4
        + [pltpu.VMEM((2, ROWS * COLS, 128), F32)]
        + [taps] * 2
        + [eight] * 2
        + [pltpu.VMEM((2, PITCH * TALL, 128), F32)]
        + [pltpu.VMEM((2, LEAD + INNER * ROWS + 16, 128), F32)],
        compiler_params=pltpu.CompilerParams(vmem_limit_bytes=60 * 1024 * 1024),
        name="both_blocks",
    )(lat, *operands)


def unpack_kernel(packed, embed, kernel1, kernel2, point1, point2, gain1, gain2, *, factor):
    for h in (0, 1):
        lanes = slice(128 * h, 128 * h + 128)
        point1[:, lanes] = packed[0:32, h].astype(F32).reshape(CHANS, 128) * factor
        point2[:, lanes] = packed[32:64, h].astype(F32).reshape(CHANS, 128) * factor
        mixed = packed[64:73, h].astype(F32).reshape(72, 128) * factor
        embed[:, lanes] = mixed[:VARS]
        gain1[:, lanes] = mixed[VARS : VARS + 1]
        gain2[:, lanes] = mixed[VARS + 1 : VARS + 2]
        kernel1[:, lanes] = (packed[73:77, h].astype(F32).reshape(32, 128) * factor)[:25]
        kernel2[:, lanes] = (packed[77:81, h].astype(F32).reshape(32, 128) * factor)[:25]


def summed(packed, factor):
    devices = lax.axis_size(AXES)
    parts = lax.all_to_all(packed, AXES, 0, 0, tiled=True)
    mine = jnp.sum(parts.reshape(devices, -1, 2, 8, 128).astype(F32), 0).astype(BF16)
    total = lax.all_to_all(jnp.tile(mine, (devices, 1, 1, 1)), AXES, 0, 0, tiled=True)
    shapes = [(VARS, CHANS), (25, CHANS), (25, CHANS), (CHANS, CHANS), (CHANS, CHANS)]
    results = pl.pallas_call(
        functools.partial(unpack_kernel, factor=factor),
        out_shape=[jax.ShapeDtypeStruct(s, F32) for s in shapes + [(1, CHANS)] * 2],
        name="unpack",
    )(total)
    return (*results[:5], results[5].reshape(CHANS), results[6].reshape(CHANS))


def shifted(before, after, axis, wrap):
    devices = lax.axis_size(axis)
    up = [(i, (i + 1) % devices) for i in range(devices if wrap else devices - 1)]
    down = [(j, i) for i, j in up]
    return lax.ppermute(after, axis, up), lax.ppermute(before, axis, down)


def on_device(points, row_len, w_embed, kernel1, gain1, point1, kernel2, gain2, point2, cotangent):
    lon_total = COLS * lax.axis_size("lon")
    rows_total = ROWS * lax.axis_size("lat")
    devices = lax.axis_size("lon")
    lon_odd = lax.axis_index("lon") % 2 == 1

    def swapped_along_lon(first, last):
        sent = (jnp.where(lon_odd, first, last), jnp.where(lon_odd, last, first))
        got = []
        for start in (0, 1):
            pairs = [(i, (i + 1) % devices) for i in range(start, devices, 2)]
            got.append(lax.ppermute(sent[start], "lon", pairs + [(j, i) for i, j in pairs]))
        return jnp.where(lon_odd, got[0], got[1]), jnp.where(lon_odd, got[1], got[0])

    cot_left, cot_right = swapped_along_lon(
        cotangent[:, :4].reshape(ROWS // 2, 8, CHANS),
        cotangent[:, COLS - 4 :].reshape(ROWS // 2, 8, CHANS),
    )
    high, low, west, east = regrid(jnp.swapaxes(points, 0, 1), row_len, lon_total)
    left, right = swapped_along_lon(west, east)

    def band(rows, pairs, lanes, edge):
        sides = [c[pairs].reshape(4, 4, CHANS) for c in (cot_left, cot_right)]
        given = jnp.concatenate([sides[0], cotangent[rows], sides[1]], 1).reshape(-1, CHANS)
        field = jnp.concatenate([left[:, edge], high[:, lanes], right[:, edge]], 1)
        pieces = [field[:, :CHANS], field[:, CHANS:]]
        pieces = [
            jnp.pad(x, ((0, 80 - VARS), (0, CHANS - x.shape[1]))) for x in pieces
        ]
        return jnp.concatenate([given, *pieces], 0)

    first_band = band(slice(0, 4), slice(0, 2), slice(0, GROUP), slice(0, STRIP))
    last_band = band(
        slice(ROWS - 4, ROWS),
        slice(ROWS // 2 - 2, ROWS // 2),
        slice(GROUP * (ROWS // 8 - 1), GROUP * (ROWS // 8)),
        slice(STRIP * (ROWS // 8 - 1), STRIP * (ROWS // 8)),
    )
    odd = lax.axis_index("lat") % 2 == 1
    sent = (jnp.where(odd, first_band, last_band), jnp.where(odd, last_band, first_band))
    swaps = []
    for start in (0, 1):
        pairs = [(i, i + 1) for i in range(start, lax.axis_size("lat") - 1, 2)]
        swaps.append(lax.ppermute(sent[start], "lat", pairs + [(j, i) for i, j in pairs]))
    above, below = swaps
    fields = (high, low, left, right, above, below, cotangent, cot_left, cot_right)
    weights = (
        w_embed, kernel1, gain1.reshape(1, CHANS), point1,
        kernel2, gain2.reshape(1, CHANS), point2,
    )
    out, packed = blocks(fields, weights, lax.axis_size("lat"))
    return (out, *summed(packed, float(rows_total * lon_total) ** (-0.5)))


def solution(mesh):
    in_specs = (
        P("lat", None, "lon"),
        P("lat"),
        P(),
        P(),
        P(),
        P(),
        P(),
        P(),
        P(),
        P("lat", "lon", None),
    )
    out_specs = (P("lat", "lon", None), P(), P(), P(), P(), P(), P(), P())
    return jax.shard_map(
        on_device, mesh=mesh, in_specs=in_specs, out_specs=out_specs, check_vma=False
    )
```
